32 devices in a mesh: dp: 4 (over z), tensor: 8 (over y, x, core).
Axes of the slice: x: 2, y: 2, z: 4, core: 2. Of those that a mesh axis runs over, the one named last changes fastest.
Arguments:
- tokens: bfloat16 [8192, 1152], P('dp'), may hold values from -6 to 6
- condition: float32 [32, 1152], P('dp'), may hold values from -6 to 6
- timesteps: int32 [32], P('dp'), may hold values from 0 to 999
- route_masks: int32 [1000, 16, 2], P(None, 'tensor'), may hold values 0 or 1
- modulate_weight: bfloat16 [1152, 6, 1152], P(None, None, 'tensor'), may hold values from -0.1875 to 0.1875
- modulate_bias: bfloat16 [6, 1152], P(None, 'tensor'), may hold values from -1.5 to 1.5
- input_weight: bfloat16 [1152, 3, 1152], P(None, None, 'tensor'), may hold values from -0.1875 to 0.1875
- input_bias: bfloat16 [2, 1152], P(None, 'tensor'), may hold values from -1.5 to 1.5
- output_weight: bfloat16 [1152, 1152], P('tensor'), may hold values from -1.5 to 1.5
- output_bias: bfloat16 [1152], replicated, may hold values from -1.5 to 1.5
- expand_weight: bfloat16 [1152, 4608], P(None, 'tensor'), may hold values from -0.1875 to 0.1875
- expand_bias: bfloat16 [4608], P('tensor'), may hold values from -1.5 to 1.5
- reduce_weight: bfloat16 [4608, 1152], P('tensor'), may hold values from -0.1875 to 0.1875
- reduce_bias: bfloat16 [1152], replicated, may hold values from -1.5 to 1.5
- router_weight: bfloat16 [1152, 16, 2], P(None, 'tensor'), may hold values from -0.1875 to 0.1875
- router_bias: bfloat16 [16, 2], P('tensor'), may hold values from -1.2 to 1.2
- out_cotangent: bfloat16 [8192, 1152], P('dp'), may hold values from -6 to 6
Outputs:
- block_output: float32 [8192, 1152], P('dp')
- tokens_grad: float32 [8192, 1152], P('dp')
- modulate_weight_grad: float32 [1152, 6, 1152], P(None, None, 'tensor')
- modulate_bias_grad: float32 [6, 1152], P(None, 'tensor')
- input_weight_grad: float32 [1152, 3, 1152], P(None, None, 'tensor')
- input_bias_grad: float32 [2, 1152], P(None, 'tensor')
- output_weight_grad: float32 [1152, 1152], P('tensor')
- output_bias_grad: float32 [1152], replicated
- expand_weight_grad: float32 [1152, 4608], P(None, 'tensor')
- expand_bias_grad: float32 [4608], P('tensor')
- reduce_weight_grad: float32 [4608, 1152], P('tensor')
- reduce_bias_grad: float32 [1152], replicated
- router_weight_grad: float32 [1152, 16, 2], P(None, 'tensor')
- router_bias_grad: float32 [16, 2], P('tensor')
The draws below stay inside these ranges and needn't reach their ends.
Inputs may be any that keep to these rules, and one draw needn't show every extreme that they name: `timesteps`: each timestep selects the row of route_masks used by its item.
All inputs are finite; a program needn't handle non-finite values. No bound on the sum of `route_masks` on one device may be relied on, other than what follows from the above.
Results may differ from the reference program's by a relative error of at most 0.013.
The reference program's roundings to bfloat16 on the way count: a program that leaves them out, or rounds other values in their place, can miss the bound.
Values may be sent and summed in bfloat16 or wider, within the bound.
A program may use at most 256 MiB of HBM per device.

```python
import math
import jax
import jax.numpy as jnp
from jax import lax

D = 1152
HEADS = 16
HDIM = 72
FF = 4608
SEQ = 256
STEPS = 1000
ITEMS = 32
TOKENS = 8192


def drawn_values(key, label, shape, spread, bound):
    own_key = jax.random.fold_in(key, label)
    values = jnp.clip(jax.random.normal(own_key, shape, jnp.float32), -bound, bound) * spread
    return values


def draw_tokens(key, part):
    return drawn_values(key, 101, (TOKENS, D), 1.0, 6.0).astype(jnp.bfloat16)


def draw_condition(key, part):
    return drawn_values(key, 102, (ITEMS, D), 1.0, 6.0)


def draw_modulate_bias(key, part):
    return drawn_values(key, 103, (6, D), 0.5, 3.0).astype(jnp.bfloat16)


def draw_input_bias(key, part):
    return drawn_values(key, 104, (2, D), 0.5, 3.0).astype(jnp.bfloat16)


def draw_output_bias(key, part):
    return drawn_values(key, 105, (D,), 0.5, 3.0).astype(jnp.bfloat16)


def draw_expand_bias(key, part):
    return drawn_values(key, 106, (FF,), 0.5, 3.0).astype(jnp.bfloat16)


def draw_reduce_bias(key, part):
    return drawn_values(key, 107, (D,), 0.5, 3.0).astype(jnp.bfloat16)


def draw_router_bias(key, part):
    return drawn_values(key, 108, (HEADS, 2), 0.3, 4.0).astype(jnp.bfloat16)


def draw_out_cotangent(key, part):
    return drawn_values(key, 109, (TOKENS, D), 1.0, 6.0).astype(jnp.bfloat16)


def with_ends(array, stream_key, least, largest):
    shape = array.shape
    place = [jax.random.randint(jax.random.fold_in(stream_key, axis), (), 0, shape[axis]) for axis in range(len(shape))]
    array = array.at[tuple(place)].set(least)
    longest = shape.index(max(shape))
    place[longest] = (place[longest] + 1) % shape[longest]
    return array.at[tuple(place)].set(largest)


def level_of(key, shape, split, smallest, largest):
    factor_of = 1.0
    for position, parts in split:
        steps = jax.random.uniform(jax.random.fold_in(jax.random.fold_in(key, 6), position), (parts,), jnp.float32, smallest / len(split), largest / len(split))
        factor_of = factor_of * jnp.repeat(jnp.exp(steps), shape[position] // parts).reshape((-1,) + (1,) * (len(shape) - 1 - position))
    return factor_of


def centred(key, dims, deviation, limit, split=(), kind=jnp.bfloat16):
    values = deviation * jax.random.normal(key, dims, jnp.float32)
    if split:
        values = values * level_of(key, dims, split, -0.22, 0.18)
    return jnp.clip(values, -limit, limit).astype(kind)


def setup_inputs(seed: int = 0) -> dict:
    splits = jax.random.split(jax.random.key(seed), 18)
    return {
        "tokens": draw_tokens(jax.random.fold_in(splits[17], 71), 0),
        "condition": draw_condition(jax.random.fold_in(splits[17], 71), 0),
        "timesteps": with_ends(jax.random.randint(splits[2], (ITEMS,), 0, STEPS), jax.random.fold_in(splits[2], 1), 0, STEPS - 1).astype(jnp.int32),
        "route_masks": with_ends((jax.random.randint(splits[3], (STEPS, HEADS, 2), 0, 4) < 3).astype(jnp.int32), jax.random.fold_in(splits[3], 1), 0, 1),
        "modulate_weight": centred(splits[4], (D, 6, D), D ** -0.5, 0.1875, ((2, 8),)),
        "modulate_bias": draw_modulate_bias(jax.random.fold_in(splits[17], 71), 0),
        "input_weight": centred(splits[6], (D, 3, D), D ** -0.5, 0.1875, ((2, 8),)),
        "input_bias": draw_input_bias(jax.random.fold_in(splits[17], 71), 0),
        "output_weight": centred(splits[8], (D, D), (HDIM // 4) ** -0.5, 1.5, ((0, 8),)),
        "output_bias": draw_output_bias(jax.random.fold_in(splits[17], 71), 0),
        "expand_weight": centred(splits[10], (D, FF), D ** -0.5, 0.1875, ((1, 8),)),
        "expand_bias": draw_expand_bias(jax.random.fold_in(splits[17], 71), 0),
        "reduce_weight": centred(splits[12], (FF, D), (FF // 4) ** -0.5, 0.1875, ((0, 8),)),
        "reduce_bias": draw_reduce_bias(jax.random.fold_in(splits[17], 71), 0),
        "router_weight": centred(splits[14], (D, HEADS, 2), D ** -0.5, 0.1875, ((1, 8),)),
        "router_bias": draw_router_bias(jax.random.fold_in(splits[17], 71), 0),
        "out_cotangent": draw_out_cotangent(jax.random.fold_in(splits[17], 71), 0),
    }


HIGHEST = lax.Precision.HIGHEST
EPSILON = 1e-06

@jax.custom_vjp
def low(v):
    return lax.optimization_barrier(v.astype(jnp.bfloat16)).astype(jnp.float32)

@jax.custom_vjp
def low_back(v):
    return v

def low_keep(v):
    return (low(v), None)

def low_pass(kept, grad):
    return (grad,)

def back_keep(v):
    return (v, None)

def back_low(kept, grad):
    return (low(grad),)
low.defvjp(low_keep, low_pass)
low_back.defvjp(back_keep, back_low)

def both_ways(values):
    return low(low_back(values))

def layer_norm(values):
    center = values - lax.optimization_barrier(jnp.mean(values, axis=-1, keepdims=True))
    return center * lax.rsqrt(lax.optimization_barrier(jnp.mean(center * center, axis=-1, keepdims=True)) + EPSILON)

def attend_item(operands):
    queries, keys_in, values_in = operands
    score_scale = 1.0 / math.sqrt(HDIM)
    scores = low_back(jnp.einsum('qhe,khe->hqk', queries, keys_in, precision=HIGHEST) * score_scale)
    softmax_low = low(jax.nn.softmax(scores, axis=-1))
    return low_back(jnp.einsum('hqk,khe->qhe', softmax_low, values_in, precision=HIGHEST))

def forward(tokens_f, modulate_weight, modulate_bias, input_weight, input_bias, output_weight, output_bias, expand_weight, expand_bias, reduce_weight, reduce_bias, router_weight, router_bias, condition, gate_masks):
    item_count = condition.shape[0]
    silu_condition = low(jax.nn.silu(condition))
    modulation = jnp.einsum('bd,dke->bke', silu_condition, modulate_weight, precision=HIGHEST) + modulate_bias
    shift_one, scale_one, gate_one, shift_two, scale_two, gate_two = [modulation[:, column][:, None, :] for column in range(6)]
    logits = jnp.einsum('bd,dhc->bhc', low(condition), router_weight, precision=HIGHEST) + router_bias
    gate_values = gate_masks * jax.nn.sigmoid(logits)
    inputs_f = tokens_f.reshape(item_count, SEQ, D)
    hidden_one = low(layer_norm(inputs_f) * (1.0 + scale_one) + shift_one)
    projected = jnp.einsum('bsd,dke->bske', hidden_one, input_weight, precision=HIGHEST)
    queries = both_ways(projected[:, :, 0] + input_bias[0]).reshape(item_count, SEQ, HEADS, HDIM)
    keys_in = both_ways(projected[:, :, 1]).reshape(item_count, SEQ, HEADS, HDIM)
    values_in = both_ways(projected[:, :, 2] + input_bias[1]).reshape(item_count, SEQ, HEADS, HDIM)
    mixed_heads = lax.map(jax.checkpoint(attend_item), (queries, keys_in, values_in))
    gated_heads = low(mixed_heads * gate_values[:, None, :, 0, None]).reshape(item_count, SEQ, D)
    attention = low_back(jnp.einsum('bsd,de->bse', gated_heads, output_weight, precision=HIGHEST) + output_bias)
    residual_one = inputs_f + gate_one * attention
    hidden_two = low(layer_norm(residual_one) * (1.0 + scale_two) + shift_two)
    expanded = low_back(jnp.einsum('bsd,df->bsf', hidden_two, expand_weight, precision=HIGHEST) + expand_bias)
    activated = jax.nn.gelu(expanded, approximate=True).reshape(item_count, SEQ, HEADS, FF // HEADS)
    gated_channels = low(activated * gate_values[:, None, :, 1, None]).reshape(item_count, SEQ, FF)
    branch_two = low_back(jnp.einsum('bsf,fd->bsd', gated_channels, reduce_weight, precision=HIGHEST) + reduce_bias)
    return (residual_one + gate_two * branch_two).reshape(item_count * SEQ, D)

def reference(tokens, condition, timesteps, route_masks, modulate_weight, modulate_bias, input_weight, input_bias, output_weight, output_bias, expand_weight, expand_bias, reduce_weight, reduce_bias, router_weight, router_bias, out_cotangent):
    gate_masks = route_masks[timesteps].astype(jnp.float32)
    params = [value.astype(jnp.float32) for value in (tokens, modulate_weight, modulate_bias, input_weight, input_bias, output_weight, output_bias, expand_weight, expand_bias, reduce_weight, reduce_bias, router_weight, router_bias)]

    def closed(*values):
        return forward(*values, condition, gate_masks)
    result, pullback = jax.vjp(closed, *params)
    gradients = pullback(out_cotangent.astype(jnp.float32))
    return (result, gradients[0], gradients[1], gradients[2], gradients[3], gradients[4], gradients[5], gradients[6], gradients[7], gradients[8], gradients[9], gradients[10], gradients[11], gradients[12])
```

```python
import functools
import math

import jax
import jax.numpy as jnp
from jax import lax
from jax.experimental import pallas as pl
from jax.experimental.pallas import tpu as pltpu
from jax.sharding import PartitionSpec as P

BF = jnp.bfloat16
F32 = jnp.float32
MESH = pl.DeviceIdType.MESH
EPSILON = 1e-06
GELU_A = math.sqrt(2.0 / math.pi)
GELU_B = 0.044715
VMEM_LIMIT = 58 << 20


def nt(left, right):
    return lax.dot_general(left, right, (((1,), (1,)), ((), ())), preferred_element_type=F32)


def nn(left, right):
    return lax.dot_general(left, right, (((1,), (0,)), ((), ())), preferred_element_type=F32)


def tn(left, right):
    return lax.dot_general(left, right, (((0,), (0,)), ((), ())), preferred_element_type=F32)


def flip(value, mask, bits):
    total = 0
    for bit in range(bits):
        unit = 1 << bit
        total = total + lax.rem(value // unit + mask // unit, 2) * unit
    return total


def norm(values):
    center = values - jnp.mean(values, axis=-1, keepdims=True)
    inverse = lax.rsqrt(jnp.mean(center * center, axis=-1, keepdims=True) + EPSILON)
    return center * inverse, inverse


def norm_back(grad, normed, inverse):
    mean_grad = jnp.mean(grad, axis=-1, keepdims=True)
    mean_cross = jnp.mean(grad * normed, axis=-1, keepdims=True)
    return inverse * (grad - mean_grad - normed * mean_cross)


class Plan:
    def __init__(self, groups, members, rows, items, width, heads, modwidth, headwidth, channels):
        self.D = groups
        self.T = members
        self.G = members // 2
        self.bits = self.G.bit_length() - 1
        self.tbits = members.bit_length() - 1
        self.dbits = groups.bit_length() - 1
        self.R = rows
        self.I = items
        self.L = rows // items
        self.W = width
        self.Rc = rows // 2
        self.Ro = rows // members
        self.Ic = items // 2
        self.sub = self.L // self.Ro
        self.lh = heads
        self.mw = modwidth
        self.cw = -(-modwidth // 128) * 128
        self.hw = headwidth
        self.hd = headwidth // heads
        self.ch = channels
        self.gc = channels // heads
        self.hr = 2 * headwidth
        self.halvings = min(self.dbits, 2)
        self.flips = [1, 3][: self.dbits] + [1 << b for b in range(2, self.dbits)]
        self.units = 1 << self.halvings
        self.zr = 4 * self.hw // (2 * self.units)

    def place(self):
        d = lax.axis_index("dp")
        t = lax.axis_index("tensor")
        return d, t, t // 2, lax.rem(t, 2)


def meet(devices):
    barrier = pltpu.get_barrier_semaphore()
    for device in devices:
        pl.semaphore_signal(barrier, inc=1, device_id=device, device_id_type=MESH)
    pl.semaphore_wait(barrier, len(devices))


def remote(src, dst, send, recv, device):
    return pltpu.make_async_remote_copy(
        src_ref=src, dst_ref=dst, send_sem=send, recv_sem=recv, device_id=device, device_id_type=MESH
    )


class GroupSum:
    def __init__(self, g, work, inbox, full, send, recv, device):
        self.g, self.work, self.inbox, self.full = g, work, inbox, full
        self.send, self.recv, self.device = send, recv, device
        d = lax.axis_index("dp")
        low, high = lax.rem(d, 2), lax.rem(d // 2, 2)
        both = low + high - 2 * low * high
        self.steps = g.dbits
        self.flips = [g.flips, g.flips[1::-1] + g.flips[2:]]
        keeps = [[low], [low]] if g.dbits == 1 else [[both, high], [high, low]]
        self.places = []
        for which in range(2):
            start, size, rows = which * g.units, g.units, []
            for step in range(self.steps):
                if step < g.halvings:
                    half = size // 2
                    keep = start + keeps[which][step] * half
                    away = start + (1 - keeps[which][step]) * half
                    rows.append((keep, away, half))
                    start, size = keep, half
                else:
                    rows.append((start, start, size))
            self.places.append(rows)

    def peer(self, which, step):
        return self.device(self.flips[which][step])

    def box(self, which, step):
        g = self.g
        base = sum(g.units >> (s + 1) if s < g.halvings else 1 for s in range(step))
        size = self.places[which][step][2]
        return self.inbox.at[which, pl.ds(base, size)]

    def copy(self, which, step):
        _, away, size = self.places[which][step]
        return remote(
            self.work.at[pl.ds(away, size)], self.box(which, step), self.send.at[which, step],
            self.recv.at[which, step], self.peer(which, step),
        )

    def start(self, step):
        for which in range(2):
            self.copy(which, step).start()

    def add(self, step):
        for which in range(2):
            keep, _, size = self.places[which][step]
            copy = self.copy(which, step)
            if step < self.g.halvings:
                copy.wait_recv()
            else:
                copy.wait()
            rows = pl.ds(keep, size)
            self.work[rows] = (self.work[rows].astype(F32) + self.box(which, step)[...].astype(F32)).astype(BF)

    def sent(self):
        for step in range(self.g.halvings):
            for which in range(2):
                self.copy(which, step).wait_send()

    def spread(self, which, step):
        keep, _, size = self.places[which][step]
        rows = self.full.at[pl.ds(keep, size)]
        slot = self.steps + step
        return remote(rows, rows, self.send.at[which, slot], self.recv.at[which, slot], self.peer(which, step))

    def gathered(self, which, step):
        _, away, size = self.places[which][step]
        rows = self.full.at[pl.ds(away, size)]
        slot = self.steps + step
        return remote(rows, rows, self.send.at[which, slot], self.recv.at[which, slot], self.peer(which, step))

    def spread_start(self, step):
        for which in range(2):
            if step == self.g.halvings - 1:
                keep, _, size = self.places[which][step]
                self.full[pl.ds(keep, size)] = self.work[pl.ds(keep, size)]
            self.spread(which, step).start()

    def spread_wait(self, step):
        for which in range(2):
            self.spread(which, step).wait_send()
            self.gathered(which, step).wait_recv()

    @staticmethod
    def scratch(g, rows):
        boxes = sum(g.units >> (s + 1) if s < g.halvings else 1 for s in range(g.dbits))
        dma = pltpu.SemaphoreType.DMA
        return [
            pltpu.VMEM((2 * g.units, rows, g.W), BF), pltpu.VMEM((2, boxes, rows, g.W), BF),
            dma((2, 2 * g.dbits)), dma((2, 2 * g.dbits)),
        ]


def call(kernel, name, inputs, in_spaces, outs, out_spaces, scratch, collective, cost=None):
    spec = {
        "v": pl.BlockSpec(memory_space=pltpu.VMEM),
        "h": pl.BlockSpec(memory_space=pl.ANY),
        "s": pl.BlockSpec(memory_space=pltpu.SMEM),
    }
    flops, moved = cost or (10**8, 10**7)
    return pl.pallas_call(
        kernel,
        name=name,
        out_shape=[jax.ShapeDtypeStruct(s, t) for s, t in outs],
        in_specs=[spec[x] for x in in_spaces],
        out_specs=[spec[x] for x in out_spaces],
        scratch_shapes=scratch,
        cost_estimate=pl.CostEstimate(flops=flops, bytes_accessed=moved, transcendentals=0),
        compiler_params=pltpu.CompilerParams(
            collective_id=collective, has_side_effects=collective is not None, vmem_limit_bytes=VMEM_LIMIT
        ),
    )(*inputs)


def start_kernel(
    g, cond, wm, mb, ts, masks, rw, rb, eb, ib, wi, we, wr,
    mod, gat, dsg, smc, call_all, wix, wex, wrx,
    mpart, gx, sx, cx, send_m, recv_m, send_w, recv_w, send_c, recv_c,
):
    d, t, p, c = g.place()
    partner = (d, p * 2 + 1 - c)
    meet(
        [(d, flip(t, k, g.tbits)) for k in range(1, g.T)] + [(flip(d, k, g.dbits), t) for k in range(1, g.D)]
    )
    pair = [
        remote(src, dst, send_w.at[index], recv_w.at[index], partner)
        for index, (src, dst) in enumerate(((wi, wix), (we, wex), (wr, wrx)))
    ]
    for copy in pair:
        copy.start()
    value = cond[...]
    silu = (value / (1.0 + jnp.exp(-value))).astype(BF)
    part = nt(silu, wm[...])
    w = g.mw
    bias = mb[...].astype(F32)
    for row in range(6):
        mpart[t, :, row * w : (row + 1) * w] = part[:, row * w : (row + 1) * w] + bias[row : row + 1]

    def spread(k):
        return remote(
            mpart.at[t], mpart.at[t], send_m.at[k], recv_m.at[k], (d, flip(t, k, g.tbits))
        )

    for k in range(1, g.T):
        spread(k).start()
    low = value.astype(BF)
    steps = masks.shape[2]
    row = lax.broadcasted_iota(jnp.int32, (g.I, steps), 0)
    wanted = jnp.zeros((g.I, steps), jnp.int32)
    for item in range(g.I):
        wanted = jnp.where(row == item, ts[item], wanted)
    hot = (wanted == lax.broadcasted_iota(jnp.int32, (g.I, steps), 1)).astype(F32).astype(BF)
    dsg[...] = jnp.zeros_like(dsg)
    gx[0] = jnp.zeros((g.I, 128), F32)
    scale = rb[...].astype(F32)
    for h in range(g.lh):
        logits = nt(low, rw[h]) + scale[h : h + 1]
        sigmoid = 1.0 / (1.0 + jnp.exp(-logits))
        mask = nt(hot, masks[h].astype(F32).astype(BF))
        dsg[:, 2 * h : 2 * h + 2] = mask * sigmoid * (1.0 - sigmoid)
        gx[0, :, 2 * h : 2 * h + 2] = mask * sigmoid
    sx[0] = jnp.zeros((8, g.W), F32)
    sx[0, 0:1, : g.ch] = eb[...]
    sx[0, 1:3, : g.hw] = ib[...].astype(F32)
    small = [
        remote(gx.at[0], gx.at[1], send_w.at[3], recv_w.at[3], partner),
        remote(sx.at[0], sx.at[1], send_w.at[4], recv_w.at[4], partner),
    ]
    for copy in small:
        copy.start()

    def conditions(k):
        return remote(cond, cx.at[d], send_c.at[k], recv_c.at[k], (flip(d, k, g.dbits), t))

    for k in range(1, g.D):
        conditions(k).start()
    cx[d] = value
    for k in range(1, g.T):
        spread(k).wait()
    for member in range(g.T):
        for row in range(6):
            mod[row, :, member * w : (member + 1) * w] = mpart[member, :, row * w : (row + 1) * w]
    for copy in small:
        copy.wait()
    gat[...] = gx[...]
    smc[...] = sx[...]
    for copy in pair:
        copy.wait()
    for k in range(1, g.D):
        conditions(k).wait()
    call_all[...] = cx[...]


def split_heads(g, wide):
    return [wide[r * g.hw + h * g.hd : r * g.hw + (h + 1) * g.hd] for r in range(3) for h in range(g.lh)]


def attend_kernel(
    g, tokens, mod, gat, smc, wi, wix, wo, ob,
    h1, qkv, lse, att, res, h2, gath, wof,
    tok, gsend, gbuf, wob, load, keep, send, recv, send_o, recv_o, send_f, recv_f,
):
    d, t, p, c = g.place()
    partner = (d, p * 2 + 1 - c)
    weights = (wi, wix)
    meet([(d, flip(p, k, g.bits) * 2 + c) for k in range(1, g.G)] + [partner])

    def share(k):
        return remote(wo, wob.at[t], send_o.at[k], recv_o.at[k], (d, flip(p, k, g.bits) * 2 + c))

    def forward(k):
        row = flip(p, k, g.bits) * 2 + c
        src = wo if k == 0 else wob.at[row]
        return remote(src, wob.at[row], send_f.at[k], recv_f.at[k], partner)

    for k in range(1, g.G):
        share(k).start()
    forward(0).start()
    wob[t] = wo[...]
    copy = pltpu.make_async_copy(tokens.at[pl.ds(pl.multiple_of(c * g.Rc, g.Rc), g.Rc)], tok, load)
    copy.start()
    copy.wait()
    scale = 1.0 / math.sqrt(g.hd)
    ones = jnp.ones((8, g.L), BF)

    def chunk(j):
        i, u = j // g.sub, lax.rem(j, g.sub)
        src = gsend.at[i] if g.sub == 1 else gsend.at[i, :, :, pl.ds(pl.multiple_of(u * g.Ro, g.Ro), g.Ro)]
        return src, gbuf.at[pl.ds(p * 2, 2)]

    def away(j):
        src, dst = chunk(j)
        return remote(src, dst, send.at[j], recv.at[p], (d, j * 2 + c))

    def arrive(j):
        src, _ = chunk(j)
        dst = gbuf.at[pl.ds(j * 2, 2)]
        return remote(src, dst, send.at[j], recv.at[j], (d, j * 2 + c))

    def home():
        src, dst = chunk(p)
        return pltpu.make_async_copy(src, dst, keep)

    def item(ii, carry):
        i = flip(p // g.sub, g.Ic - 1 - ii, g.bits)
        rows = pl.ds(pl.multiple_of(i * g.L, g.L), g.L)
        row = c * g.Ic + i
        normed, _ = norm(tok[rows].astype(F32))
        hidden = (
            normed * (1.0 + mod[1, pl.ds(row, 1), :]) + mod[0, pl.ds(row, 1), :]
        ).astype(BF)
        h1[rows] = hidden
        for s in range(2):
            wide = nt(weights[s][...], hidden)
            core = c + s - 2 * c * s
            parts = split_heads(g, wide)
            rowsum = smc[s].astype(BF)
            bias = []
            for r in (1, 2):
                line = jnp.where(lax.broadcasted_iota(jnp.int32, (8, g.hw), 0) == r, rowsum[:, : g.hw].astype(F32), 0.0)
                bias.append(tn(line.astype(BF), ones))
            for h in range(g.lh):
                hh = s * g.lh + h
                rows_h = slice(h * g.hd, (h + 1) * g.hd)
                q = (parts[h] + bias[0][rows_h]).astype(BF)
                k = parts[g.lh + h].astype(BF)
                v = (parts[2 * g.lh + h] + bias[1][rows_h]).astype(BF)
                qkv[hh * 3 + 0, :, rows] = q
                qkv[hh * 3 + 1, :, rows] = k
                qkv[hh * 3 + 2, :, rows] = v
                scores = tn(k, q) * scale
                peak = jnp.max(scores, axis=0, keepdims=True)
                powers = jnp.exp(scores - peak)
                total = jnp.sum(powers, axis=0, keepdims=True)
                lse[hh : hh + 1, rows] = peak + jnp.log(total)
                probs = (powers * (1.0 / total)).astype(BF)
                mixed = nn(v, probs)
                gate = gat[s, pl.ds(row, 1), 2 * h : 2 * h + 1]
                gsend[i, core, rows_h, :] = (mixed * gate).astype(BF)
        for u in range(g.sub):
            j = i * g.sub + u

            @pl.when(j == p)
            def _():
                home().start()

            @pl.when(j != p)
            def _():
                away(j).start()

        return carry

    lax.fori_loop(0, g.Ic, item, 0)
    home().wait()
    for k in range(1, g.G):
        arrive(flip(p, k, g.bits)).wait_recv()
    heads = gbuf[...].reshape(g.T * g.hw, g.Ro)
    gath[...] = heads
    for k in range(1, g.G):
        share(k).wait_recv()
        forward(k).start()
    for k in range(g.G):
        forward(k).wait_recv()
    full = wob[...].reshape(g.T * g.hw, g.W)
    wof[...] = full
    attention = tn(heads, full) + ob[...]
    own = c * g.Ic + p // g.sub
    base = tok[pl.ds(pl.multiple_of(p * g.Ro, g.Ro), g.Ro)].astype(F32)
    residual = base + mod[2, pl.ds(own, 1), :] * attention
    att[...] = attention
    res[...] = residual
    normed, _ = norm(residual)
    h2[...] = (normed * (1.0 + mod[4, pl.ds(own, 1), :]) + mod[3, pl.ds(own, 1), :]).astype(BF)
    for k in range(1, g.G):
        away(flip(p, k, g.bits)).wait_send()
        share(k).wait_send()
    for k in range(g.G):
        forward(k).wait_send()


def feed_kernel(
    g, h2, cotangent, mod, gat, smc, we_in, wex_in, wr_in, wrx_in,
    grad_out, mpart, dwf, small, gates, ebs,
    cot, we, wex, wr, wrx, h2buf, bgbuf, gch, egb, sgb, rgb, own_g, xs, xr,
    load, send_h, recv_h, send_g, recv_g, send_p, recv_p,
):
    d, t, p, c = g.place()
    partner = (d, p * 2 + 1 - c)
    wec = (we, wex)
    wrc = (wr, wrx)

    def chip(k):
        return (d, flip(p, k, g.bits) * 2 + c)

    cot_rows = cotangent.at[pl.ds(pl.multiple_of(c * g.Rc, g.Rc), g.Rc)]
    loads = [
        pltpu.make_async_copy(src, dst, load.at[index])
        for index, (src, dst) in enumerate(
            ((cot_rows, cot), (wr_in, wr), (wrx_in, wrx), (we_in, we), (wex_in, wex))
        )
    ]
    for copy in loads:
        copy.start()
    meet([chip(k) for k in range(1, g.G)] + [partner])

    def spread(k):
        return remote(h2, h2buf.at[k], send_h.at[k], recv_h.at[k], chip(k))

    for k in range(1, g.G):
        spread(k).start()
    h2buf[0] = h2[...]
    for copy in loads:
        copy.wait()
    lane = lax.broadcasted_iota(jnp.int32, (1, g.ch), 1)
    tile_row = lax.broadcasted_iota(jnp.int32, (8, 128), 0)
    tile_lane = lax.broadcasted_iota(jnp.int32, (8, 128), 1)
    ebs[...] = jnp.zeros_like(ebs)
    gates[...] = jnp.zeros_like(gates)

    def back(k):
        return remote(sgb.at[k - 1], rgb.at[k - 1], send_g.at[k], recv_g.at[k], chip(k))

    def block(k, carry):
        j = flip(p, k, g.bits)
        local = j // g.sub
        item = c * g.Ic + local
        rows = pl.ds(pl.multiple_of(j * g.Ro, g.Ro), g.Ro)
        here = pl.ds(pl.multiple_of(k * g.Ro, g.Ro), g.Ro)
        branch = (mod[5, pl.ds(item, 1), :] * cot[rows].astype(F32)).astype(BF)
        bgbuf[here] = branch
        grads = [nt(branch, wrc[s][...]) for s in range(2)]

        @pl.when(k > 0)
        def _():
            spread(k).wait_recv()

        hidden = h2buf[k]
        total = None
        for s in range(2):
            wide = nt(hidden, wec[s][...]) + smc[s, 0:1, : g.ch]
            inner = GELU_A * (wide + GELU_B * wide * wide * wide)
            tanh = jnp.tanh(inner)
            act = 0.5 * wide * (1.0 + tanh)
            slope = 0.5 * (1.0 + tanh) + 0.5 * wide * (1.0 - tanh * tanh) * (
                GELU_A * (1.0 + 3.0 * GELU_B * wide * wide)
            )
            gate = gat[s, pl.ds(item, 1), 1:2]
            for h in range(1, g.lh):
                gate = jnp.where(lane >= h * g.gc, gat[s, pl.ds(item, 1), 2 * h + 1 : 2 * h + 2], gate)
            gch[s, here] = (act * gate).astype(BF)
            line = jnp.sum(grads[s] * act, axis=0, keepdims=True)
            tile = gates[s]
            for h in range(g.lh):
                inside = jnp.where((lane >= h * g.gc) & (lane < (h + 1) * g.gc), line, 0.0)
                value = jnp.sum(inside, axis=1, keepdims=True)
                tile = tile + jnp.where((tile_row == local) & (tile_lane == 2 * h + 1), value, 0.0)
            gates[s] = tile
            egrad = (grads[s] * gate * slope).astype(BF)
            egb[s, here] = egrad
            ebs[s, 0:1, : g.ch] += jnp.sum(egrad.astype(F32), axis=0, keepdims=True)
            part = nn(egrad, wec[s][...])
            total = part if total is None else total + part

        @pl.when(k > 0)
        def _():
            sgb[k - 1] = total.astype(BF)
            back(k).start()

        @pl.when(k == 0)
        def _():
            own_g[...] = total

        return carry

    lax.fori_loop(0, g.G, block, 0)
    xs[0] = tn(gch[1], bgbuf[...]).astype(BF)

    def swap(index):
        return remote(xs.at[index], xr.at[index], send_p.at[index], recv_p.at[index], partner)

    swap(0).start()
    xs[1] = tn(egb[1], h2buf[...].reshape(g.Rc, g.W)).astype(BF)
    swap(1).start()
    unit = g.ch // g.units
    for index, (left, right) in enumerate(
        ((gch[0], bgbuf[...]), (egb[0], h2buf[...].reshape(g.Rc, g.W)))
    ):
        value = tn(left, right)
        swap(index).wait_recv()
        value = (value + xr[index].astype(F32)).astype(BF)
        for u in range(g.units):
            dwf[index * g.units + u] = value[u * unit : (u + 1) * unit]
    for k in range(g.G):
        rows = pl.ds(k * g.Ro, g.Ro)
        mpart[k] = (nn(gch[0, rows], wr[...]) + nn(gch[1, rows], wrx[...])).astype(BF)
    small[...] = jnp.zeros_like(small)
    small[7:8, :] = jnp.sum(bgbuf[0 : g.Ro].astype(F32), axis=0, keepdims=True)
    grad = own_g[...]
    for k in range(1, g.G):
        back(k).wait_recv()
        grad = grad + rgb[k - 1].astype(F32)
    grad_out[...] = grad
    for k in range(1, g.G):
        spread(k).wait_send()
        back(k).wait_send()
    swap(0).wait_send()
    swap(1).wait_send()


def unattend_kernel(
    g, hgrad, h1, qkv, lse, gat, wi, wix, small_in, mpart, dwf, mod, att, res, wof, gath, cotangent, rbias, ebs,
    gates_in,
    grad, rgrad, bout, dwz, dwf_out, lines, sums, pay, gates,
    hgs, hgbuf, wof_x, orr, osum, small, dqkv, acc, own_g, sgb, rgb, rmb, xs, xr, orv, sx, cot,
    work, inbox, send_z, recv_z,
    send_g, recv_g, send_m, recv_m, send_o, recv_o, send_s, recv_s, send_p, recv_p, send_a, recv_a, send_x, recv_x,
    load,
):
    d, t, p, c = g.place()
    partner = (d, p * 2 + 1 - c)
    weights = (wi, wix)
    block = c * g.G + p

    def chip(k):
        return (d, flip(p, k, g.bits) * 2 + c)

    def peer(k):
        return (d, flip(t, k, g.tbits))

    def group(k):
        return (flip(d, k, g.dbits), t)

    fetch = pltpu.make_async_copy(
        cotangent.at[pl.ds(pl.multiple_of(block * g.Ro, g.Ro), g.Ro)], cot, load.at[0]
    )
    fetch.start()
    half = pltpu.make_async_copy(dwf, work, load.at[1])
    half.start()
    first = pltpu.make_async_copy(mpart.at[0], rmb.at[0], load.at[2])
    first.start()
    meet([peer(k) for k in range(1, g.T)] + [group(k) for k in g.flips])

    def rest(k):
        return remote(osum.at[flip(p, k, g.bits)], orv.at[k - 1], send_o.at[k], recv_o.at[k], chip(k))

    def on(k):
        return remote(mpart.at[k], rmb.at[k], send_m.at[k], recv_m.at[k], chip(k))

    def sumup(k):
        return remote(small, sx.at[k], send_s.at[k], recv_s.at[k], peer(k))

    def heads_out(k):
        return remote(hgs.at[pl.ds(flip(p, k, g.bits) * 2, 2)], hgbuf.at[k], send_a.at[k], recv_a.at[k], chip(k))

    def cross(q):
        return remote(wof_x.at[2 * q + 1 - c], orr.at[q], send_x.at[q], recv_x.at[q], partner)

    half.wait()
    zsum = GroupSum(g, work, inbox, dwf_out, send_z, recv_z, group)
    zsum.start(0)
    fetch.wait()
    value = hgrad[...]
    own = c * g.Ic + p // g.sub
    normed, inverse = norm(res[...])
    cot_own = cot[...].astype(F32)
    residual = cot_own + norm_back(value * (1.0 + mod[4, pl.ds(own, 1), :]), normed, inverse)
    branch_one = (mod[2, pl.ds(own, 1), :] * residual).astype(BF)
    hgs[...] = nt(wof[...], branch_one).astype(BF).reshape(g.T, g.hw, g.Ro)
    for k in range(1, g.G):
        heads_out(k).start()
    hgbuf[0] = hgs[pl.ds(p * 2, 2)]
    for k in range(1, g.G):
        on(k).start()
    rgrad[...] = residual
    small[...] = small_in[...]
    small[2:3, :] = jnp.sum(residual * att[...], axis=0, keepdims=True)
    small[3:4, :] = jnp.sum(value, axis=0, keepdims=True)
    small[4:5, :] = jnp.sum(value * normed, axis=0, keepdims=True)
    small[6:7, :] = jnp.sum(branch_one.astype(F32), axis=0, keepdims=True)
    for k in range(1, g.T):
        sumup(k).start()
    wof_x[...] = nn(gath[...], branch_one).astype(BF).reshape(g.T, g.hw, g.W)
    for q in range(g.G):
        cross(q).start()
    scale = 1.0 / math.sqrt(g.hd)
    acc[...] = jnp.zeros_like(acc)
    ones = jnp.ones((8, g.L), BF)
    tile_row = lax.broadcasted_iota(jnp.int32, (8, 128), 0)
    tile_lane = lax.broadcasted_iota(jnp.int32, (8, 128), 1)
    gates[...] = gates_in[...]
    pay[...] = ebs[...]

    def back(k):
        return remote(sgb.at[k - 1], rgb.at[k - 1], send_g.at[k], recv_g.at[k], chip(k))

    def item(ii, carry):
        i = flip(p // g.sub, ii, g.bits)
        row = c * g.Ic + i
        rows = pl.ds(pl.multiple_of(i * g.L, g.L), g.L)
        slots = [ii * g.sub + (flip(lax.rem(p, g.sub), u, 4) if g.sub > 1 else 0) for u in range(g.sub)]
        hidden = h1[rows]
        total = None
        for u, slot in enumerate(slots):

            @pl.when(slot != 0)
            def _():
                heads_out(slot).wait_recv()

        @pl.when(ii == 1)
        def _():
            for q in range(g.G):
                cross(q).wait()
                osum[q] = (wof_x[2 * q + c].astype(F32) + orr[q].astype(F32)).astype(BF)
            for k in range(1, g.G):
                rest(k).start()

        @pl.when(ii == g.Ic - 1)
        def _():
            zsum.add(0)
            if g.dbits > 1:
                zsum.start(1)

        for s in range(2):
            core = c + s - 2 * c * s
            tile = gates[s]
            for h in range(g.lh):
                hh = s * g.lh + h
                q = qkv[hh * 3 + 0, :, rows]
                k = qkv[hh * 3 + 1, :, rows]
                v = qkv[hh * 3 + 2, :, rows]
                pieces = [hgbuf[slot, core, h * g.hd : (h + 1) * g.hd, :] for slot in slots]
                heads = (pieces[0] if g.sub == 1 else jnp.concatenate(pieces, axis=1)).astype(F32)
                probs = jnp.exp(tn(k, q) * scale - lse[hh : hh + 1, rows])
                low = probs.astype(BF)
                mixed = nn(v, low)
                value = jnp.sum(jnp.sum(heads * mixed, axis=0, keepdims=True), axis=1, keepdims=True)
                tile = tile + jnp.where((tile_row == i) & (tile_lane == 2 * h), value, 0.0)
                mixed_grad = (gat[s, pl.ds(row, 1), 2 * h : 2 * h + 1] * heads).astype(BF)
                probs_grad = tn(v, mixed_grad)
                values_grad = nt(mixed_grad, low)
                score = (
                    probs * (probs_grad - jnp.sum(probs_grad * probs, axis=0, keepdims=True))
                ).astype(BF)
                queries_grad = nn(k, score) * scale
                keys_grad = nt(q, score) * scale
                for r, value in enumerate((queries_grad, keys_grad, values_grad)):
                    dqkv[s, r * g.hw + h * g.hd : r * g.hw + (h + 1) * g.hd, :] = value.astype(BF)
            gates[s] = tile
            wide = dqkv[s]
            part = tn(wide, weights[s][...])
            total = part if total is None else total + part
            acc[s] += nn(wide, hidden)
            pay[s, 1:2, : 3 * g.hw] += nt(ones, wide)[0:1]
        for u, slot in enumerate(slots):
            piece = total[u * g.Ro : (u + 1) * g.Ro]

            @pl.when(slot == 0)
            def _():
                own_g[...] = piece

            @pl.when(slot != 0)
            def _():
                sgb[slot - 1] = piece.astype(BF)
                back(slot).start()

        return carry

    lax.fori_loop(0, g.Ic, item, 0)
    xs[...] = acc[1].astype(BF)
    swap = remote(xs, xr, send_p, recv_p, partner)
    swap.start()
    for step in range(1, g.dbits):
        zsum.add(step)
        if step + 1 < g.dbits:
            zsum.start(step + 1)
    zsum.spread_start(g.halvings - 1)
    value = small[...]
    for k in range(1, g.T):
        sumup(k).wait()
        value = value + sx[k]
    sums[...] = value
    out = osum[p].astype(F32)
    for k in range(1, g.G):
        rest(k).wait()
        out = out + orv[k - 1].astype(F32)
    swap.wait()
    for u in range(2 * g.units):
        low = u * g.zr
        if low < 3 * g.hw:
            span = slice(low, low + g.zr)
            dwz[u] = (acc[0, span] + xr[span].astype(F32)).astype(BF)
        else:
            dwz[u] = out[low - 3 * g.hw : low - 3 * g.hw + g.zr].astype(BF)
    for step in reversed(range(g.halvings - 1)):
        zsum.spread_wait(step + 1)
        zsum.spread_start(step)
    first.wait()
    branch = rmb[0].astype(F32)
    for k in range(1, g.G):
        on(k).wait()
        branch = branch + rmb[k].astype(F32)
    branch = branch + rbias[...]
    bout[...] = (res[...] + mod[5, pl.ds(own, 1), :] * branch).astype(BF)
    lines[...] = small[...]
    lines[5:6, :] = jnp.sum(cot[...].astype(F32) * branch, axis=0, keepdims=True)
    value = own_g[...]
    for k in range(1, g.G):
        back(k).wait()
        value = value + rgb[k - 1].astype(F32)
    grad[...] = value
    zsum.spread_wait(0)
    zsum.sent()
    for k in range(1, g.G):
        heads_out(k).wait_send()


def finish_kernel(
    g, grad, rgrad, tokens, mod, lines_in, sums, bout, pay, gates, dsg, dwz,
    tall, ball, colall, zall, logall, dwz_out,
    tok, tsend, stage, cbuf, zbuf, lbuf, pbuf, gbuf, work, inbox, send_z, recv_z,
    load, send_t, recv_t, send_f, recv_f, send_c, recv_c, send_p, recv_p, send_s, recv_s, keep,
):
    d, t, p, c = g.place()
    partner = (d, p * 2 + 1 - c)

    def chip(k):
        return (d, flip(p, k, g.bits) * 2 + c)

    def peer(k):
        return (d, flip(t, k, g.tbits))

    def group(k):
        return (flip(d, k, g.dbits), t)

    meet([peer(k) for k in range(1, g.T)] + [group(k) for k in range(1, g.D)])
    block = c * g.G + p
    mine = pl.ds(pl.multiple_of(block * g.Ro, g.Ro), g.Ro)
    copy = pltpu.make_async_copy(tokens.at[mine], tok, load)
    copy.start()
    swaps = [
        remote(pay.at[1], pbuf, send_p.at[0], recv_p.at[0], partner),
        remote(gates.at[1], gbuf, send_p.at[1], recv_p.at[1], partner),
    ]
    for swap in swaps:
        swap.start()
    zsum = GroupSum(g, work, inbox, dwz_out, send_z, recv_z, group)
    work[...] = dwz[...]
    zsum.start(0)

    def spread(which, src, dst, k):
        return remote(src, dst.at[mine], send_t.at[which, k], recv_t.at[which, k], chip(k))

    for k in range(1, g.G):
        spread(0, bout, ball, k).start()
    copy.wait()
    own = c * g.Ic + p // g.sub
    normed, inverse = norm(tok[...].astype(F32))
    value = grad[...]
    scaled = value * (1.0 + mod[1, pl.ds(own, 1), :])
    tsend[...] = (rgrad[...] + norm_back(scaled, normed, inverse)).astype(BF)
    lines = lines_in[...]
    kind = lax.broadcasted_iota(jnp.int32, lines.shape, 0)
    first = jnp.sum(value, axis=0, keepdims=True)
    second = jnp.sum(value * normed, axis=0, keepdims=True)
    lines = jnp.where(kind == 0, first, jnp.where(kind == 1, second, lines))
    w = g.mw
    stage[...] = jnp.zeros_like(stage)
    for member in range(g.T):
        stage[member, :, :w] = lines[:, member * w : (member + 1) * w]

    def columns(k):
        return remote(stage.at[flip(t, k, g.tbits)], cbuf.at[d, t], send_c.at[k], recv_c.at[k], peer(k))

    def column_in(k):
        return remote(stage.at[t], cbuf.at[d, flip(t, k, g.tbits)], send_c.at[k], recv_c.at[k], peer(k))

    for k in range(1, g.T):
        columns(k).start()
    cbuf[d, t] = stage[t]
    for k in range(1, g.G):
        spread(1, tsend, tall, k).start()
    local = [
        pltpu.make_async_copy(bout, ball.at[mine], keep.at[0]),
        pltpu.make_async_copy(tsend, tall.at[mine], keep.at[1]),
    ]
    for item in local:
        item.start()

    def forward(which, dst, k):
        rows = pl.ds(pl.multiple_of((c * g.G + flip(p, k, g.bits)) * g.Ro, g.Ro), g.Ro)
        return remote(dst.at[rows], dst.at[rows], send_f.at[which, k], recv_f.at[which, k], partner)

    def arrive(which, dst, k):
        rows = pl.ds(pl.multiple_of((c * g.G + flip(p, k, g.bits)) * g.Ro, g.Ro), g.Ro)
        return remote(bout, dst.at[rows], send_t.at[which, k], recv_t.at[which, k], chip(k))

    def arrive_forward(which, dst, k):
        rows = pl.ds(pl.multiple_of(((1 - c) * g.G + flip(p, k, g.bits)) * g.Ro, g.Ro), g.Ro)
        return remote(dst.at[rows], dst.at[rows], send_f.at[which, k], recv_f.at[which, k], partner)

    for step in range(g.dbits):
        zsum.add(step)
        if step + 1 < g.dbits:
            zsum.start(step + 1)
    zsum.spread_start(g.halvings - 1)
    for swap in swaps:
        swap.wait()
    zbuf[d] = jnp.zeros((8, g.W), F32)
    zbuf[d, 0:2] = pay[0, 0:2] + pbuf[0:2]
    zbuf[d, 2:4] = sums[6:8]
    both = jnp.concatenate([gates[0, : g.Ic], gbuf[: g.Ic]], axis=0)
    turned = jnp.concatenate([gbuf[: g.Ic], gates[0, : g.Ic]], axis=0)
    lbuf[d] = jnp.where(c == 0, both, turned) * dsg[...]
    for step in reversed(range(g.halvings - 1)):
        zsum.spread_wait(step + 1)
        zsum.spread_start(step)
    for k in range(1, g.T):
        columns(k).wait_send()
        column_in(k).wait_recv()

    def share(k):
        return [
            remote(cbuf.at[d], cbuf.at[d], send_s.at[0, k], recv_s.at[0, k], group(k)),
            remote(zbuf.at[d], zbuf.at[d], send_s.at[1, k], recv_s.at[1, k], group(k)),
            remote(lbuf.at[d], lbuf.at[d], send_s.at[2, k], recv_s.at[2, k], group(k)),
        ]

    def shared(k):
        other = flip(d, k, g.dbits)
        return [
            remote(cbuf.at[other], cbuf.at[other], send_s.at[0, k], recv_s.at[0, k], group(k)),
            remote(zbuf.at[other], zbuf.at[other], send_s.at[1, k], recv_s.at[1, k], group(k)),
            remote(lbuf.at[other], lbuf.at[other], send_s.at[2, k], recv_s.at[2, k], group(k)),
        ]

    for k in range(1, g.D):
        for item in share(k):
            item.start()
    for which, dst in ((0, ball), (1, tall)):
        local[which].wait()
        forward(which, dst, 0).start()
    for k in range(1, g.G):
        arrive(0, ball, k).wait_recv()
        forward(0, ball, k).start()
    for k in range(1, g.D):
        for item in share(k):
            item.wait_send()
        for item in shared(k):
            item.wait_recv()
    colall[...] = cbuf[...]
    zall[...] = zbuf[...]
    logall[...] = lbuf[...]
    for k in range(1, g.G):
        arrive(1, tall, k).wait_recv()
        forward(1, tall, k).start()
    zsum.spread_wait(0)
    zsum.sent()
    for which, src, dst in ((0, bout, ball), (1, tsend, tall)):
        for k in range(1, g.G):
            spread(which, src, dst, k).wait_send()
        for k in range(g.G):
            forward(which, dst, k).wait_send()
            arrive_forward(which, dst, k).wait_recv()


def wrap_kernel(g, colall, zall, logall, conds, dwm, dmb, drw, drb, dib, vectors):
    rows = []
    for member in range(g.T):
        rows.append(((member % 2) * g.G + member // 2) * g.Ro // g.L)
    value = conds[...]
    silu = value / (1.0 + jnp.exp(-value))
    picked = jnp.concatenate([silu[z, i : i + 1] for z in range(g.D) for i in rows], axis=0).astype(BF)
    twice = jnp.concatenate([picked, picked], axis=0)
    w = g.mw
    for row in range(6):
        part = jnp.concatenate(
            [colall[z, member, row : row + 1, :] for z in range(g.D) for member in range(g.T)], axis=0
        )
        dmb[row : row + 1, :] = jnp.sum(part, axis=0, keepdims=True)[:, :w]
        high = part.astype(BF)
        low = (part - high.astype(F32)).astype(BF)
        dwm[row * w : (row + 1) * w, :] = tn(jnp.concatenate([high, low], axis=0), twice)[:w]
    logits = jnp.concatenate([logall[z] for z in range(g.D)], axis=0)
    high = logits.astype(BF)
    low = (logits - high.astype(F32)).astype(BF)
    flat = jnp.concatenate([value[z] for z in range(g.D)], axis=0).astype(BF)
    router = tn(jnp.concatenate([high, low], axis=0), jnp.concatenate([flat, flat], axis=0))
    sums = jnp.sum(logits, axis=0, keepdims=True)
    for h in range(g.lh):
        drw[h] = router[2 * h : 2 * h + 2, :]
        drb[h : h + 1, :] = sums[:, 2 * h : 2 * h + 2]
    total = zall[0]
    for z in range(1, g.D):
        total = total + zall[z]
    dib[0:1, :] = total[1:2, : g.hw]
    dib[1:2, :] = total[1:2, 2 * g.hw : 3 * g.hw]
    vectors[...] = total


def body(
    groups, members,
    tokens, condition, timesteps, route_masks, modulate_weight, modulate_bias, input_weight, input_bias,
    output_weight, output_bias, expand_weight, expand_bias, reduce_weight, reduce_bias, router_weight, router_bias,
    out_cotangent,
):
    g = Plan(
        groups, members, tokens.shape[0], condition.shape[0], tokens.shape[1], router_weight.shape[1],
        modulate_weight.shape[2], input_weight.shape[2], expand_weight.shape[1],
    )
    dma = pltpu.SemaphoreType.DMA
    V = pltpu.VMEM
    W, T, G, D, I = g.W, g.T, g.G, g.D, g.I
    wide = 2 * g.lh
    wm = jnp.transpose(modulate_weight, (1, 2, 0)).reshape(6 * g.mw, W)
    wi = jnp.transpose(input_weight, (1, 2, 0)).reshape(3 * g.hw, W)
    we = expand_weight.T
    wr = reduce_weight
    rw = jnp.transpose(router_weight, (1, 2, 0))
    masks = jnp.transpose(route_masks, (1, 2, 0))
    eb = expand_bias.astype(F32)[None]
    ob = output_bias.astype(F32)[None]
    rbias = reduce_bias.astype(F32)[None]
    ru = g.ch // g.units

    mod, gat, dsg, smc, conds, wix, wex, wrx = call(
        functools.partial(start_kernel, g), "start",
        (condition, wm, modulate_bias, timesteps, masks, rw, router_bias, eb, input_bias, wi, we, wr),
        "vvvsvvvvvhhh",
        [
            ((6, I, W), F32), ((2, I, 128), F32), ((I, 128), F32), ((2, 8, W), F32), ((D, I, W), F32),
            ((3 * g.hw, W), BF), ((g.ch, W), BF), ((g.ch, W), BF),
        ],
        "vvvvvhhh",
        [
            V((T, I, 6 * g.mw), F32), V((2, I, 128), F32), V((2, 8, W), F32), V((D, I, W), F32),
            dma((T,)), dma((T,)), dma((5,)), dma((5,)), dma((D,)), dma((D,)),
        ],
        1,
    )
    h1, qkv, lse, att, res, h2, gath, wof = call(
        functools.partial(attend_kernel, g), "attend",
        (tokens, mod, gat, smc, wi, wix, output_weight, ob), "hvvvvvvv",
        [
            ((g.Rc, W), BF), ((wide * 3, g.hd, g.Rc), BF), ((wide, g.Rc), F32),
            ((g.Ro, W), F32), ((g.Ro, W), F32), ((g.Ro, W), BF), ((T * g.hw, g.Ro), BF), ((T * g.hw, W), BF),
        ],
        "vvvvvvvv",
        [
            V((g.Rc, W), BF), V((g.Ic, 2, g.hw, g.L), BF), V((T, g.hw, g.Ro), BF), V((T, g.hw, W), BF),
            dma, dma, dma((G,)), dma((G,)), dma((G,)), dma((G,)), dma((G,)), dma((G,)),
        ],
        2,
    )
    hgrad, mpart, dwf, small, gates, ebs = call(
        functools.partial(feed_kernel, g), "feed",
        (h2, out_cotangent, mod, gat, smc, we, wex, wr, wrx), "vhvvvhhhh",
        [
            ((g.Ro, W), F32), ((G, g.Ro, W), BF), ((2 * g.units, ru, W), BF),
            ((8, W), F32), ((2, 8, 128), F32), ((2, 8, W), F32),
        ],
        "vvvvvv",
        [
            V((g.Rc, W), BF), V((g.ch, W), BF), V((g.ch, W), BF), V((g.ch, W), BF), V((g.ch, W), BF),
            V((G, g.Ro, W), BF), V((g.Rc, W), BF), V((2, g.Rc, g.ch), BF), V((2, g.Rc, g.ch), BF),
            V((G - 1, g.Ro, W), BF), V((G - 1, g.Ro, W), BF), V((g.Ro, W), F32),
            V((2, g.ch, W), BF), V((2, g.ch, W), BF),
            dma((5,)), dma((G,)), dma((G,)), dma((G,)), dma((G,)), dma((2,)), dma((2,)),
        ],
        3,
    )
    grad, rgrad, bout, dwz, dwf, lines, sums, pay, gates = call(
        functools.partial(unattend_kernel, g), "unattend",
        (
            hgrad, h1, qkv, lse, gat, wi, wix, small, mpart, dwf, mod, att, res, wof, gath, out_cotangent, rbias, ebs,
            gates,
        ),
        "vvvvvvvvhhvvvvvhvvv",
        [
            ((g.Ro, W), F32), ((g.Ro, W), F32), ((g.Ro, W), BF), ((2 * g.units, g.zr, W), BF),
            ((2 * g.units, ru, W), BF), ((8, W), F32), ((8, W), F32), ((2, 8, W), F32), ((2, 8, 128), F32),
        ],
        "vvvvvvvvv",
        [
            V((T, g.hw, g.Ro), BF), V((G, 2, g.hw, g.Ro), BF), V((T, g.hw, W), BF), V((G, g.hw, W), BF),
            V((G, g.hw, W), BF), V((8, W), F32),
            V((2, 3 * g.hw, g.L), BF), V((2, 3 * g.hw, W), F32), V((g.Ro, W), F32), V((G - 1, g.Ro, W), BF),
            V((G - 1, g.Ro, W), BF), V((G, g.Ro, W), BF), V((3 * g.hw, W), BF), V((3 * g.hw, W), BF),
            V((G - 1, g.hw, W), BF), V((T, 8, W), F32), V((g.Ro, W), BF),
        ]
        + GroupSum.scratch(g, ru)
        + [
            dma((G,)), dma((G,)), dma((G,)), dma((G,)), dma((G,)), dma((G,)), dma((T,)), dma((T,)), dma, dma,
            dma((G,)), dma((G,)), dma((G,)), dma((G,)), dma((3,)),
        ],
        4,
    )
    tall, ball, colall, zall, logall, dwz = call(
        functools.partial(finish_kernel, g), "finish",
        (grad, rgrad, tokens, mod, lines, sums, bout, pay, gates, dsg, dwz), "vvhvvvvvvvv",
        [
            ((g.R, W), BF), ((g.R, W), BF), ((D, T, 8, g.cw), F32), ((D, 8, W), F32), ((D, I, 128), F32),
            ((2 * g.units, g.zr, W), BF),
        ],
        "hhvvvv",
        [
            V((g.Ro, W), BF), V((g.Ro, W), BF), V((T, 8, g.cw), F32), V((D, T, 8, g.cw), F32), V((D, 8, W), F32),
            V((D, I, 128), F32), V((8, W), F32), V((8, 128), F32),
        ]
        + GroupSum.scratch(g, g.zr)
        + [
            dma, dma((2, G)), dma((2, G)), dma((2, G)), dma((2, G)), dma((T,)), dma((T,)), dma((2,)), dma((2,)),
            dma((3, D)), dma((3, D)), dma((2,)),
        ],
        5,
    )
    dwm, dmb, drw, drb, dib, vectors = call(
        functools.partial(wrap_kernel, g), "wrap", (colall, zall, logall, conds), "vvvv",
        [
            ((6 * g.mw, W), F32), ((6, g.mw), F32), ((g.lh, 2, W), F32), ((g.lh, 2), F32), ((2, g.hw), F32),
            ((8, W), F32),
        ],
        "vvvvvv", [], None,
    )
    dwf = dwf.astype(F32).reshape(2, g.ch, W)
    dwz = dwz.astype(F32).reshape(4 * g.hw, W)
    return (
        ball.astype(F32),
        tall.astype(F32),
        jnp.transpose(dwm.reshape(6, g.mw, W), (2, 0, 1)),
        dmb,
        jnp.transpose(dwz[: 3 * g.hw].reshape(3, g.hw, W), (2, 0, 1)),
        dib,
        dwz[3 * g.hw :],
        vectors[2],
        dwf[1].T,
        vectors[0, : g.ch],
        dwf[0],
        vectors[3],
        jnp.transpose(drw, (2, 0, 1)),
        drb,
    )


def solution(mesh):
    return jax.shard_map(
        functools.partial(body, mesh.shape["dp"], mesh.shape["tensor"]),
        mesh=mesh,
        in_specs=(
            P("dp", None), P("dp", None), P("dp"), P(None, "tensor", None), P(None, None, "tensor"),
            P(None, "tensor"), P(None, None, "tensor"), P(None, "tensor"), P("tensor", None), P(),
            P(None, "tensor"), P("tensor"), P("tensor", None), P(), P(None, "tensor", None), P("tensor", None),
            P("dp", None),
        ),
        out_specs=(
            P("dp", None), P("dp", None), P(None, None, "tensor"), P(None, "tensor"), P(None, None, "tensor"),
            P(None, "tensor"), P("tensor", None), P(), P(None, "tensor"), P("tensor"), P("tensor", None), P(),
            P(None, "tensor", None), P("tensor", None),
        ),
        check_vma=False,
    )
```

```python
import functools
import math

import jax
import jax.numpy as jnp
from jax import lax
from jax.experimental import pallas as pl
from jax.experimental.pallas import tpu as pltpu
from jax.sharding import PartitionSpec as P

BF = jnp.bfloat16
F32 = jnp.float32
MESH = pl.DeviceIdType.MESH
EPSILON = 1e-06
GELU_A = math.sqrt(2.0 / math.pi)
GELU_B = 0.044715
VMEM_LIMIT = 58 << 20


def nt(left, right):
    return lax.dot_general(left, right, (((1,), (1,)), ((), ())), preferred_element_type=F32)


def nn(left, right):
    return lax.dot_general(left, right, (((1,), (0,)), ((), ())), preferred_element_type=F32)


def tn(left, right):
    return lax.dot_general(left, right, (((0,), (0,)), ((), ())), preferred_element_type=F32)


def flip(value, mask, bits):
    total = 0
    for bit in range(bits):
        unit = 1 << bit
        total = total + lax.rem(value // unit + mask // unit, 2) * unit
    return total


def norm(values):
    center = values - jnp.mean(values, axis=-1, keepdims=True)
    inverse = lax.rsqrt(jnp.mean(center * center, axis=-1, keepdims=True) + EPSILON)
    return center * inverse, inverse


def norm_back(grad, normed, inverse):
    mean_grad = jnp.mean(grad, axis=-1, keepdims=True)
    mean_cross = jnp.mean(grad * normed, axis=-1, keepdims=True)
    return inverse * (grad - mean_grad - normed * mean_cross)


class Plan:
    def __init__(self, groups, members, rows, items, width, heads, modwidth, headwidth, channels):
        self.D = groups
        self.T = members
        self.G = members // 2
        self.bits = self.G.bit_length() - 1
        self.tbits = members.bit_length() - 1
        self.dbits = groups.bit_length() - 1
        self.R = rows
        self.I = items
        self.L = rows // items
        self.W = width
        self.Rc = rows // 2
        self.Ro = rows // members
        self.Ic = items // 2
        self.sub = self.L // self.Ro
        self.lh = heads
        self.mw = modwidth
        self.cw = -(-modwidth // 128) * 128
        self.hw = headwidth
        self.hd = headwidth // heads
        self.ch = channels
        self.gc = channels // heads
        self.hr = 2 * headwidth
        self.units = 8
        self.fr = 2 * channels // self.units
        self.zr = 4 * headwidth // self.units
        self.fe = 2
        self.ze = 4

    def place(self):
        d = lax.axis_index("dp")
        t = lax.axis_index("tensor")
        return d, t, t // 2, lax.rem(t, 2)


def meet(devices):
    barrier = pltpu.get_barrier_semaphore()
    for device in devices:
        pl.semaphore_signal(barrier, inc=1, device_id=device, device_id_type=MESH)
    pl.semaphore_wait(barrier, len(devices))


def meet_line(g, devices, group, middle):
    barrier = pltpu.get_barrier_semaphore()
    for device in devices + [group(1)]:
        pl.semaphore_signal(barrier, inc=1, device_id=device, device_id_type=MESH)
    others = [group(3)] + [group(4 << level) for level in range(g.dbits - 2)]

    @pl.when(middle == 1)
    def _():
        for device in others:
            pl.semaphore_signal(barrier, inc=1, device_id=device, device_id_type=MESH)
        pl.semaphore_wait(barrier, len(devices) + 1 + len(others))

    @pl.when(middle == 0)
    def _():
        pl.semaphore_wait(barrier, len(devices) + 1)


def remote(src, dst, send, recv, device):
    return pltpu.make_async_remote_copy(
        src_ref=src, dst_ref=dst, send_sem=send, recv_sem=recv, device_id=device, device_id_type=MESH
    )


class GroupSum:
    def __init__(self, g, count, work, first, second, more, full, sems):
        self.g, self.count, self.work, self.first, self.second = g, count, work, first, second
        self.more, self.full, self.sems = more, full, sems
        self.d, self.t = lax.axis_index("dp"), lax.axis_index("tensor")
        self.middle = lax.rem(lax.rem(self.d, 4) + 1, 4) // 2

    def device(self, mask):
        return (flip(self.d, mask, self.g.dbits), self.t)

    def copy(self, kind, src, dst, unit, mask):
        return remote(src.at[unit], dst.at[unit], self.sems.at[kind, unit], self.sems.at[kind + 1, unit], self.device(mask))

    def up(self, unit):
        return self.copy(0, self.work, self.first, unit, 1)

    def over(self, unit):
        return self.copy(2, self.work, self.second, unit, 3)

    def down(self, unit):
        return self.copy(4, self.full, self.full, unit, 1)

    def across(self, unit, level):
        src = self.more.at[2 * level, unit]
        dst = self.more.at[2 * level + 1, unit]
        kind = 6 + 2 * level
        return remote(src, dst, self.sems.at[kind, unit], self.sems.at[kind + 1, unit], self.device(4 << level))

    def start(self, units):
        @pl.when(self.middle == 0)
        def _():
            for unit in units:
                self.up(unit).start()

    def resume(self, units):
        @pl.when(self.middle == 1)
        def _():
            for unit in units:
                self.over(unit).start()

    def join(self, units):
        @pl.when(self.middle == 1)
        def _():
            for unit in units:
                self.up(unit).wait_recv()
                self.work[unit] = (self.work[unit].astype(F32) + self.first[unit].astype(F32)).astype(BF)
                self.over(unit).start()

    def settle(self, units):
        @pl.when(self.middle == 1)
        def _():
            for unit in units:
                self.over(unit).wait_recv()
                value = (self.work[unit].astype(F32) + self.second[unit].astype(F32)).astype(BF)
                for level in range(self.g.dbits - 2):
                    self.more[2 * level, unit] = value
                    copy = self.across(unit, level)
                    copy.start()
                    copy.wait()
                    value = (value.astype(F32) + self.more[2 * level + 1, unit].astype(F32)).astype(BF)
                self.full[unit] = value
                self.down(unit).start()

    def end(self, units, started):
        @pl.when(self.middle == 0)
        def _():
            for unit in started:
                self.up(unit).wait_send()
            for unit in units:
                self.down(unit).wait_recv()

        @pl.when(self.middle == 1)
        def _():
            for unit in units:
                self.over(unit).wait_send()
                self.down(unit).wait_send()

    @staticmethod
    def scratch(g, count, rows):
        levels = max(g.dbits - 2, 0)
        return [
            pltpu.VMEM((count, rows, g.W), BF), pltpu.VMEM((count, rows, g.W), BF), pltpu.VMEM((count, rows, g.W), BF),
            pltpu.VMEM((max(2 * levels, 1), count if levels else 1, rows if levels else 16, g.W), BF),
            pltpu.SemaphoreType.DMA((6 + 2 * levels, count)),
        ]


class FirstLeg:
    def __init__(self, g, units, work, inbox, sems):
        self.g, self.units, self.work, self.inbox, self.sems = g, units, work, inbox, sems
        d = lax.axis_index("dp")
        self.middle = lax.rem(lax.rem(d, 4) + 1, 4) // 2
        self.other = (flip(d, 1, g.dbits), lax.axis_index("tensor"))

    def copy(self, unit):
        return remote(self.work.at[unit], self.inbox.at[unit], self.sems.at[0, unit], self.sems.at[1, unit], self.other)

    def start(self):
        @pl.when(self.middle == 0)
        def _():
            for unit in range(self.units):
                self.copy(unit).start()

    def add(self):
        @pl.when(self.middle == 1)
        def _():
            for unit in range(self.units):
                self.copy(unit).wait_recv()
                self.work[unit] = (self.work[unit].astype(F32) + self.inbox[unit].astype(F32)).astype(BF)

    def sent(self):
        @pl.when(self.middle == 0)
        def _():
            for unit in range(self.units):
                self.copy(unit).wait_send()

    @staticmethod
    def scratch(g, units, rows):
        return [pltpu.VMEM((units, rows, g.W), BF), pltpu.SemaphoreType.DMA((2, units))]


def half(g, ref, which):
    return ref.at[pl.ds(which * (g.Ro // 2), g.Ro // 2)]


class PlaneGather:
    def __init__(self, g, src, place, send, recv, chip, p):
        self.g, self.src, self.place, self.send, self.recv, self.chip, self.p = g, src, place, send, recv, chip, p
        self.relayed = g.G == 4

    def source(self, k):
        return flip(self.p, k, self.g.bits)

    def own(self, k, h):
        g = self.g
        return remote(
            half(g, self.src, h), half(g, self.place(k, self.p), h), self.send.at[k, h], self.recv.at[k, h], self.chip(k)
        )

    def arrival(self, k, h):
        g = self.g
        place = half(g, self.place(k, self.source(k)), h)
        return remote(place, place, self.send.at[k, h], self.recv.at[k, h], self.chip(k))

    def onward(self, h):
        g = self.g
        k = 1 + h
        src = half(g, self.place(k, self.source(k)), h)
        dst = half(g, self.place(3, self.source(k)), h)
        return remote(src, dst, self.send.at[3, h], self.recv.at[3, h], self.chip(2 - h))

    def start(self):
        if self.relayed:
            for k, h in ((1, 0), (2, 1), (1, 1), (2, 0)):
                self.own(k, h).start()
        else:
            for k in range(1, self.g.G):
                for h in range(2):
                    self.own(k, h).start()

    def relay(self):
        if self.relayed:
            for h in range(2):
                self.arrival(1 + h, h).wait_recv()
                self.onward(h).start()

    def wait(self, k):
        for h in range(2):
            if not (self.relayed and k < 3 and h == k - 1):
                self.arrival(k, h).wait_recv()

    def sent(self):
        for h in range(2):
            for k in range(1, 3 if self.relayed else self.g.G):
                self.own(k, h).wait_send()
            if self.relayed:
                self.onward(h).wait_send()


class PlaneScatter:
    def __init__(self, g, part, joint, final, send, recv, chip):
        self.g, self.part, self.joint, self.final = g, part, joint, final
        self.send, self.recv, self.chip = send, recv, chip
        self.relayed = g.G == 4

    def far(self, h):
        return remote(
            half(self.g, self.part(3), h), self.joint.at[h], self.send.at[2, h], self.recv.at[2, h], self.chip(1 + h)
        )

    def near(self, k, h):
        g = self.g
        return remote(
            half(g, self.part(k), h), half(g, self.final.at[k - 1], h), self.send.at[k - 1, h], self.recv.at[k - 1, h],
            self.chip(k),
        )

    def put(self, k):
        if not self.relayed:
            for h in range(2):
                self.near(k, h).start()
        elif isinstance(k, int):
            if k == 3:
                self.far(0).start()
                self.far(1).start()
            else:
                self.near(k, k - 1).start()
        else:
            for kk in range(1, 4):

                @pl.when(k == kk)
                def _():
                    self.put(kk)

    def join(self):
        if self.relayed:
            for h in range(2):
                k = 2 - h
                self.far(h).wait_recv()
                rows = pl.ds(h * (self.g.Ro // 2), self.g.Ro // 2)
                ref = self.part(k)
                ref[rows] = (ref[rows].astype(F32) + self.joint[h].astype(F32)).astype(BF)
                self.near(k, h).start()

    def total(self, value):
        for k in range(1, 3 if self.relayed else self.g.G):
            for h in range(2):
                self.near(k, h).wait_recv()
            value = value + self.final[k - 1].astype(F32)
        return value

    def sent(self):
        for h in range(2):
            for k in range(1, 3 if self.relayed else self.g.G):
                self.near(k, h).wait_send()
            if self.relayed:
                self.far(h).wait_send()

    @staticmethod
    def scratch(g):
        dma = pltpu.SemaphoreType.DMA
        return [
            pltpu.VMEM((2, g.Ro // 2, g.W), BF), pltpu.VMEM((2 if g.G == 4 else g.G - 1, g.Ro, g.W), BF),
            dma((g.G, 2)), dma((g.G, 2)),
        ]


def call(kernel, name, inputs, in_spaces, outs, out_spaces, scratch, collective, cost=None):
    spec = {
        "v": pl.BlockSpec(memory_space=pltpu.VMEM),
        "h": pl.BlockSpec(memory_space=pl.ANY),
        "s": pl.BlockSpec(memory_space=pltpu.SMEM),
    }
    flops, moved = cost or (10**8, 10**7)
    return pl.pallas_call(
        kernel,
        name=name,
        out_shape=[jax.ShapeDtypeStruct(s, t) for s, t in outs],
        in_specs=[spec[x] for x in in_spaces],
        out_specs=[spec[x] for x in out_spaces],
        scratch_shapes=scratch,
        cost_estimate=pl.CostEstimate(flops=flops, bytes_accessed=moved, transcendentals=0),
        compiler_params=pltpu.CompilerParams(
            collective_id=collective, has_side_effects=collective is not None, vmem_limit_bytes=VMEM_LIMIT
        ),
    )(*inputs)


def start_kernel(
    g, cond, wm, mb, ts, masks, rw, rb, eb, ib, wi, we, wr,
    mod, gat, dsg, smc, call_all, wix, wex, wrx,
    mpart, gx, sx, cx, send_m, recv_m, send_w, recv_w, send_c, recv_c,
):
    d, t, p, c = g.place()
    partner = (d, p * 2 + 1 - c)
    meet(
        [(d, flip(t, k, g.tbits)) for k in range(1, g.T)] + [(flip(d, k, g.dbits), t) for k in range(1, g.D)]
    )
    pair = [
        remote(src, dst, send_w.at[index], recv_w.at[index], partner)
        for index, (src, dst) in enumerate(((wi, wix), (we, wex), (wr, wrx)))
    ]
    for copy in pair:
        copy.start()
    value = cond[...]
    silu = (value / (1.0 + jnp.exp(-value))).astype(BF)
    part = nt(silu, wm[...])
    w = g.mw
    bias = mb[...].astype(F32)
    for row in range(6):
        mpart[t, :, row * w : (row + 1) * w] = part[:, row * w : (row + 1) * w] + bias[row : row + 1]

    def spread(k):
        return remote(
            mpart.at[t], mpart.at[t], send_m.at[k], recv_m.at[k], (d, flip(t, k, g.tbits))
        )

    for k in range(1, g.T):
        spread(k).start()
    low = value.astype(BF)
    steps = masks.shape[2]
    row = lax.broadcasted_iota(jnp.int32, (g.I, steps), 0)
    wanted = jnp.zeros((g.I, steps), jnp.int32)
    for item in range(g.I):
        wanted = jnp.where(row == item, ts[item], wanted)
    hot = (wanted == lax.broadcasted_iota(jnp.int32, (g.I, steps), 1)).astype(F32).astype(BF)
    dsg[...] = jnp.zeros_like(dsg)
    gx[0] = jnp.zeros((g.I, 128), F32)
    scale = rb[...].astype(F32)
    for h in range(g.lh):
        logits = nt(low, rw[h]) + scale[h : h + 1]
        sigmoid = 1.0 / (1.0 + jnp.exp(-logits))
        mask = nt(hot, masks[h].astype(F32).astype(BF))
        dsg[:, 2 * h : 2 * h + 2] = mask * sigmoid * (1.0 - sigmoid)
        gx[0, :, 2 * h : 2 * h + 2] = mask * sigmoid
    sx[0] = jnp.zeros((8, g.W), F32)
    sx[0, 0:1, : g.ch] = eb[...]
    sx[0, 1:3, : g.hw] = ib[...].astype(F32)
    small = [
        remote(gx.at[0], gx.at[1], send_w.at[3], recv_w.at[3], partner),
        remote(sx.at[0], sx.at[1], send_w.at[4], recv_w.at[4], partner),
    ]
    for copy in small:
        copy.start()

    def conditions(k):
        return remote(cond, cx.at[d], send_c.at[k], recv_c.at[k], (flip(d, k, g.dbits), t))

    for k in range(1, g.D):
        conditions(k).start()
    cx[d] = value
    for k in range(1, g.T):
        spread(k).wait()
    for member in range(g.T):
        for row in range(6):
            mod[row, :, member * w : (member + 1) * w] = mpart[member, :, row * w : (row + 1) * w]
    for copy in small:
        copy.wait()
    gat[...] = gx[...]
    smc[...] = sx[...]
    for copy in pair:
        copy.wait()
    for k in range(1, g.D):
        conditions(k).wait()
    call_all[...] = cx[...]


def split_heads(g, wide):
    return [wide[r * g.hw + h * g.hd : r * g.hw + (h + 1) * g.hd] for r in range(3) for h in range(g.lh)]


def attend_kernel(
    g, tokens, mod, gat, smc, wi, wix, wo, ob,
    h1_out, qkv_out, lse, att, res, h2, gath, wof,
    tok, h1, qkv, gsend, gbuf, wob, load, keep, save, send, recv, send_o, recv_o, send_f, recv_f,
):
    d, t, p, c = g.place()
    partner = (d, p * 2 + 1 - c)
    weights = (wi, wix)
    copy = pltpu.make_async_copy(tokens.at[pl.ds(pl.multiple_of(c * g.Rc, g.Rc), g.Rc)], tok, load)
    copy.start()
    meet([(d, flip(p, k, g.bits) * 2 + c) for k in range(1, g.G)] + [partner])

    def share(k):
        return remote(wo, wob.at[t], send_o.at[k], recv_o.at[k], (d, flip(p, k, g.bits) * 2 + c))

    def forward(k):
        row = flip(p, k, g.bits) * 2 + c
        src = wo if k == 0 else wob.at[row]
        return remote(src, wob.at[row], send_f.at[k], recv_f.at[k], partner)

    for k in range(1, g.G):
        share(k).start()
    forward(0).start()
    wob[t] = wo[...]
    copy.wait()
    scale = 1.0 / math.sqrt(g.hd)
    ones = jnp.ones((8, g.L), BF)

    def chunk(j):
        i, u = j // g.sub, lax.rem(j, g.sub)
        src = gsend.at[i] if g.sub == 1 else gsend.at[i, :, :, pl.ds(pl.multiple_of(u * g.Ro, g.Ro), g.Ro)]
        return src, gbuf.at[pl.ds(p * 2, 2)]

    def away(j):
        src, dst = chunk(j)
        return remote(src, dst, send.at[j], recv.at[p], (d, j * 2 + c))

    def arrive(j):
        src, _ = chunk(j)
        dst = gbuf.at[pl.ds(j * 2, 2)]
        return remote(src, dst, send.at[j], recv.at[j], (d, j * 2 + c))

    def home():
        src, dst = chunk(p)
        return pltpu.make_async_copy(src, dst, keep)

    def item(ii, carry):
        i = flip(p // g.sub, g.Ic - 1 - ii, g.bits)
        rows = pl.ds(pl.multiple_of(i * g.L, g.L), g.L)
        row = c * g.Ic + i

        @pl.when(ii == g.Ic - 1)
        def _():
            for k in range(1, g.G):
                share(k).wait_recv()
                forward(k).start()

        normed, _ = norm(tok[rows].astype(F32))
        hidden = (
            normed * (1.0 + mod[1, pl.ds(row, 1), :]) + mod[0, pl.ds(row, 1), :]
        ).astype(BF)
        h1[rows] = hidden
        for s in range(2):
            wide = nt(weights[s][...], hidden)
            core = c + s - 2 * c * s
            parts = split_heads(g, wide)
            rowsum = smc[s].astype(BF)
            bias = []
            for r in (1, 2):
                line = jnp.where(lax.broadcasted_iota(jnp.int32, (8, g.hw), 0) == r, rowsum[:, : g.hw].astype(F32), 0.0)
                bias.append(tn(line.astype(BF), ones))
            for h in range(g.lh):
                hh = s * g.lh + h
                rows_h = slice(h * g.hd, (h + 1) * g.hd)
                q = (parts[h] + bias[0][rows_h]).astype(BF)
                k = parts[g.lh + h].astype(BF)
                v = (parts[2 * g.lh + h] + bias[1][rows_h]).astype(BF)
                qkv[hh * 3 + 0, :, rows] = q
                qkv[hh * 3 + 1, :, rows] = k
                qkv[hh * 3 + 2, :, rows] = v
                scores = tn(k, q) * scale
                peak = jnp.max(scores, axis=0, keepdims=True)
                powers = jnp.exp(scores - peak)
                total = jnp.sum(powers, axis=0, keepdims=True)
                lse[hh : hh + 1, rows] = peak + jnp.log(total)
                probs = (powers * (1.0 / total)).astype(BF)
                mixed = nn(v, probs)
                gate = gat[s, pl.ds(row, 1), 2 * h : 2 * h + 1]
                gsend[i, core, rows_h, :] = (mixed * gate).astype(BF)
        for u in range(g.sub):
            j = i * g.sub + u

            @pl.when(j == p)
            def _():
                home().start()

            @pl.when(j != p)
            def _():
                away(j).start()

        return carry

    lax.fori_loop(0, g.Ic, item, 0)
    saves = [pltpu.make_async_copy(h1, h1_out, save.at[0]), pltpu.make_async_copy(qkv, qkv_out, save.at[1])]
    for copy in saves:
        copy.start()
    home().wait()
    for k in range(1, g.G):
        arrive(flip(p, k, g.bits)).wait_recv()
    heads = gbuf[...].reshape(g.T * g.hw, g.Ro)
    gath[...] = heads
    for k in range(g.G):
        forward(k).wait_recv()
    saves.append(pltpu.make_async_copy(wob, wof, save.at[2]))
    saves[-1].start()
    full = wob[...].reshape(g.T * g.hw, g.W)
    attention = tn(heads, full) + ob[...]
    own = c * g.Ic + p // g.sub
    base = tok[pl.ds(pl.multiple_of(p * g.Ro, g.Ro), g.Ro)].astype(F32)
    residual = base + mod[2, pl.ds(own, 1), :] * attention
    att[...] = attention
    res[...] = residual
    normed, _ = norm(residual)
    h2[...] = (normed * (1.0 + mod[4, pl.ds(own, 1), :]) + mod[3, pl.ds(own, 1), :]).astype(BF)
    for k in range(1, g.G):
        away(flip(p, k, g.bits)).wait_send()
        share(k).wait_send()
    for k in range(g.G):
        forward(k).wait_send()
    for copy in saves:
        copy.wait()


def feed_kernel(
    g, h2, cotangent, mod, gat, smc, we_in, wex_in, wr_in, wrx_in,
    grad_out, mpart_out, dwf_out, small, gates, ebs,
    cot, we, wex, wr, wrx, h2buf, bgbuf, gch, egb, sgb, own_g, xs, xr, mpart, dwf,
    joint, final, send_g, recv_g, leg_box, leg_sems, done, load, save, send_h, recv_h, send_p, recv_p,
):
    d, t, p, c = g.place()
    partner = (d, p * 2 + 1 - c)
    wec = (we, wex)
    wrc = (wr, wrx)

    def chip(k):
        return (d, flip(p, k, g.bits) * 2 + c)

    cot_rows = cotangent.at[pl.ds(pl.multiple_of(c * g.Rc, g.Rc), g.Rc)]
    loads = [
        pltpu.make_async_copy(src, dst, load.at[index])
        for index, (src, dst) in enumerate(
            ((cot_rows, cot), (wr_in, wr), (wrx_in, wrx), (we_in, we), (wex_in, wex))
        )
    ]
    for copy in loads:
        copy.start()
    leg = FirstLeg(g, g.fe, dwf, leg_box, leg_sems)
    meet([chip(k) for k in range(1, g.G)] + [partner, leg.other])

    spread = PlaneGather(g, h2, lambda k, source: h2buf.at[k], send_h, recv_h, chip, p)
    spread.start()
    back = PlaneScatter(g, lambda k: sgb.at[k - 1], joint, final, send_g, recv_g, chip)
    h2buf[0] = h2[...]
    for copy in loads:
        copy.wait()
    lane = lax.broadcasted_iota(jnp.int32, (1, g.ch), 1)
    tile_row = lax.broadcasted_iota(jnp.int32, (8, 128), 0)
    tile_lane = lax.broadcasted_iota(jnp.int32, (8, 128), 1)
    ebs[...] = jnp.zeros_like(ebs)
    gates[...] = jnp.zeros_like(gates)

    def block(k, carry):
        j = flip(p, k, g.bits)
        local = j // g.sub
        item = c * g.Ic + local
        rows = pl.ds(pl.multiple_of(j * g.Ro, g.Ro), g.Ro)
        here = pl.ds(pl.multiple_of(k * g.Ro, g.Ro), g.Ro)
        branch = (mod[5, pl.ds(item, 1), :] * cot[rows].astype(F32)).astype(BF)
        bgbuf[here] = branch
        grads = [nt(branch, wrc[s][...]) for s in range(2)]

        @pl.when(k == 1)
        def _():
            spread.relay()

        for kk in range(1, g.G):

            @pl.when(k == kk)
            def _():
                spread.wait(kk)

        hidden = h2buf[k]
        total = None
        for s in range(2):
            wide = nt(hidden, wec[s][...]) + smc[s, 0:1, : g.ch]
            inner = GELU_A * (wide + GELU_B * wide * wide * wide)
            tanh = jnp.tanh(inner)
            act = 0.5 * wide * (1.0 + tanh)
            slope = 0.5 * (1.0 + tanh) + 0.5 * wide * (1.0 - tanh * tanh) * (
                GELU_A * (1.0 + 3.0 * GELU_B * wide * wide)
            )
            gate = gat[s, pl.ds(item, 1), 1:2]
            for h in range(1, g.lh):
                gate = jnp.where(lane >= h * g.gc, gat[s, pl.ds(item, 1), 2 * h + 1 : 2 * h + 2], gate)
            gch[s, here] = (act * gate).astype(BF)
            line = jnp.sum(grads[s] * act, axis=0, keepdims=True)
            tile = gates[s]
            for h in range(g.lh):
                inside = jnp.where((lane >= h * g.gc) & (lane < (h + 1) * g.gc), line, 0.0)
                value = jnp.sum(inside, axis=1, keepdims=True)
                tile = tile + jnp.where((tile_row == local) & (tile_lane == 2 * h + 1), value, 0.0)
            gates[s] = tile
            egrad = (grads[s] * gate * slope).astype(BF)
            egb[s, here] = egrad
            ebs[s, 0:1, : g.ch] += jnp.sum(egrad.astype(F32), axis=0, keepdims=True)
            part = nn(egrad, wec[s][...])
            total = part if total is None else total + part

        @pl.when(k > 0)
        def _():
            sgb[k - 1] = total.astype(BF)
            back.put(k)

        @pl.when(k == 0)
        def _():
            own_g[...] = total

        return carry

    lax.fori_loop(0, g.G, block, 0)
    def swap(index):
        return remote(xs.at[index], xr.at[index], send_p.at[index], recv_p.at[index], partner)

    half_units = g.units // 2
    saves = []
    for index, left in enumerate((gch, egb)):
        right = bgbuf[...] if index == 0 else h2buf[...].reshape(g.Rc, g.W)
        xs[index] = tn(left[1], right).astype(BF)
        swap(index).start()
        value = tn(left[0], right)
        swap(index).wait_recv()
        value = (value + xr[index].astype(F32)).astype(BF)
        for u in range(half_units):
            dwf[index * half_units + u] = value[u * g.fr : (u + 1) * g.fr]
        if index == 0:
            leg.start()
            back.join()
    copy = pltpu.make_async_copy(dwf.at[pl.ds(g.fe, g.units - g.fe)], dwf_out.at[pl.ds(g.fe, g.units - g.fe)], save.at[0])
    copy.start()
    saves.append(copy)
    for k in range(g.G):
        rows = pl.ds(k * g.Ro, g.Ro)
        mpart[k] = (nn(gch[0, rows], wr[...]) + nn(gch[1, rows], wrx[...])).astype(BF)
    saves.append(pltpu.make_async_copy(mpart, mpart_out, save.at[2]))
    saves[-1].start()
    small[...] = jnp.zeros_like(small)
    small[7:8, :] = jnp.sum(bgbuf[0 : g.Ro].astype(F32), axis=0, keepdims=True)
    grad_out[...] = back.total(own_g[...])
    leg.add()
    copy = pltpu.make_async_copy(dwf.at[pl.ds(0, g.fe)], dwf_out.at[pl.ds(0, g.fe)], save.at[1])
    copy.start()
    saves.append(copy)
    leg.sent()

    @pl.when(leg.middle == 1)
    def _():
        pl.semaphore_signal(done, inc=1, device_id=leg.other, device_id_type=MESH)

    @pl.when(leg.middle == 0)
    def _():
        pl.semaphore_wait(done, 1)

    spread.sent()
    back.sent()
    swap(0).wait_send()
    swap(1).wait_send()
    for copy in saves:
        copy.wait()


def unattend_kernel(
    g, hgrad, h1_in, qkv_in, lse, gat, wi_in, wix_in, small_in, mpart_in, dwf, mod, att, res, wof_in, gath_in,
    cotangent, rbias, ebs, gates_in,
    grad, rgrad, bout, dwz, dwf_out, lines, sums, pay, gates,
    h1, qkv, wi, wix, mpart, wof, gath,
    hgs, hgbuf, wof_x, orr, osum, small, dqkv, acc, own_g, sgb, xs, xr, orv, sx, cot,
    work, first_z, second_z, more_z, sems_z, leg_box, leg_sems, joint_g, final_g, send_g, recv_g, joint_m, final_m, send_m, recv_m,
    send_o, recv_o, send_s, recv_s, send_p, recv_p, send_a, recv_a, send_x, recv_x,
    load,
):
    d, t, p, c = g.place()
    partner = (d, p * 2 + 1 - c)
    weights = (wi, wix)
    block = c * g.G + p

    def chip(k):
        return (d, flip(p, k, g.bits) * 2 + c)

    def peer(k):
        return (d, flip(t, k, g.tbits))

    def group(k):
        return (flip(d, k, g.dbits), t)

    fetch = pltpu.make_async_copy(
        cotangent.at[pl.ds(pl.multiple_of(block * g.Ro, g.Ro), g.Ro)], cot, load.at[0]
    )
    fetch.start()
    half = pltpu.make_async_copy(dwf, work, load.at[1])
    half.start()
    loads = [
        pltpu.make_async_copy(src, dst, load.at[2 + index])
        for index, (src, dst) in enumerate(
            (
                (wof_in, wof), (mpart_in, mpart), (gath_in, gath), (h1_in, h1), (qkv_in, qkv), (wi_in, wi),
                (wix_in, wix),
            )
        )
    ]
    for copy in loads:
        copy.start()
    zsum = GroupSum(g, g.units, work, first_z, second_z, more_z, dwf_out, sems_z)
    meet_line(g, [peer(k) for k in range(1, g.T)], group, zsum.middle)

    def rest(k):
        return remote(osum.at[flip(p, k, g.bits)], orv.at[k - 1], send_o.at[k], recv_o.at[k], chip(k))

    on = PlaneScatter(g, lambda k: mpart.at[k], joint_m, final_m, send_m, recv_m, chip)
    back = PlaneScatter(g, lambda k: sgb.at[k - 1], joint_g, final_g, send_g, recv_g, chip)

    def sumup(k):
        return remote(small, sx.at[k], send_s.at[k], recv_s.at[k], peer(k))

    def heads_out(k):
        return remote(hgs.at[pl.ds(flip(p, k, g.bits) * 2, 2)], hgbuf.at[k], send_a.at[k], recv_a.at[k], chip(k))

    def cross(q):
        return remote(wof_x.at[2 * q + 1 - c], orr.at[q], send_x.at[q], recv_x.at[q], partner)

    half.wait()
    everything = list(range(g.units))
    zsum.resume(everything[: g.fe])
    zsum.start(everything[g.fe :])
    leg = FirstLeg(g, g.ze, dwz, leg_box, leg_sems)
    fetch.wait()
    value = hgrad[...]
    own = c * g.Ic + p // g.sub
    normed, inverse = norm(res[...])
    cot_own = cot[...].astype(F32)
    residual = cot_own + norm_back(value * (1.0 + mod[4, pl.ds(own, 1), :]), normed, inverse)
    branch_one = (mod[2, pl.ds(own, 1), :] * residual).astype(BF)
    loads[0].wait()
    hgs[...] = nt(wof[...], branch_one).astype(BF).reshape(g.T, g.hw, g.Ro)
    for k in reversed(range(1, g.G)):
        heads_out(k).start()
    hgbuf[0] = hgs[pl.ds(p * 2, 2)]
    loads[1].wait()
    for k in reversed(range(1, g.G)):
        on.put(k)
    rgrad[...] = residual
    small[...] = small_in[...]
    small[2:3, :] = jnp.sum(residual * att[...], axis=0, keepdims=True)
    small[3:4, :] = jnp.sum(value, axis=0, keepdims=True)
    small[4:5, :] = jnp.sum(value * normed, axis=0, keepdims=True)
    small[6:7, :] = jnp.sum(branch_one.astype(F32), axis=0, keepdims=True)
    for k in range(1, g.T):
        sumup(k).start()
    for copy in loads[2:]:
        copy.wait()
    wof_x[...] = nn(gath[...], branch_one).astype(BF).reshape(g.T, g.hw, g.W)
    for q in range(g.G):
        cross(q).start()
    scale = 1.0 / math.sqrt(g.hd)
    acc[...] = jnp.zeros_like(acc)
    ones = jnp.ones((8, g.L), BF)
    tile_row = lax.broadcasted_iota(jnp.int32, (8, 128), 0)
    tile_lane = lax.broadcasted_iota(jnp.int32, (8, 128), 1)
    gates[...] = gates_in[...]
    pay[...] = ebs[...]

    def item(ii, carry):
        kk = lax.rem(g.Ic - ii, g.Ic)
        i = flip(p // g.sub, kk, g.bits)
        row = c * g.Ic + i
        rows = pl.ds(pl.multiple_of(i * g.L, g.L), g.L)
        slots = [kk * g.sub + (flip(lax.rem(p, g.sub), u, 4) if g.sub > 1 else 0) for u in range(g.sub)]
        hidden = h1[rows]
        total = None
        for u, slot in enumerate(slots):

            @pl.when(slot != 0)
            def _():
                heads_out(slot).wait_recv()

        @pl.when(ii == min(2, g.Ic - 1))
        def _():
            zsum.settle([1])
            zsum.join([3])

        @pl.when(ii == 1)
        def _():
            zsum.settle([0])
            zsum.join([2])
            for q in range(g.G):
                cross(q).wait()
                osum[q] = (wof_x[2 * q + c].astype(F32) + orr[q].astype(F32)).astype(BF)
            for k in range(1, g.G):
                rest(k).start()

        @pl.when(ii == g.Ic - 1)
        def _():
            on.join()

        for s in range(2):
            core = c + s - 2 * c * s
            tile = gates[s]
            for h in range(g.lh):
                hh = s * g.lh + h
                q = qkv[hh * 3 + 0, :, rows]
                k = qkv[hh * 3 + 1, :, rows]
                v = qkv[hh * 3 + 2, :, rows]
                pieces = [hgbuf[slot, core, h * g.hd : (h + 1) * g.hd, :] for slot in slots]
                heads = (pieces[0] if g.sub == 1 else jnp.concatenate(pieces, axis=1)).astype(F32)
                probs = jnp.exp(tn(k, q) * scale - lse[hh : hh + 1, rows])
                low = probs.astype(BF)
                mixed = nn(v, low)
                value = jnp.sum(jnp.sum(heads * mixed, axis=0, keepdims=True), axis=1, keepdims=True)
                tile = tile + jnp.where((tile_row == i) & (tile_lane == 2 * h), value, 0.0)
                mixed_grad = (gat[s, pl.ds(row, 1), 2 * h : 2 * h + 1] * heads).astype(BF)
                probs_grad = tn(v, mixed_grad)
                values_grad = nt(mixed_grad, low)
                score = (
                    probs * (probs_grad - jnp.sum(probs_grad * probs, axis=0, keepdims=True))
                ).astype(BF)
                queries_grad = nn(k, score) * scale
                keys_grad = nt(q, score) * scale
                for r, value in enumerate((queries_grad, keys_grad, values_grad)):
                    dqkv[s, r * g.hw + h * g.hd : r * g.hw + (h + 1) * g.hd, :] = value.astype(BF)
            gates[s] = tile
            wide = dqkv[s]
            part = tn(wide, weights[s][...])
            total = part if total is None else total + part
            acc[s] += nn(wide, hidden)
            pay[s, 1:2, : 3 * g.hw] += nt(ones, wide)[0:1]
        for u, slot in enumerate(slots):
            piece = total[u * g.Ro : (u + 1) * g.Ro]

            @pl.when(slot == 0)
            def _():
                own_g[...] = piece

            @pl.when(slot != 0)
            def _():
                sgb[slot - 1] = piece.astype(BF)
                back.put(slot)

        return carry

    lax.fori_loop(0, g.Ic, item, 0)
    xs[...] = acc[1].astype(BF)
    swap = remote(xs, xr, send_p, recv_p, partner)
    swap.start()
    zsum.settle([2])
    zsum.join([4])
    swap.wait()
    for u in range(g.units):
        low = u * g.zr
        if low < 3 * g.hw:
            span = slice(low, low + g.zr)
            dwz[u] = (acc[0, span] + xr[span].astype(F32)).astype(BF)
    leg.start()
    zsum.settle([3])
    zsum.join([5])
    zsum.settle([4])
    zsum.join([6])
    back.join()
    zsum.settle([5])
    zsum.join([7])
    value = small[...]
    for k in range(1, g.T):
        sumup(k).wait()
        value = value + sx[k]
    sums[...] = value
    out = osum[p].astype(F32)
    for k in range(1, g.G):
        rest(k).wait()
        out = out + orv[k - 1].astype(F32)
    for u in range(g.units):
        low = u * g.zr
        if low >= 3 * g.hw:
            dwz[u] = out[low - 3 * g.hw : low - 3 * g.hw + g.zr].astype(BF)
    zsum.settle([6])
    branch = on.total(mpart[0].astype(F32)) + rbias[...]
    bout[...] = (res[...] + mod[5, pl.ds(own, 1), :] * branch).astype(BF)
    lines[...] = small[...]
    lines[5:6, :] = jnp.sum(cot[...].astype(F32) * branch, axis=0, keepdims=True)
    grad[...] = back.total(own_g[...])
    on.sent()
    back.sent()
    zsum.settle([7])
    leg.add()
    zsum.end(everything, everything[g.fe :])
    leg.sent()
    for k in range(1, g.G):
        heads_out(k).wait_send()


def finish_kernel(
    g, grad, rgrad, tokens, mod, lines_in, sums, bout, pay, gates, dsg, dwz,
    tall, ball, colall, zall, logall, dwz_out,
    tok, tsend, stage, cbuf, zbuf, lbuf, pbuf, gbuf, work, first_z, second_z, more_z, sems_z,
    load, send_t, recv_t, send_f, recv_f, send_c, recv_c, send_p, recv_p, send_s, recv_s, keep,
):
    d, t, p, c = g.place()
    partner = (d, p * 2 + 1 - c)

    def chip(k):
        return (d, flip(p, k, g.bits) * 2 + c)

    def peer(k):
        return (d, flip(t, k, g.tbits))

    def group(k):
        return (flip(d, k, g.dbits), t)

    meet([peer(k) for k in range(1, g.T)] + [group(k) for k in range(1, g.D)])
    block = c * g.G + p
    mine = pl.ds(pl.multiple_of(block * g.Ro, g.Ro), g.Ro)
    copy = pltpu.make_async_copy(tokens.at[mine], tok, load)
    copy.start()
    swaps = [
        remote(pay.at[1], pbuf, send_p.at[0], recv_p.at[0], partner),
        remote(gates.at[1], gbuf, send_p.at[1], recv_p.at[1], partner),
    ]
    for swap in swaps:
        swap.start()
    zsum = GroupSum(g, g.units, work, first_z, second_z, more_z, dwz_out, sems_z)
    everything = list(range(g.units))
    work[...] = dwz[...]
    zsum.resume(everything[: g.ze])
    zsum.start(everything[g.ze :])

    def rows_of(dst):
        return lambda k, source: dst.at[pl.ds(pl.multiple_of((c * g.G + source) * g.Ro, g.Ro), g.Ro)]

    outs = PlaneGather(g, bout, rows_of(ball), send_t.at[0], recv_t.at[0], chip, p)
    grads = PlaneGather(g, tsend, rows_of(tall), send_t.at[1], recv_t.at[1], chip, p)
    outs.start()
    copy.wait()
    own = c * g.Ic + p // g.sub
    normed, inverse = norm(tok[...].astype(F32))
    value = grad[...]
    scaled = value * (1.0 + mod[1, pl.ds(own, 1), :])
    tsend[...] = (rgrad[...] + norm_back(scaled, normed, inverse)).astype(BF)
    lines = lines_in[...]
    kind = lax.broadcasted_iota(jnp.int32, lines.shape, 0)
    first = jnp.sum(value, axis=0, keepdims=True)
    second = jnp.sum(value * normed, axis=0, keepdims=True)
    lines = jnp.where(kind == 0, first, jnp.where(kind == 1, second, lines))
    w = g.mw
    stage[...] = jnp.zeros_like(stage)
    for member in range(g.T):
        stage[member, :, :w] = lines[:, member * w : (member + 1) * w]

    def columns(k):
        return remote(stage.at[flip(t, k, g.tbits)], cbuf.at[d, t], send_c.at[k], recv_c.at[k], peer(k))

    def column_in(k):
        return remote(stage.at[t], cbuf.at[d, flip(t, k, g.tbits)], send_c.at[k], recv_c.at[k], peer(k))

    for k in range(1, g.T):
        columns(k).start()
    cbuf[d, t] = stage[t]
    grads.start()
    local = [
        pltpu.make_async_copy(bout, ball.at[mine], keep.at[0]),
        pltpu.make_async_copy(tsend, tall.at[mine], keep.at[1]),
    ]
    for item in local:
        item.start()

    def forward(which, dst, k):
        rows = pl.ds(pl.multiple_of((c * g.G + flip(p, k, g.bits)) * g.Ro, g.Ro), g.Ro)
        return remote(dst.at[rows], dst.at[rows], send_f.at[which, k], recv_f.at[which, k], partner)

    def arrive_forward(which, dst, k):
        rows = pl.ds(pl.multiple_of(((1 - c) * g.G + flip(p, k, g.bits)) * g.Ro, g.Ro), g.Ro)
        return remote(dst.at[rows], dst.at[rows], send_f.at[which, k], recv_f.at[which, k], partner)

    outs.relay()
    zsum.join([4])
    zsum.settle([0, 1])
    for swap in swaps:
        swap.wait()
    zbuf[d] = jnp.zeros((8, g.W), F32)
    zbuf[d, 0:2] = pay[0, 0:2] + pbuf[0:2]
    zbuf[d, 2:4] = sums[6:8]
    both = jnp.concatenate([gates[0, : g.Ic], gbuf[: g.Ic]], axis=0)
    turned = jnp.concatenate([gbuf[: g.Ic], gates[0, : g.Ic]], axis=0)
    lbuf[d] = jnp.where(c == 0, both, turned) * dsg[...]
    zsum.join([5, 6])
    zsum.settle([2])
    for k in range(1, g.T):
        columns(k).wait_send()
        column_in(k).wait_recv()

    def share(k):
        return [
            remote(cbuf.at[d], cbuf.at[d], send_s.at[0, k], recv_s.at[0, k], group(k)),
            remote(zbuf.at[d], zbuf.at[d], send_s.at[1, k], recv_s.at[1, k], group(k)),
            remote(lbuf.at[d], lbuf.at[d], send_s.at[2, k], recv_s.at[2, k], group(k)),
        ]

    def shared(k):
        other = flip(d, k, g.dbits)
        return [
            remote(cbuf.at[other], cbuf.at[other], send_s.at[0, k], recv_s.at[0, k], group(k)),
            remote(zbuf.at[other], zbuf.at[other], send_s.at[1, k], recv_s.at[1, k], group(k)),
            remote(lbuf.at[other], lbuf.at[other], send_s.at[2, k], recv_s.at[2, k], group(k)),
        ]

    for k in range(1, g.D):
        for item in share(k):
            item.start()
    for which, dst in ((0, ball), (1, tall)):
        local[which].wait()
        forward(which, dst, 0).start()
    zsum.join([7])
    zsum.settle([3, 4])
    grads.relay()
    zsum.settle([5, 6, 7])
    for k in range(1, g.G):
        outs.wait(k)
        forward(0, ball, k).start()
    for k in range(1, g.D):
        for item in share(k):
            item.wait_send()
        for item in shared(k):
            item.wait_recv()
    colall[...] = cbuf[...]
    zall[...] = zbuf[...]
    logall[...] = lbuf[...]
    for k in range(1, g.G):
        grads.wait(k)
        forward(1, tall, k).start()
    zsum.end(everything, everything[g.ze :])
    outs.sent()
    grads.sent()
    for which, dst in ((0, ball), (1, tall)):
        for k in range(g.G):
            forward(which, dst, k).wait_send()
            arrive_forward(which, dst, k).wait_recv()


def wrap_kernel(g, colall, zall, logall, conds, dwm, dmb, drw, drb, dib, vectors):
    rows = []
    for member in range(g.T):
        rows.append(((member % 2) * g.G + member // 2) * g.Ro // g.L)
    value = conds[...]
    silu = value / (1.0 + jnp.exp(-value))
    picked = jnp.concatenate([silu[z, i : i + 1] for z in range(g.D) for i in rows], axis=0).astype(BF)
    twice = jnp.concatenate([picked, picked], axis=0)
    w = g.mw
    for row in range(6):
        part = jnp.concatenate(
            [colall[z, member, row : row + 1, :] for z in range(g.D) for member in range(g.T)], axis=0
        )
        dmb[row : row + 1, :] = jnp.sum(part, axis=0, keepdims=True)[:, :w]
        high = part.astype(BF)
        low = (part - high.astype(F32)).astype(BF)
        dwm[row * w : (row + 1) * w, :] = tn(jnp.concatenate([high, low], axis=0), twice)[:w]
    logits = jnp.concatenate([logall[z] for z in range(g.D)], axis=0)
    high = logits.astype(BF)
    low = (logits - high.astype(F32)).astype(BF)
    flat = jnp.concatenate([value[z] for z in range(g.D)], axis=0).astype(BF)
    router = tn(jnp.concatenate([high, low], axis=0), jnp.concatenate([flat, flat], axis=0))
    sums = jnp.sum(logits, axis=0, keepdims=True)
    for h in range(g.lh):
        drw[h] = router[2 * h : 2 * h + 2, :]
        drb[h : h + 1, :] = sums[:, 2 * h : 2 * h + 2]
    total = zall[0]
    for z in range(1, g.D):
        total = total + zall[z]
    dib[0:1, :] = total[1:2, : g.hw]
    dib[1:2, :] = total[1:2, 2 * g.hw : 3 * g.hw]
    vectors[...] = total


def body(
    groups, members,
    tokens, condition, timesteps, route_masks, modulate_weight, modulate_bias, input_weight, input_bias,
    output_weight, output_bias, expand_weight, expand_bias, reduce_weight, reduce_bias, router_weight, router_bias,
    out_cotangent,
):
    g = Plan(
        groups, members, tokens.shape[0], condition.shape[0], tokens.shape[1], router_weight.shape[1],
        modulate_weight.shape[2], input_weight.shape[2], expand_weight.shape[1],
    )
    dma = pltpu.SemaphoreType.DMA
    V = pltpu.VMEM
    W, T, G, D, I = g.W, g.T, g.G, g.D, g.I
    wide = 2 * g.lh
    wm = jnp.transpose(modulate_weight, (1, 2, 0)).reshape(6 * g.mw, W)
    wi = jnp.transpose(input_weight, (1, 2, 0)).reshape(3 * g.hw, W)
    we = expand_weight.T
    wr = reduce_weight
    rw = jnp.transpose(router_weight, (1, 2, 0))
    masks = jnp.transpose(route_masks, (1, 2, 0))
    eb = expand_bias.astype(F32)[None]
    ob = output_bias.astype(F32)[None]
    rbias = reduce_bias.astype(F32)[None]

    mod, gat, dsg, smc, conds, wix, wex, wrx = call(
        functools.partial(start_kernel, g), "start",
        (condition, wm, modulate_bias, timesteps, masks, rw, router_bias, eb, input_bias, wi, we, wr),
        "vvvsvvvvvhhh",
        [
            ((6, I, W), F32), ((2, I, 128), F32), ((I, 128), F32), ((2, 8, W), F32), ((D, I, W), F32),
            ((3 * g.hw, W), BF), ((g.ch, W), BF), ((g.ch, W), BF),
        ],
        "vvvvvhhh",
        [
            V((T, I, 6 * g.mw), F32), V((2, I, 128), F32), V((2, 8, W), F32), V((D, I, W), F32),
            dma((T,)), dma((T,)), dma((5,)), dma((5,)), dma((D,)), dma((D,)),
        ],
        1,
    )
    h1, qkv, lse, att, res, h2, gath, wof = call(
        functools.partial(attend_kernel, g), "attend",
        (tokens, mod, gat, smc, wi, wix, output_weight, ob), "hvvvvvvv",
        [
            ((g.Rc, W), BF), ((wide * 3, g.hd, g.Rc), BF), ((wide, g.Rc), F32),
            ((g.Ro, W), F32), ((g.Ro, W), F32), ((g.Ro, W), BF), ((T * g.hw, g.Ro), BF), ((T, g.hw, W), BF),
        ],
        "hhvvvvvh",
        [
            V((g.Rc, W), BF), V((g.Rc, W), BF), V((wide * 3, g.hd, g.Rc), BF), V((g.Ic, 2, g.hw, g.L), BF), V((T, g.hw, g.Ro), BF), V((T, g.hw, W), BF),
            dma, dma, dma((3,)), dma((G,)), dma((G,)), dma((G,)), dma((G,)), dma((G,)), dma((G,)),
        ],
        2,
    )
    hgrad, mpart, dwf, small, gates, ebs = call(
        functools.partial(feed_kernel, g), "feed",
        (h2, out_cotangent, mod, gat, smc, we, wex, wr, wrx), "vhvvvhhhh",
        [
            ((g.Ro, W), F32), ((G, g.Ro, W), BF), ((g.units, g.fr, W), BF),
            ((8, W), F32), ((2, 8, 128), F32), ((2, 8, W), F32),
        ],
        "vhhvvv",
        [
            V((g.Rc, W), BF), V((g.ch, W), BF), V((g.ch, W), BF), V((g.ch, W), BF), V((g.ch, W), BF),
            V((G, g.Ro, W), BF), V((g.Rc, W), BF), V((2, g.Rc, g.ch), BF), V((2, g.Rc, g.ch), BF),
            V((G - 1, g.Ro, W), BF), V((g.Ro, W), F32),
            V((2, g.ch, W), BF), V((2, g.ch, W), BF), V((G, g.Ro, W), BF), V((g.units, g.fr, W), BF),
        ]
        + PlaneScatter.scratch(g)
        + FirstLeg.scratch(g, g.fe, g.fr)
        + [pltpu.SemaphoreType.REGULAR, dma((5,)), dma((3,)), dma((G, 2)), dma((G, 2)), dma((2,)), dma((2,))],
        3,
    )
    grad, rgrad, bout, dwz, dwf, lines, sums, pay, gates = call(
        functools.partial(unattend_kernel, g), "unattend",
        (
            hgrad, h1, qkv, lse, gat, wi, wix, small, mpart, dwf, mod, att, res,
            wof.reshape(T * g.hw, W), gath, out_cotangent, rbias, ebs, gates,
        ),
        "vhhvvhhvhhvvvhhhvvv",
        [
            ((g.Ro, W), F32), ((g.Ro, W), F32), ((g.Ro, W), BF), ((g.units, g.zr, W), BF),
            ((g.units, g.fr, W), BF), ((8, W), F32), ((8, W), F32), ((2, 8, W), F32), ((2, 8, 128), F32),
        ],
        "vvvvvvvvv",
        [
            V((g.Rc, W), BF), V((wide * 3, g.hd, g.Rc), BF), V((3 * g.hw, W), BF), V((3 * g.hw, W), BF),
            V((G, g.Ro, W), BF), V((T * g.hw, W), BF), V((T * g.hw, g.Ro), BF),
            V((T, g.hw, g.Ro), BF), V((G, 2, g.hw, g.Ro), BF), V((T, g.hw, W), BF), V((G, g.hw, W), BF),
            V((G, g.hw, W), BF), V((8, W), F32),
            V((2, 3 * g.hw, g.L), BF), V((2, 3 * g.hw, W), F32), V((g.Ro, W), F32), V((G - 1, g.Ro, W), BF),
            V((3 * g.hw, W), BF), V((3 * g.hw, W), BF),
            V((G - 1, g.hw, W), BF), V((T, 8, W), F32), V((g.Ro, W), BF),
        ]
        + GroupSum.scratch(g, g.units, g.fr)
        + FirstLeg.scratch(g, g.ze, g.zr)
        + PlaneScatter.scratch(g)
        + PlaneScatter.scratch(g)
        + [
            dma((G,)), dma((G,)), dma((T,)), dma((T,)), dma, dma,
            dma((G,)), dma((G,)), dma((G,)), dma((G,)), dma((9,)),
        ],
        4,
    )
    tall, ball, colall, zall, logall, dwz = call(
        functools.partial(finish_kernel, g), "finish",
        (grad, rgrad, tokens, mod, lines, sums, bout, pay, gates, dsg, dwz), "vvhvvvvvvvv",
        [
            ((g.R, W), BF), ((g.R, W), BF), ((D, T, 8, g.cw), F32), ((D, 8, W), F32), ((D, I, 128), F32),
            ((g.units, g.zr, W), BF),
        ],
        "hhvvvv",
        [
            V((g.Ro, W), BF), V((g.Ro, W), BF), V((T, 8, g.cw), F32), V((D, T, 8, g.cw), F32), V((D, 8, W), F32),
            V((D, I, 128), F32), V((8, W), F32), V((8, 128), F32),
        ]
        + GroupSum.scratch(g, g.units, g.zr)
        + [
            dma, dma((2, G, 2)), dma((2, G, 2)), dma((2, G)), dma((2, G)), dma((T,)), dma((T,)), dma((2,)), dma((2,)),
            dma((3, D)), dma((3, D)), dma((2,)),
        ],
        5,
    )
    dwm, dmb, drw, drb, dib, vectors = call(
        functools.partial(wrap_kernel, g), "wrap", (colall, zall, logall, conds), "vvvv",
        [
            ((6 * g.mw, W), F32), ((6, g.mw), F32), ((g.lh, 2, W), F32), ((g.lh, 2), F32), ((2, g.hw), F32),
            ((8, W), F32),
        ],
        "vvvvvv", [], None,
    )
    dwf = dwf.astype(F32).reshape(2, g.ch, W)
    dwz = dwz.astype(F32).reshape(4 * g.hw, W)
    return (
        ball.astype(F32),
        tall.astype(F32),
        jnp.transpose(dwm.reshape(6, g.mw, W), (2, 0, 1)),
        dmb,
        jnp.transpose(dwz[: 3 * g.hw].reshape(3, g.hw, W), (2, 0, 1)),
        dib,
        dwz[3 * g.hw :],
        vectors[2],
        dwf[1].T,
        vectors[0, : g.ch],
        dwf[0],
        vectors[3],
        jnp.transpose(drw, (2, 0, 1)),
        drb,
    )


def solution(mesh):
    return jax.shard_map(
        functools.partial(body, mesh.shape["dp"], mesh.shape["tensor"]),
        mesh=mesh,
        in_specs=(
            P("dp", None), P("dp", None), P("dp"), P(None, "tensor", None), P(None, None, "tensor"),
            P(None, "tensor"), P(None, None, "tensor"), P(None, "tensor"), P("tensor", None), P(),
            P(None, "tensor"), P("tensor"), P("tensor", None), P(), P(None, "tensor", None), P("tensor", None),
            P("dp", None),
        ),
        out_specs=(
            P("dp", None), P("dp", None), P(None, None, "tensor"), P(None, "tensor"), P(None, None, "tensor"),
            P(None, "tensor"), P("tensor", None), P(), P(None, "tensor"), P("tensor"), P("tensor", None), P(),
            P(None, "tensor", None), P("tensor", None),
        ),
        check_vma=False,
    )
```

```python
import functools
import math

import jax
import jax.numpy as jnp
from jax import lax
from jax.experimental import pallas as pl
from jax.experimental.pallas import tpu as pltpu
from jax.sharding import PartitionSpec as P

BF = jnp.bfloat16
F32 = jnp.float32
MESH = pl.DeviceIdType.MESH
EPSILON = 1e-06
GELU_A = math.sqrt(2.0 / math.pi)
GELU_B = 0.044715
VMEM_LIMIT = 58 << 20


def nt(left, right):
    return lax.dot_general(left, right, (((1,), (1,)), ((), ())), preferred_element_type=F32)


def nn(left, right):
    return lax.dot_general(left, right, (((1,), (0,)), ((), ())), preferred_element_type=F32)


def tn(left, right):
    return lax.dot_general(left, right, (((0,), (0,)), ((), ())), preferred_element_type=F32)


def flip(value, mask, bits):
    total = 0
    for bit in range(bits):
        unit = 1 << bit
        total = total + lax.rem(value // unit + mask // unit, 2) * unit
    return total


def norm(values):
    center = values - jnp.mean(values, axis=-1, keepdims=True)
    inverse = lax.rsqrt(jnp.mean(center * center, axis=-1, keepdims=True) + EPSILON)
    return center * inverse, inverse


def norm_back(grad, normed, inverse):
    mean_grad = jnp.mean(grad, axis=-1, keepdims=True)
    mean_cross = jnp.mean(grad * normed, axis=-1, keepdims=True)
    return inverse * (grad - mean_grad - normed * mean_cross)


class Plan:
    def __init__(self, groups, members, rows, items, width, heads, modwidth, headwidth, channels):
        self.D = groups
        self.T = members
        self.G = members // 2
        self.bits = self.G.bit_length() - 1
        self.tbits = members.bit_length() - 1
        self.dbits = groups.bit_length() - 1
        self.R = rows
        self.I = items
        self.L = rows // items
        self.W = width
        self.Rc = rows // 2
        self.Ro = rows // members
        self.Ic = items // 2
        self.sub = self.L // self.Ro
        self.lh = heads
        self.mw = modwidth
        self.cw = -(-modwidth // 128) * 128
        self.hw = headwidth
        self.hd = headwidth // heads
        self.ch = channels
        self.gc = channels // heads
        self.hr = 2 * headwidth
        self.units = 8
        self.fr = 2 * channels // self.units
        self.zr = 4 * headwidth // self.units
        self.fe = 2
        self.ze = 4

    def place(self):
        d = lax.axis_index("dp")
        t = lax.axis_index("tensor")
        return d, t, t // 2, lax.rem(t, 2)


def greet(devices):
    barrier = pltpu.get_barrier_semaphore()
    for device in devices:
        pl.semaphore_signal(barrier, inc=1, device_id=device, device_id_type=MESH)
    return barrier


def meet(devices):
    pl.semaphore_wait(greet(devices), len(devices))


def meet_line(g, devices, group, middle):
    barrier = pltpu.get_barrier_semaphore()
    for device in devices + [group(1)]:
        pl.semaphore_signal(barrier, inc=1, device_id=device, device_id_type=MESH)
    others = [group(3)] + [group(4 << level) for level in range(g.dbits - 2)]

    @pl.when(middle == 1)
    def _():
        for device in others:
            pl.semaphore_signal(barrier, inc=1, device_id=device, device_id_type=MESH)
        pl.semaphore_wait(barrier, len(devices) + 1 + len(others))

    @pl.when(middle == 0)
    def _():
        pl.semaphore_wait(barrier, len(devices) + 1)


def remote(src, dst, send, recv, device):
    return pltpu.make_async_remote_copy(
        src_ref=src, dst_ref=dst, send_sem=send, recv_sem=recv, device_id=device, device_id_type=MESH
    )


class GroupSum:
    def __init__(self, g, count, work, first, second, more, full, sems):
        self.g, self.count, self.work, self.first, self.second = g, count, work, first, second
        self.more, self.full, self.sems = more, full, sems
        self.d, self.t = lax.axis_index("dp"), lax.axis_index("tensor")
        self.middle = lax.rem(lax.rem(self.d, 4) + 1, 4) // 2

    def device(self, mask):
        return (flip(self.d, mask, self.g.dbits), self.t)

    def copy(self, kind, src, dst, unit, mask):
        return remote(src.at[unit], dst.at[unit], self.sems.at[kind, unit], self.sems.at[kind + 1, unit], self.device(mask))

    def up(self, unit):
        return self.copy(0, self.work, self.first, unit, 1)

    def over(self, unit):
        return self.copy(2, self.work, self.second, unit, 3)

    def down(self, unit):
        return self.copy(4, self.full, self.full, unit, 1)

    def across(self, unit, level):
        src = self.more.at[2 * level, unit]
        dst = self.more.at[2 * level + 1, unit]
        kind = 6 + 2 * level
        return remote(src, dst, self.sems.at[kind, unit], self.sems.at[kind + 1, unit], self.device(4 << level))

    def start(self, units):
        @pl.when(self.middle == 0)
        def _():
            for unit in units:
                self.up(unit).start()

    def resume(self, units):
        @pl.when(self.middle == 1)
        def _():
            for unit in units:
                self.over(unit).start()

    def join(self, units):
        @pl.when(self.middle == 1)
        def _():
            for unit in units:
                self.up(unit).wait_recv()
                self.work[unit] = (self.work[unit].astype(F32) + self.first[unit].astype(F32)).astype(BF)
                self.over(unit).start()

    def settle(self, units):
        @pl.when(self.middle == 1)
        def _():
            for unit in units:
                self.over(unit).wait_recv()
                value = (self.work[unit].astype(F32) + self.second[unit].astype(F32)).astype(BF)
                for level in range(self.g.dbits - 2):
                    self.more[2 * level, unit] = value
                    copy = self.across(unit, level)
                    copy.start()
                    copy.wait()
                    value = (value.astype(F32) + self.more[2 * level + 1, unit].astype(F32)).astype(BF)
                self.full[unit] = value
                self.down(unit).start()

    def end(self, units, started):
        @pl.when(self.middle == 0)
        def _():
            for unit in started:
                self.up(unit).wait_send()
            for unit in units:
                self.down(unit).wait_recv()

        @pl.when(self.middle == 1)
        def _():
            for unit in units:
                self.over(unit).wait_send()
                self.down(unit).wait_send()

    @staticmethod
    def scratch(g, count, rows):
        levels = max(g.dbits - 2, 0)
        return [
            pltpu.VMEM((count, rows, g.W), BF), pltpu.VMEM((count, rows, g.W), BF), pltpu.VMEM((count, rows, g.W), BF),
            pltpu.VMEM((max(2 * levels, 1), count if levels else 1, rows if levels else 16, g.W), BF),
            pltpu.SemaphoreType.DMA((6 + 2 * levels, count)),
        ]


class FirstLeg:
    def __init__(self, g, units, work, inbox, sems):
        self.g, self.units, self.work, self.inbox, self.sems = g, units, work, inbox, sems
        d = lax.axis_index("dp")
        self.middle = lax.rem(lax.rem(d, 4) + 1, 4) // 2
        self.other = (flip(d, 1, g.dbits), lax.axis_index("tensor"))

    def copy(self, unit):
        return remote(self.work.at[unit], self.inbox.at[unit], self.sems.at[0, unit], self.sems.at[1, unit], self.other)

    def start(self):
        @pl.when(self.middle == 0)
        def _():
            for unit in range(self.units):
                self.copy(unit).start()

    def add(self):
        @pl.when(self.middle == 1)
        def _():
            for unit in range(self.units):
                self.copy(unit).wait_recv()
                self.work[unit] = (self.work[unit].astype(F32) + self.inbox[unit].astype(F32)).astype(BF)

    def sent(self):
        @pl.when(self.middle == 0)
        def _():
            for unit in range(self.units):
                self.copy(unit).wait_send()

    @staticmethod
    def scratch(g, units, rows):
        return [pltpu.VMEM((units, rows, g.W), BF), pltpu.SemaphoreType.DMA((2, units))]


def half(g, ref, which):
    return ref.at[pl.ds(which * (g.Ro // 2), g.Ro // 2)]


class PlaneGather:
    def __init__(self, g, src, place, send, recv, chip, p):
        self.g, self.src, self.place, self.send, self.recv, self.chip, self.p = g, src, place, send, recv, chip, p
        self.relayed = g.G == 4

    def source(self, k):
        return flip(self.p, k, self.g.bits)

    def own(self, k, h):
        g = self.g
        return remote(
            half(g, self.src, h), half(g, self.place(k, self.p), h), self.send.at[k, h], self.recv.at[k, h], self.chip(k)
        )

    def arrival(self, k, h):
        g = self.g
        place = half(g, self.place(k, self.source(k)), h)
        return remote(place, place, self.send.at[k, h], self.recv.at[k, h], self.chip(k))

    def onward(self, h):
        g = self.g
        k = 1 + h
        src = half(g, self.place(k, self.source(k)), h)
        dst = half(g, self.place(3, self.source(k)), h)
        return remote(src, dst, self.send.at[3, h], self.recv.at[3, h], self.chip(2 - h))

    def start(self):
        if self.relayed:
            for k, h in ((1, 0), (2, 1), (1, 1), (2, 0)):
                self.own(k, h).start()
        else:
            for k in range(1, self.g.G):
                for h in range(2):
                    self.own(k, h).start()

    def relay(self):
        if self.relayed:
            for h in range(2):
                self.arrival(1 + h, h).wait_recv()
                self.onward(h).start()

    def wait(self, k):
        for h in range(2):
            if not (self.relayed and k < 3 and h == k - 1):
                self.arrival(k, h).wait_recv()

    def sent(self):
        for h in range(2):
            for k in range(1, 3 if self.relayed else self.g.G):
                self.own(k, h).wait_send()
            if self.relayed:
                self.onward(h).wait_send()


class PlaneScatter:
    def __init__(self, g, part, joint, final, send, recv, chip):
        self.g, self.part, self.joint, self.final = g, part, joint, final
        self.send, self.recv, self.chip = send, recv, chip
        self.relayed = g.G == 4

    def far(self, h):
        return remote(
            half(self.g, self.part(3), h), self.joint.at[h], self.send.at[2, h], self.recv.at[2, h], self.chip(1 + h)
        )

    def near(self, k, h):
        g = self.g
        return remote(
            half(g, self.part(k), h), half(g, self.final.at[k - 1], h), self.send.at[k - 1, h], self.recv.at[k - 1, h],
            self.chip(k),
        )

    def put(self, k):
        if not self.relayed:
            for h in range(2):
                self.near(k, h).start()
        elif isinstance(k, int):
            if k == 3:
                self.far(0).start()
                self.far(1).start()
            else:
                self.near(k, k - 1).start()
        else:
            for kk in range(1, 4):

                @pl.when(k == kk)
                def _():
                    self.put(kk)

    def join(self):
        if self.relayed:
            for h in range(2):
                k = 2 - h
                self.far(h).wait_recv()
                rows = pl.ds(h * (self.g.Ro // 2), self.g.Ro // 2)
                ref = self.part(k)
                ref[rows] = (ref[rows].astype(F32) + self.joint[h].astype(F32)).astype(BF)
                self.near(k, h).start()

    def total(self, value):
        for k in range(1, 3 if self.relayed else self.g.G):
            for h in range(2):
                self.near(k, h).wait_recv()
            value = value + self.final[k - 1].astype(F32)
        return value

    def sent(self):
        for h in range(2):
            for k in range(1, 3 if self.relayed else self.g.G):
                self.near(k, h).wait_send()
            if self.relayed:
                self.far(h).wait_send()

    @staticmethod
    def scratch(g):
        dma = pltpu.SemaphoreType.DMA
        return [
            pltpu.VMEM((2, g.Ro // 2, g.W), BF), pltpu.VMEM((2 if g.G == 4 else g.G - 1, g.Ro, g.W), BF),
            dma((g.G, 2)), dma((g.G, 2)),
        ]


def call(kernel, name, inputs, in_spaces, outs, out_spaces, scratch, collective, cost=None):
    spec = {
        "v": pl.BlockSpec(memory_space=pltpu.VMEM),
        "h": pl.BlockSpec(memory_space=pl.ANY),
        "s": pl.BlockSpec(memory_space=pltpu.SMEM),
    }
    flops, moved = cost or (10**8, 10**7)
    return pl.pallas_call(
        kernel,
        name=name,
        out_shape=[jax.ShapeDtypeStruct(s, t) for s, t in outs],
        in_specs=[spec[x] for x in in_spaces],
        out_specs=[spec[x] for x in out_spaces],
        scratch_shapes=scratch,
        cost_estimate=pl.CostEstimate(flops=flops, bytes_accessed=moved, transcendentals=0),
        compiler_params=pltpu.CompilerParams(
            collective_id=collective, has_side_effects=collective is not None, vmem_limit_bytes=VMEM_LIMIT
        ),
    )(*inputs)


def start_kernel(
    g, cond, wm, mb, ts, masks, rw, rb, eb, ib, wi,
    mod, gat, dsg, smc, call_all, wix,
    mpart, gx, sx, cx, send_m, recv_m, send_w, recv_w, send_c, recv_c,
):
    d, t, p, c = g.place()
    partner = (d, p * 2 + 1 - c)
    devices = [(d, flip(t, k, g.tbits)) for k in range(1, g.T)]
    devices = devices + [(flip(d, k, g.dbits), t) for k in range(1, g.D)]
    barrier = greet(devices)
    value = cond[...]
    silu = (value / (1.0 + jnp.exp(-value))).astype(BF)
    part = nt(silu, wm[...])
    w = g.mw
    bias = mb[...].astype(F32)
    for row in range(6):
        mpart[t, :, row * w : (row + 1) * w] = part[:, row * w : (row + 1) * w] + bias[row : row + 1]

    pl.semaphore_wait(barrier, len(devices))
    pair = remote(wi, wix, send_w.at[2], recv_w.at[2], partner)

    def spread(k):
        return remote(
            mpart.at[t], mpart.at[t], send_m.at[k], recv_m.at[k], (d, flip(t, k, g.tbits))
        )

    for k in range(1, g.T):
        spread(k).start()
    pair.start()
    low = value.astype(BF)
    steps = masks.shape[2]
    row = lax.broadcasted_iota(jnp.int32, (g.I, steps), 0)
    wanted = jnp.zeros((g.I, steps), jnp.int32)
    for item in range(g.I):
        wanted = jnp.where(row == item, ts[item], wanted)
    hot = (wanted == lax.broadcasted_iota(jnp.int32, (g.I, steps), 1)).astype(F32).astype(BF)
    dsg[...] = jnp.zeros_like(dsg)
    gx[0] = jnp.zeros((g.I, 128), F32)
    scale = rb[...].astype(F32)
    for h in range(g.lh):
        logits = nt(low, rw[h]) + scale[h : h + 1]
        sigmoid = 1.0 / (1.0 + jnp.exp(-logits))
        mask = nt(hot, masks[h].astype(F32).astype(BF))
        dsg[:, 2 * h : 2 * h + 2] = mask * sigmoid * (1.0 - sigmoid)
        gx[0, :, 2 * h : 2 * h + 2] = mask * sigmoid
    sx[0] = jnp.zeros((8, g.W), F32)
    sx[0, 0:1, : g.ch] = eb[...]
    sx[0, 1:3, : g.hw] = ib[...].astype(F32)
    small = [
        remote(gx.at[0], gx.at[1], send_w.at[0], recv_w.at[0], partner),
        remote(sx.at[0], sx.at[1], send_w.at[1], recv_w.at[1], partner),
    ]
    for copy in small:
        copy.start()

    def conditions(k):
        return remote(cond, cx.at[d], send_c.at[k], recv_c.at[k], (flip(d, k, g.dbits), t))

    for k in range(1, g.D):
        conditions(k).start()
    cx[d] = value
    for k in range(1, g.T):
        spread(k).wait()
    for member in range(g.T):
        for row in range(6):
            mod[row, :, member * w : (member + 1) * w] = mpart[member, :, row * w : (row + 1) * w]
    for copy in small:
        copy.wait()
    gat[...] = gx[...]
    smc[...] = sx[...]
    pair.wait()
    for k in range(1, g.D):
        conditions(k).wait()
    call_all[...] = cx[...]


def split_heads(g, wide):
    return [wide[r * g.hw + h * g.hd : r * g.hw + (h + 1) * g.hd] for r in range(3) for h in range(g.lh)]


def attend_kernel(
    g, tokens, mod, gat, smc, wi, wix, wo, ob, we, wr,
    h1_out, qkv_out, lse, att, res, h2, gath, wof, wex, wrx,
    tok, h1, qkv, gsend, gbuf, wob, bias, send_w, recv_w, load, keep, save, send, recv, send_o, recv_o, send_f, recv_f,
):
    d, t, p, c = g.place()
    partner = (d, p * 2 + 1 - c)
    weights = (wi, wix)
    copy = pltpu.make_async_copy(tokens.at[pl.ds(pl.multiple_of(c * g.Rc, g.Rc), g.Rc)], tok, load)
    copy.start()
    meet([(d, flip(p, k, g.bits) * 2 + c) for k in range(1, g.G)] + [partner])

    def share(k):
        return remote(wo, wob.at[t], send_o.at[k], recv_o.at[k], (d, flip(p, k, g.bits) * 2 + c))

    def forward(k):
        row = flip(p, k, g.bits) * 2 + c
        src = wo if k == 0 else wob.at[row]
        return remote(src, wob.at[row], send_f.at[k], recv_f.at[k], partner)

    for k in range(1, g.G):
        share(k).start()
    forward(0).start()
    pair = [
        remote(src, dst, send_w.at[index], recv_w.at[index], partner)
        for index, (src, dst) in enumerate(((we, wex), (wr, wrx)))
    ]
    for weight in pair:
        weight.start()
    wob[t] = wo[...]
    copy.wait()
    scale = 1.0 / math.sqrt(g.hd)
    ones = jnp.ones((8, g.L), BF)
    for s in range(2):
        for r in range(2):
            line = jnp.where(
                lax.broadcasted_iota(jnp.int32, (8, g.hw), 0) == r + 1, smc[s, :, : g.hw], 0.0
            )
            bias[s, r] = tn(line.astype(BF), ones)

    def chunk(j):
        i, u = j // g.sub, lax.rem(j, g.sub)
        src = gsend.at[i] if g.sub == 1 else gsend.at[i, :, :, pl.ds(pl.multiple_of(u * g.Ro, g.Ro), g.Ro)]
        return src, gbuf.at[pl.ds(p * 2, 2)]

    def away(j):
        src, dst = chunk(j)
        return remote(src, dst, send.at[j], recv.at[p], (d, j * 2 + c))

    def arrive(j):
        src, _ = chunk(j)
        dst = gbuf.at[pl.ds(j * 2, 2)]
        return remote(src, dst, send.at[j], recv.at[j], (d, j * 2 + c))

    def home():
        src, dst = chunk(p)
        return pltpu.make_async_copy(src, dst, keep)

    def item(ii, carry):
        i = flip(p // g.sub, g.Ic - 1 - ii, g.bits)
        rows = pl.ds(pl.multiple_of(i * g.L, g.L), g.L)
        row = c * g.Ic + i

        @pl.when(ii == g.Ic - 1)
        def _():
            for k in range(1, g.G):
                share(k).wait_recv()
                forward(k).start()

        normed, _ = norm(tok[rows].astype(F32))
        hidden = (
            normed * (1.0 + mod[1, pl.ds(row, 1), :]) + mod[0, pl.ds(row, 1), :]
        ).astype(BF)
        h1[rows] = hidden
        for s in range(2):
            wide = nt(weights[s][...], hidden)
            core = c + s - 2 * c * s
            parts = split_heads(g, wide)
            for h in range(g.lh):
                hh = s * g.lh + h
                rows_h = slice(h * g.hd, (h + 1) * g.hd)
                q = (parts[h] + bias[s, 0, rows_h]).astype(BF)
                k = parts[g.lh + h].astype(BF)
                v = (parts[2 * g.lh + h] + bias[s, 1, rows_h]).astype(BF)
                qkv[hh * 3 + 0, :, rows] = q
                qkv[hh * 3 + 1, :, rows] = k
                qkv[hh * 3 + 2, :, rows] = v
                scores = tn(k, q) * scale
                peak = jnp.max(scores, axis=0, keepdims=True)
                powers = jnp.exp(scores - peak)
                total = jnp.sum(powers, axis=0, keepdims=True)
                lse[hh : hh + 1, rows] = peak + jnp.log(total)
                probs = (powers * (1.0 / total)).astype(BF)
                mixed = nn(v, probs)
                gate = gat[s, pl.ds(row, 1), 2 * h : 2 * h + 1]
                gsend[i, core, rows_h, :] = (mixed * gate).astype(BF)
        for u in range(g.sub):
            j = i * g.sub + u

            @pl.when(j == p)
            def _():
                home().start()

            @pl.when(j != p)
            def _():
                away(j).start()

        return carry

    lax.fori_loop(0, g.Ic, item, 0)
    saves = [pltpu.make_async_copy(h1, h1_out, save.at[0]), pltpu.make_async_copy(qkv, qkv_out, save.at[1])]
    for copy in saves:
        copy.start()
    home().wait()
    for k in range(1, g.G):
        arrive(flip(p, k, g.bits)).wait_recv()
    heads = gbuf[...].reshape(g.T * g.hw, g.Ro)
    gath[...] = heads
    for k in range(g.G):
        forward(k).wait_recv()
    saves.append(pltpu.make_async_copy(wob, wof, save.at[2]))
    saves[-1].start()
    full = wob[...].reshape(g.T * g.hw, g.W)
    attention = tn(heads, full) + ob[...]
    own = c * g.Ic + p // g.sub
    base = tok[pl.ds(pl.multiple_of(p * g.Ro, g.Ro), g.Ro)].astype(F32)
    residual = base + mod[2, pl.ds(own, 1), :] * attention
    att[...] = attention
    res[...] = residual
    normed, _ = norm(residual)
    h2[...] = (normed * (1.0 + mod[4, pl.ds(own, 1), :]) + mod[3, pl.ds(own, 1), :]).astype(BF)
    for k in range(1, g.G):
        away(flip(p, k, g.bits)).wait_send()
        share(k).wait_send()
    for k in range(g.G):
        forward(k).wait_send()
    for copy in saves:
        copy.wait()
    for copy in pair:
        copy.wait()


def feed_kernel(
    g, h2, cotangent, mod, gat, smc, we_in, wex_in, wr_in, wrx_in,
    grad_out, mpart_out, dwf_out, small, gates, ebs,
    cot, we, wex, wr, wrx, h2buf, bgbuf, gch, egb, sgb, own_g, xs, xr, mpart, dwf,
    joint, final, send_g, recv_g, leg_box, leg_sems, done, load, save, send_h, recv_h, send_p, recv_p,
):
    d, t, p, c = g.place()
    partner = (d, p * 2 + 1 - c)
    wec = (we, wex)
    wrc = (wr, wrx)

    def chip(k):
        return (d, flip(p, k, g.bits) * 2 + c)

    cot_rows = cotangent.at[pl.ds(pl.multiple_of(c * g.Rc, g.Rc), g.Rc)]
    loads = [
        pltpu.make_async_copy(src, dst, load.at[index])
        for index, (src, dst) in enumerate(
            ((cot_rows, cot), (wr_in, wr), (wrx_in, wrx), (we_in, we), (wex_in, wex))
        )
    ]
    for copy in loads:
        copy.start()
    leg = FirstLeg(g, g.fe, dwf, leg_box, leg_sems)
    meet([chip(k) for k in range(1, g.G)] + [partner, leg.other])

    spread = PlaneGather(g, h2, lambda k, source: h2buf.at[k], send_h, recv_h, chip, p)
    spread.start()
    back = PlaneScatter(g, lambda k: sgb.at[k - 1], joint, final, send_g, recv_g, chip)
    h2buf[0] = h2[...]
    for copy in loads:
        copy.wait()
    lane = lax.broadcasted_iota(jnp.int32, (1, g.ch), 1)
    tile_row = lax.broadcasted_iota(jnp.int32, (8, 128), 0)
    tile_lane = lax.broadcasted_iota(jnp.int32, (8, 128), 1)
    ebs[...] = jnp.zeros_like(ebs)
    gates[...] = jnp.zeros_like(gates)

    def block(k, carry):
        j = flip(p, k, g.bits)
        local = j // g.sub
        item = c * g.Ic + local
        rows = pl.ds(pl.multiple_of(j * g.Ro, g.Ro), g.Ro)
        here = pl.ds(pl.multiple_of(k * g.Ro, g.Ro), g.Ro)
        branch = (mod[5, pl.ds(item, 1), :] * cot[rows].astype(F32)).astype(BF)
        bgbuf[here] = branch
        grads = [nt(branch, wrc[s][...]) for s in range(2)]

        @pl.when(k == 1)
        def _():
            spread.relay()

        for kk in range(1, g.G):

            @pl.when(k == kk)
            def _():
                spread.wait(kk)

        hidden = h2buf[k]
        total = None
        for s in range(2):
            wide = nt(hidden, wec[s][...]) + smc[s, 0:1, : g.ch]
            inner = GELU_A * (wide + GELU_B * wide * wide * wide)
            tanh = jnp.tanh(inner)
            act = 0.5 * wide * (1.0 + tanh)
            slope = 0.5 * (1.0 + tanh) + 0.5 * wide * (1.0 - tanh * tanh) * (
                GELU_A * (1.0 + 3.0 * GELU_B * wide * wide)
            )
            gate = gat[s, pl.ds(item, 1), 1:2]
            for h in range(1, g.lh):
                gate = jnp.where(lane >= h * g.gc, gat[s, pl.ds(item, 1), 2 * h + 1 : 2 * h + 2], gate)
            gch[s, here] = (act * gate).astype(BF)
            line = jnp.sum(grads[s] * act, axis=0, keepdims=True)
            tile = gates[s]
            for h in range(g.lh):
                inside = jnp.where((lane >= h * g.gc) & (lane < (h + 1) * g.gc), line, 0.0)
                value = jnp.sum(inside, axis=1, keepdims=True)
                tile = tile + jnp.where((tile_row == local) & (tile_lane == 2 * h + 1), value, 0.0)
            gates[s] = tile
            egrad = (grads[s] * gate * slope).astype(BF)
            egb[s, here] = egrad
            ebs[s, 0:1, : g.ch] += jnp.sum(egrad.astype(F32), axis=0, keepdims=True)
            part = nn(egrad, wec[s][...])
            total = part if total is None else total + part

        @pl.when(k > 0)
        def _():
            sgb[k - 1] = total.astype(BF)
            back.put(k)

        @pl.when(k == 0)
        def _():
            own_g[...] = total

        return carry

    lax.fori_loop(0, g.G, block, 0)
    def swap(index):
        return remote(xs.at[index], xr.at[index], send_p.at[index], recv_p.at[index], partner)

    half_units = g.units // 2
    saves = []
    for index, left in enumerate((gch, egb)):
        right = bgbuf[...] if index == 0 else h2buf[...].reshape(g.Rc, g.W)
        xs[index] = tn(left[1], right).astype(BF)
        swap(index).start()
        value = tn(left[0], right)
        swap(index).wait_recv()
        value = (value + xr[index].astype(F32)).astype(BF)
        for u in range(half_units):
            dwf[index * half_units + u] = value[u * g.fr : (u + 1) * g.fr]
        if index == 0:
            leg.start()
            back.join()
    copy = pltpu.make_async_copy(dwf.at[pl.ds(g.fe, g.units - g.fe)], dwf_out.at[pl.ds(g.fe, g.units - g.fe)], save.at[0])
    copy.start()
    saves.append(copy)
    for k in range(g.G):
        rows = pl.ds(k * g.Ro, g.Ro)
        mpart[k] = (nn(gch[0, rows], wr[...]) + nn(gch[1, rows], wrx[...])).astype(BF)
    saves.append(pltpu.make_async_copy(mpart, mpart_out, save.at[2]))
    saves[-1].start()
    small[...] = jnp.zeros_like(small)
    small[7:8, :] = jnp.sum(bgbuf[0 : g.Ro].astype(F32), axis=0, keepdims=True)
    grad_out[...] = back.total(own_g[...])
    leg.add()
    copy = pltpu.make_async_copy(dwf.at[pl.ds(0, g.fe)], dwf_out.at[pl.ds(0, g.fe)], save.at[1])
    copy.start()
    saves.append(copy)
    leg.sent()

    @pl.when(leg.middle == 1)
    def _():
        pl.semaphore_signal(done, inc=1, device_id=leg.other, device_id_type=MESH)

    @pl.when(leg.middle == 0)
    def _():
        pl.semaphore_wait(done, 1)

    spread.sent()
    back.sent()
    swap(0).wait_send()
    swap(1).wait_send()
    for copy in saves:
        copy.wait()


def unattend_kernel(
    g, hgrad, h1_in, qkv_in, lse, gat, wi_in, wix_in, small_in, mpart_in, dwf, mod, att, res, wof_in, gath_in,
    cotangent, rbias, ebs, gates_in,
    grad, rgrad, bout, dwz, dwf_out, lines, sums, pay, gates,
    h1, qkv, wi, wix, mpart, wof, gath,
    hgs, hgbuf, wof_x, orr, osum, small, dqkv, acc, own_g, sgb, xs, xr, orv, sx, cot,
    work, first_z, second_z, more_z, sems_z, leg_box, leg_sems, joint_g, final_g, send_g, recv_g, joint_m, final_m, send_m, recv_m,
    send_o, recv_o, send_s, recv_s, send_p, recv_p, send_a, recv_a, send_x, recv_x,
    load,
):
    d, t, p, c = g.place()
    partner = (d, p * 2 + 1 - c)
    weights = (wi, wix)
    block = c * g.G + p

    def chip(k):
        return (d, flip(p, k, g.bits) * 2 + c)

    def peer(k):
        return (d, flip(t, k, g.tbits))

    def group(k):
        return (flip(d, k, g.dbits), t)

    fetch = pltpu.make_async_copy(
        cotangent.at[pl.ds(pl.multiple_of(block * g.Ro, g.Ro), g.Ro)], cot, load.at[0]
    )
    fetch.start()
    half = pltpu.make_async_copy(dwf, work, load.at[1])
    half.start()
    loads = [
        pltpu.make_async_copy(src, dst, load.at[2 + index])
        for index, (src, dst) in enumerate(
            (
                (wof_in, wof), (mpart_in, mpart), (gath_in, gath), (h1_in, h1), (qkv_in, qkv), (wi_in, wi),
                (wix_in, wix),
            )
        )
    ]
    for copy in loads:
        copy.start()
    zsum = GroupSum(g, g.units, work, first_z, second_z, more_z, dwf_out, sems_z)
    meet_line(g, [peer(k) for k in range(1, g.T)], group, zsum.middle)

    def rest(k):
        return remote(osum.at[flip(p, k, g.bits)], orv.at[k - 1], send_o.at[k], recv_o.at[k], chip(k))

    on = PlaneScatter(g, lambda k: mpart.at[k], joint_m, final_m, send_m, recv_m, chip)
    back = PlaneScatter(g, lambda k: sgb.at[k - 1], joint_g, final_g, send_g, recv_g, chip)

    def sumup(k):
        return remote(small, sx.at[k], send_s.at[k], recv_s.at[k], peer(k))

    def heads_out(k):
        return remote(hgs.at[pl.ds(flip(p, k, g.bits) * 2, 2)], hgbuf.at[k], send_a.at[k], recv_a.at[k], chip(k))

    def cross(q):
        return remote(wof_x.at[2 * q + 1 - c], orr.at[q], send_x.at[q], recv_x.at[q], partner)

    half.wait()
    everything = list(range(g.units))
    zsum.resume(everything[: g.fe])
    zsum.start(everything[g.fe :])
    leg = FirstLeg(g, g.ze, dwz, leg_box, leg_sems)
    fetch.wait()
    value = hgrad[...]
    own = c * g.Ic + p // g.sub
    normed, inverse = norm(res[...])
    cot_own = cot[...].astype(F32)
    residual = cot_own + norm_back(value * (1.0 + mod[4, pl.ds(own, 1), :]), normed, inverse)
    branch_one = (mod[2, pl.ds(own, 1), :] * residual).astype(BF)
    loads[0].wait()
    hgs[...] = nt(wof[...], branch_one).astype(BF).reshape(g.T, g.hw, g.Ro)
    for k in reversed(range(1, g.G)):
        heads_out(k).start()
    hgbuf[0] = hgs[pl.ds(p * 2, 2)]
    loads[1].wait()
    for k in reversed(range(1, g.G)):
        on.put(k)
    rgrad[...] = residual
    small[...] = small_in[...]
    small[2:3, :] = jnp.sum(residual * att[...], axis=0, keepdims=True)
    small[3:4, :] = jnp.sum(value, axis=0, keepdims=True)
    small[4:5, :] = jnp.sum(value * normed, axis=0, keepdims=True)
    small[6:7, :] = jnp.sum(branch_one.astype(F32), axis=0, keepdims=True)
    for k in range(1, g.T):
        sumup(k).start()
    for copy in loads[2:]:
        copy.wait()
    wof_x[...] = nn(gath[...], branch_one).astype(BF).reshape(g.T, g.hw, g.W)
    for q in range(g.G):
        cross(q).start()
    scale = 1.0 / math.sqrt(g.hd)
    acc[...] = jnp.zeros_like(acc)
    ones = jnp.ones((8, g.L), BF)
    tile_row = lax.broadcasted_iota(jnp.int32, (8, 128), 0)
    tile_lane = lax.broadcasted_iota(jnp.int32, (8, 128), 1)
    gates[...] = gates_in[...]
    pay[...] = ebs[...]

    def item(ii, carry):
        kk = lax.rem(g.Ic - ii, g.Ic)
        i = flip(p // g.sub, kk, g.bits)
        row = c * g.Ic + i
        rows = pl.ds(pl.multiple_of(i * g.L, g.L), g.L)
        slots = [kk * g.sub + (flip(lax.rem(p, g.sub), u, 4) if g.sub > 1 else 0) for u in range(g.sub)]
        hidden = h1[rows]
        total = None
        for u, slot in enumerate(slots):

            @pl.when(slot != 0)
            def _():
                heads_out(slot).wait_recv()

        @pl.when(ii == min(2, g.Ic - 1))
        def _():
            zsum.settle([1])
            zsum.join([3])

        @pl.when(ii == 1)
        def _():
            zsum.settle([0])
            zsum.join([2])
            for q in range(g.G):
                cross(q).wait()
                osum[q] = (wof_x[2 * q + c].astype(F32) + orr[q].astype(F32)).astype(BF)
            for k in range(1, g.G):
                rest(k).start()

        @pl.when(ii == g.Ic - 1)
        def _():
            on.join()

        for s in range(2):
            core = c + s - 2 * c * s
            tile = gates[s]
            for h in range(g.lh):
                hh = s * g.lh + h
                q = qkv[hh * 3 + 0, :, rows]
                k = qkv[hh * 3 + 1, :, rows]
                v = qkv[hh * 3 + 2, :, rows]
                pieces = [hgbuf[slot, core, h * g.hd : (h + 1) * g.hd, :] for slot in slots]
                heads = (pieces[0] if g.sub == 1 else jnp.concatenate(pieces, axis=1)).astype(F32)
                probs = jnp.exp(tn(k, q) * scale - lse[hh : hh + 1, rows])
                low = probs.astype(BF)
                mixed = nn(v, low)
                value = jnp.sum(jnp.sum(heads * mixed, axis=0, keepdims=True), axis=1, keepdims=True)
                tile = tile + jnp.where((tile_row == i) & (tile_lane == 2 * h), value, 0.0)
                mixed_grad = (gat[s, pl.ds(row, 1), 2 * h : 2 * h + 1] * heads).astype(BF)
                probs_grad = tn(v, mixed_grad)
                values_grad = nt(mixed_grad, low)
                score = (
                    probs * (probs_grad - jnp.sum(probs_grad * probs, axis=0, keepdims=True))
                ).astype(BF)
                queries_grad = nn(k, score) * scale
                keys_grad = nt(q, score) * scale
                for r, value in enumerate((queries_grad, keys_grad, values_grad)):
                    dqkv[s, r * g.hw + h * g.hd : r * g.hw + (h + 1) * g.hd, :] = value.astype(BF)
            gates[s] = tile
            wide = dqkv[s]
            part = tn(wide, weights[s][...])
            total = part if total is None else total + part
            acc[s] += nn(wide, hidden)
            pay[s, 1:2, : 3 * g.hw] += nt(ones, wide)[0:1]
        for u, slot in enumerate(slots):
            piece = total[u * g.Ro : (u + 1) * g.Ro]

            @pl.when(slot == 0)
            def _():
                own_g[...] = piece

            @pl.when(slot != 0)
            def _():
                sgb[slot - 1] = piece.astype(BF)
                back.put(slot)

        return carry

    lax.fori_loop(0, g.Ic, item, 0)
    xs[...] = acc[1].astype(BF)
    swap = remote(xs, xr, send_p, recv_p, partner)
    swap.start()
    zsum.settle([2])
    zsum.join([4])
    swap.wait()
    for u in range(g.units):
        low = u * g.zr
        if low < 3 * g.hw:
            span = slice(low, low + g.zr)
            dwz[u] = (acc[0, span] + xr[span].astype(F32)).astype(BF)
    leg.start()
    zsum.settle([3])
    zsum.join([5])
    zsum.settle([4])
    zsum.join([6])
    back.join()
    zsum.settle([5])
    zsum.join([7])
    value = small[...]
    for k in range(1, g.T):
        sumup(k).wait()
        value = value + sx[k]
    sums[...] = value
    out = osum[p].astype(F32)
    for k in range(1, g.G):
        rest(k).wait()
        out = out + orv[k - 1].astype(F32)
    for u in range(g.units):
        low = u * g.zr
        if low >= 3 * g.hw:
            dwz[u] = out[low - 3 * g.hw : low - 3 * g.hw + g.zr].astype(BF)
    zsum.settle([6])
    branch = on.total(mpart[0].astype(F32)) + rbias[...]
    bout[...] = (res[...] + mod[5, pl.ds(own, 1), :] * branch).astype(BF)
    lines[...] = small[...]
    lines[5:6, :] = jnp.sum(cot[...].astype(F32) * branch, axis=0, keepdims=True)
    grad[...] = back.total(own_g[...])
    on.sent()
    back.sent()
    zsum.settle([7])
    leg.add()
    zsum.end(everything, everything[g.fe :])
    leg.sent()
    for k in range(1, g.G):
        heads_out(k).wait_send()


def finish_kernel(
    g, grad, rgrad, tokens, mod, lines_in, sums, bout, pay, gates, dsg, dwz,
    tall, ball, colall, zall, logall, dwz_out,
    tok, tsend, stage, cbuf, zbuf, lbuf, pbuf, gbuf, work, first_z, second_z, more_z, sems_z,
    load, send_t, recv_t, send_f, recv_f, send_c, recv_c, send_p, recv_p, send_s, recv_s, keep,
):
    d, t, p, c = g.place()
    partner = (d, p * 2 + 1 - c)

    def chip(k):
        return (d, flip(p, k, g.bits) * 2 + c)

    def peer(k):
        return (d, flip(t, k, g.tbits))

    def group(k):
        return (flip(d, k, g.dbits), t)

    meet([peer(k) for k in range(1, g.T)] + [group(k) for k in range(1, g.D)])
    block = c * g.G + p
    mine = pl.ds(pl.multiple_of(block * g.Ro, g.Ro), g.Ro)
    copy = pltpu.make_async_copy(tokens.at[mine], tok, load)
    copy.start()
    swaps = [
        remote(pay.at[1], pbuf, send_p.at[0], recv_p.at[0], partner),
        remote(gates.at[1], gbuf, send_p.at[1], recv_p.at[1], partner),
    ]
    for swap in swaps:
        swap.start()
    zsum = GroupSum(g, g.units, work, first_z, second_z, more_z, dwz_out, sems_z)
    everything = list(range(g.units))
    work[...] = dwz[...]
    zsum.resume(everything[: g.ze])
    zsum.start(everything[g.ze :])

    def rows_of(dst):
        return lambda k, source: dst.at[pl.ds(pl.multiple_of((c * g.G + source) * g.Ro, g.Ro), g.Ro)]

    outs = PlaneGather(g, bout, rows_of(ball), send_t.at[0], recv_t.at[0], chip, p)
    grads = PlaneGather(g, tsend, rows_of(tall), send_t.at[1], recv_t.at[1], chip, p)
    outs.start()
    copy.wait()
    own = c * g.Ic + p // g.sub
    normed, inverse = norm(tok[...].astype(F32))
    value = grad[...]
    scaled = value * (1.0 + mod[1, pl.ds(own, 1), :])
    tsend[...] = (rgrad[...] + norm_back(scaled, normed, inverse)).astype(BF)
    lines = lines_in[...]
    kind = lax.broadcasted_iota(jnp.int32, lines.shape, 0)
    first = jnp.sum(value, axis=0, keepdims=True)
    second = jnp.sum(value * normed, axis=0, keepdims=True)
    lines = jnp.where(kind == 0, first, jnp.where(kind == 1, second, lines))
    w = g.mw
    stage[...] = jnp.zeros_like(stage)
    for member in range(g.T):
        stage[member, :, :w] = lines[:, member * w : (member + 1) * w]

    def columns(k):
        return remote(stage.at[flip(t, k, g.tbits)], cbuf.at[d, t], send_c.at[k], recv_c.at[k], peer(k))

    def column_in(k):
        return remote(stage.at[t], cbuf.at[d, flip(t, k, g.tbits)], send_c.at[k], recv_c.at[k], peer(k))

    for k in range(1, g.T):
        columns(k).start()
    cbuf[d, t] = stage[t]
    grads.start()
    local = [
        pltpu.make_async_copy(bout, ball.at[mine], keep.at[0]),
        pltpu.make_async_copy(tsend, tall.at[mine], keep.at[1]),
    ]
    for item in local:
        item.start()

    def forward(which, dst, k):
        rows = pl.ds(pl.multiple_of((c * g.G + flip(p, k, g.bits)) * g.Ro, g.Ro), g.Ro)
        return remote(dst.at[rows], dst.at[rows], send_f.at[which, k], recv_f.at[which, k], partner)

    def arrive_forward(which, dst, k):
        rows = pl.ds(pl.multiple_of(((1 - c) * g.G + flip(p, k, g.bits)) * g.Ro, g.Ro), g.Ro)
        return remote(dst.at[rows], dst.at[rows], send_f.at[which, k], recv_f.at[which, k], partner)

    outs.relay()
    zsum.join([4])
    zsum.settle([0, 1])
    for swap in swaps:
        swap.wait()
    zbuf[d] = jnp.zeros((8, g.W), F32)
    zbuf[d, 0:2] = pay[0, 0:2] + pbuf[0:2]
    zbuf[d, 2:4] = sums[6:8]
    both = jnp.concatenate([gates[0, : g.Ic], gbuf[: g.Ic]], axis=0)
    turned = jnp.concatenate([gbuf[: g.Ic], gates[0, : g.Ic]], axis=0)
    lbuf[d] = jnp.where(c == 0, both, turned) * dsg[...]
    zsum.join([5, 6])
    zsum.settle([2])
    for k in range(1, g.T):
        columns(k).wait_send()
        column_in(k).wait_recv()

    def share(k):
        return [
            remote(cbuf.at[d], cbuf.at[d], send_s.at[0, k], recv_s.at[0, k], group(k)),
            remote(zbuf.at[d], zbuf.at[d], send_s.at[1, k], recv_s.at[1, k], group(k)),
            remote(lbuf.at[d], lbuf.at[d], send_s.at[2, k], recv_s.at[2, k], group(k)),
        ]

    def shared(k):
        other = flip(d, k, g.dbits)
        return [
            remote(cbuf.at[other], cbuf.at[other], send_s.at[0, k], recv_s.at[0, k], group(k)),
            remote(zbuf.at[other], zbuf.at[other], send_s.at[1, k], recv_s.at[1, k], group(k)),
            remote(lbuf.at[other], lbuf.at[other], send_s.at[2, k], recv_s.at[2, k], group(k)),
        ]

    for k in range(1, g.D):
        for item in share(k):
            item.start()
    for which, dst in ((0, ball), (1, tall)):
        local[which].wait()
        forward(which, dst, 0).start()
    zsum.join([7])
    zsum.settle([3, 4])
    grads.relay()
    zsum.settle([5, 6, 7])
    for k in range(1, g.G):
        outs.wait(k)
        forward(0, ball, k).start()
    for k in range(1, g.D):
        for item in share(k):
            item.wait_send()
        for item in shared(k):
            item.wait_recv()
    colall[...] = cbuf[...]
    zall[...] = zbuf[...]
    logall[...] = lbuf[...]
    for k in range(1, g.G):
        grads.wait(k)
        forward(1, tall, k).start()
    zsum.end(everything, everything[g.ze :])
    outs.sent()
    grads.sent()
    for which, dst in ((0, ball), (1, tall)):
        for k in range(g.G):
            forward(which, dst, k).wait_send()
            arrive_forward(which, dst, k).wait_recv()


def wrap_kernel(
    g, ball, tall, dwf, dwz, colall, zall, logall, conds,
    out, tokens_grad, dwr, dwe, dwi, dwo, dwm, dmb, drw, drb, dib, deb, dob, drb_all,
    twice,
):
    step = pl.program_id(0)
    out[...] = ball[...].astype(F32)
    tokens_grad[...] = tall[...].astype(F32)
    half_units = g.units // 2
    heads = 3 * g.units // 4

    @pl.when(step < half_units)
    def _():
        dwr[...] = dwf[...].astype(F32)

    @pl.when(step >= half_units)
    def _():
        dwe[...] = dwf[...].astype(F32)

    @pl.when(step < heads)
    def _():
        dwi[...] = dwz[...].astype(F32)

    @pl.when(step >= heads)
    def _():
        dwo[...] = dwz[...].astype(F32)

    w = g.mw

    @pl.when(step == 0)
    def _():
        rows = []
        for member in range(g.T):
            rows.append(((member % 2) * g.G + member // 2) * g.Ro // g.L)
        value = conds[...]
        silu = value / (1.0 + jnp.exp(-value))
        picked = jnp.concatenate([silu[z, i : i + 1] for z in range(g.D) for i in rows], axis=0).astype(BF)
        twice[...] = jnp.concatenate([picked, picked], axis=0)
        logits = jnp.concatenate([logall[z] for z in range(g.D)], axis=0)
        high = logits.astype(BF)
        low = (logits - high.astype(F32)).astype(BF)
        flat = jnp.concatenate([value[z] for z in range(g.D)], axis=0).astype(BF)
        router = tn(jnp.concatenate([high, low], axis=0), jnp.concatenate([flat, flat], axis=0))
        sums = jnp.sum(logits, axis=0, keepdims=True)
        for h in range(g.lh):
            drw[h] = router[2 * h : 2 * h + 2, :]
            drb[h : h + 1, :] = sums[:, 2 * h : 2 * h + 2]
        total = zall[0]
        for z in range(1, g.D):
            total = total + zall[z]
        dib[0:1, :] = total[1:2, : g.hw]
        dib[1:2, :] = total[1:2, 2 * g.hw : 3 * g.hw]
        deb[...] = total[0, : g.ch]
        dob[...] = total[2]
        drb_all[...] = total[3]

    @pl.when(step < 6)
    def _():
        part = jnp.concatenate(
            [colall[z, member, pl.ds(step, 1), :] for z in range(g.D) for member in range(g.T)], axis=0
        )
        dmb[pl.ds(step, 1), :] = jnp.sum(part, axis=0, keepdims=True)[:, :w]
        high = part.astype(BF)
        low = (part - high.astype(F32)).astype(BF)
        dwm[...] = tn(jnp.concatenate([high, low], axis=0), twice[...])[:w]


def wrap(g, ball, tall, dwf, dwz, colall, zall, logall, conds):
    n, W = g.units, g.W
    half_units, heads = n // 2, 3 * n // 4
    rows = g.R // n

    def whole(shape):
        return pl.BlockSpec(shape, lambda i: (0,) * len(shape))

    def part(shape, low, count):
        return pl.BlockSpec(shape, lambda i: (jnp.clip(i - low, 0, count - 1),) + (0,) * (len(shape) - 1))

    outs = [
        ((g.R, W), part((rows, W), 0, n)), ((g.R, W), part((rows, W), 0, n)),
        ((half_units, g.fr, W), part((1, g.fr, W), 0, half_units)),
        ((half_units, g.fr, W), part((1, g.fr, W), half_units, half_units)),
        ((heads, g.zr, W), part((1, g.zr, W), 0, heads)), ((n - heads, g.zr, W), part((1, g.zr, W), heads, n - heads)),
        ((6 * g.mw, W), part((g.mw, W), 0, 6)), ((6, g.mw), whole((6, g.mw))), ((g.lh, 2, W), whole((g.lh, 2, W))),
        ((g.lh, 2), whole((g.lh, 2))), ((2, g.hw), whole((2, g.hw))), ((g.ch,), whole((g.ch,))), ((W,), whole((W,))),
        ((W,), whole((W,))),
    ]
    return pl.pallas_call(
        functools.partial(wrap_kernel, g),
        name="wrap",
        grid=(n,),
        out_shape=[jax.ShapeDtypeStruct(s, F32) for s, _ in outs],
        in_specs=[
            part((rows, W), 0, n), part((rows, W), 0, n), part((1, g.fr, W), 0, n), part((1, g.zr, W), 0, n),
            whole(colall.shape), whole(zall.shape), whole(logall.shape), whole(conds.shape),
        ],
        out_specs=[spec for _, spec in outs],
        scratch_shapes=[pltpu.VMEM((2 * g.D * g.T, W), BF)],
        cost_estimate=pl.CostEstimate(flops=10**9, bytes_accessed=4 * 10**7, transcendentals=0),
        compiler_params=pltpu.CompilerParams(vmem_limit_bytes=VMEM_LIMIT),
    )(ball, tall, dwf, dwz, colall, zall, logall, conds)


def body(
    groups, members,
    tokens, condition, timesteps, route_masks, modulate_weight, modulate_bias, input_weight, input_bias,
    output_weight, output_bias, expand_weight, expand_bias, reduce_weight, reduce_bias, router_weight, router_bias,
    out_cotangent,
):
    g = Plan(
        groups, members, tokens.shape[0], condition.shape[0], tokens.shape[1], router_weight.shape[1],
        modulate_weight.shape[2], input_weight.shape[2], expand_weight.shape[1],
    )
    dma = pltpu.SemaphoreType.DMA
    V = pltpu.VMEM
    W, T, G, D, I = g.W, g.T, g.G, g.D, g.I
    wide = 2 * g.lh
    wm = jnp.transpose(modulate_weight, (1, 2, 0)).reshape(6 * g.mw, W)
    wi = jnp.transpose(input_weight, (1, 2, 0)).reshape(3 * g.hw, W)
    we = expand_weight.T
    wr = reduce_weight
    rw = jnp.transpose(router_weight, (1, 2, 0))
    masks = jnp.transpose(route_masks, (1, 2, 0))
    eb = expand_bias.astype(F32)[None]
    ob = output_bias.astype(F32)[None]
    rbias = reduce_bias.astype(F32)[None]

    mod, gat, dsg, smc, conds, wix = call(
        functools.partial(start_kernel, g), "start",
        (condition, wm, modulate_bias, timesteps, masks, rw, router_bias, eb, input_bias, wi),
        "vvvsvvvvvh",
        [
            ((6, I, W), F32), ((2, I, 128), F32), ((I, 128), F32), ((2, 8, W), F32), ((D, I, W), F32),
            ((3 * g.hw, W), BF),
        ],
        "vvvvvh",
        [
            V((T, I, 6 * g.mw), F32), V((2, I, 128), F32), V((2, 8, W), F32), V((D, I, W), F32),
            dma((T,)), dma((T,)), dma((3,)), dma((3,)), dma((D,)), dma((D,)),
        ],
        1,
    )
    h1, qkv, lse, att, res, h2, gath, wof, wex, wrx = call(
        functools.partial(attend_kernel, g), "attend",
        (tokens, mod, gat, smc, wi, wix, output_weight, ob, we, wr), "hvvvvvvvhh",
        [
            ((g.Rc, W), BF), ((wide * 3, g.hd, g.Rc), BF), ((wide, g.Rc), F32),
            ((g.Ro, W), F32), ((g.Ro, W), F32), ((g.Ro, W), BF), ((T * g.hw, g.Ro), BF), ((T, g.hw, W), BF),
            ((g.ch, W), BF), ((g.ch, W), BF),
        ],
        "hhvvvvvhhh",
        [
            V((g.Rc, W), BF), V((g.Rc, W), BF), V((wide * 3, g.hd, g.Rc), BF), V((g.Ic, 2, g.hw, g.L), BF), V((T, g.hw, g.Ro), BF), V((T, g.hw, W), BF),
            V((2, 2, g.hw, g.L), F32), dma((2,)), dma((2,)), dma, dma, dma((3,)), dma((G,)), dma((G,)), dma((G,)), dma((G,)), dma((G,)), dma((G,)),
        ],
        2,
    )
    hgrad, mpart, dwf, small, gates, ebs = call(
        functools.partial(feed_kernel, g), "feed",
        (h2, out_cotangent, mod, gat, smc, we, wex, wr, wrx), "vhvvvhhhh",
        [
            ((g.Ro, W), F32), ((G, g.Ro, W), BF), ((g.units, g.fr, W), BF),
            ((8, W), F32), ((2, 8, 128), F32), ((2, 8, W), F32),
        ],
        "vhhvvv",
        [
            V((g.Rc, W), BF), V((g.ch, W), BF), V((g.ch, W), BF), V((g.ch, W), BF), V((g.ch, W), BF),
            V((G, g.Ro, W), BF), V((g.Rc, W), BF), V((2, g.Rc, g.ch), BF), V((2, g.Rc, g.ch), BF),
            V((G - 1, g.Ro, W), BF), V((g.Ro, W), F32),
            V((2, g.ch, W), BF), V((2, g.ch, W), BF), V((G, g.Ro, W), BF), V((g.units, g.fr, W), BF),
        ]
        + PlaneScatter.scratch(g)
        + FirstLeg.scratch(g, g.fe, g.fr)
        + [pltpu.SemaphoreType.REGULAR, dma((5,)), dma((3,)), dma((G, 2)), dma((G, 2)), dma((2,)), dma((2,))],
        3,
    )
    grad, rgrad, bout, dwz, dwf, lines, sums, pay, gates = call(
        functools.partial(unattend_kernel, g), "unattend",
        (
            hgrad, h1, qkv, lse, gat, wi, wix, small, mpart, dwf, mod, att, res,
            wof.reshape(T * g.hw, W), gath, out_cotangent, rbias, ebs, gates,
        ),
        "vhhvvhhvhhvvvhhhvvv",
        [
            ((g.Ro, W), F32), ((g.Ro, W), F32), ((g.Ro, W), BF), ((g.units, g.zr, W), BF),
            ((g.units, g.fr, W), BF), ((8, W), F32), ((8, W), F32), ((2, 8, W), F32), ((2, 8, 128), F32),
        ],
        "vvvvvvvvv",
        [
            V((g.Rc, W), BF), V((wide * 3, g.hd, g.Rc), BF), V((3 * g.hw, W), BF), V((3 * g.hw, W), BF),
            V((G, g.Ro, W), BF), V((T * g.hw, W), BF), V((T * g.hw, g.Ro), BF),
            V((T, g.hw, g.Ro), BF), V((G, 2, g.hw, g.Ro), BF), V((T, g.hw, W), BF), V((G, g.hw, W), BF),
            V((G, g.hw, W), BF), V((8, W), F32),
            V((2, 3 * g.hw, g.L), BF), V((2, 3 * g.hw, W), F32), V((g.Ro, W), F32), V((G - 1, g.Ro, W), BF),
            V((3 * g.hw, W), BF), V((3 * g.hw, W), BF),
            V((G - 1, g.hw, W), BF), V((T, 8, W), F32), V((g.Ro, W), BF),
        ]
        + GroupSum.scratch(g, g.units, g.fr)
        + FirstLeg.scratch(g, g.ze, g.zr)
        + PlaneScatter.scratch(g)
        + PlaneScatter.scratch(g)
        + [
            dma((G,)), dma((G,)), dma((T,)), dma((T,)), dma, dma,
            dma((G,)), dma((G,)), dma((G,)), dma((G,)), dma((9,)),
        ],
        4,
    )
    tall, ball, colall, zall, logall, dwz = call(
        functools.partial(finish_kernel, g), "finish",
        (grad, rgrad, tokens, mod, lines, sums, bout, pay, gates, dsg, dwz), "vvhvvvvvvvv",
        [
            ((g.R, W), BF), ((g.R, W), BF), ((D, T, 8, g.cw), F32), ((D, 8, W), F32), ((D, I, 128), F32),
            ((g.units, g.zr, W), BF),
        ],
        "hhvvvv",
        [
            V((g.Ro, W), BF), V((g.Ro, W), BF), V((T, 8, g.cw), F32), V((D, T, 8, g.cw), F32), V((D, 8, W), F32),
            V((D, I, 128), F32), V((8, W), F32), V((8, 128), F32),
        ]
        + GroupSum.scratch(g, g.units, g.zr)
        + [
            dma, dma((2, G, 2)), dma((2, G, 2)), dma((2, G)), dma((2, G)), dma((T,)), dma((T,)), dma((2,)), dma((2,)),
            dma((3, D)), dma((3, D)), dma((2,)),
        ],
        5,
    )
    out, tokens_grad, dwr, dwe, dwi, dwo, dwm, dmb, drw, drb, dib, deb, dob, drb_all = wrap(
        g, ball, tall, dwf, dwz, colall, zall, logall, conds
    )
    return (
        out,
        tokens_grad,
        jnp.transpose(dwm.reshape(6, g.mw, W), (2, 0, 1)),
        dmb,
        jnp.transpose(dwi.reshape(3, g.hw, W), (2, 0, 1)),
        dib,
        dwo.reshape(g.hw, W),
        dob,
        dwe.reshape(g.ch, W).T,
        deb,
        dwr.reshape(g.ch, W),
        drb_all,
        jnp.transpose(drw, (2, 0, 1)),
        drb,
    )


def solution(mesh):
    return jax.shard_map(
        functools.partial(body, mesh.shape["dp"], mesh.shape["tensor"]),
        mesh=mesh,
        in_specs=(
            P("dp", None), P("dp", None), P("dp"), P(None, "tensor", None), P(None, None, "tensor"),
            P(None, "tensor"), P(None, None, "tensor"), P(None, "tensor"), P("tensor", None), P(),
            P(None, "tensor"), P("tensor"), P("tensor", None), P(), P(None, "tensor", None), P("tensor", None),
            P("dp", None),
        ),
        out_specs=(
            P("dp", None), P("dp", None), P(None, None, "tensor"), P(None, "tensor"), P(None, None, "tensor"),
            P(None, "tensor"), P("tensor", None), P(), P(None, "tensor"), P("tensor"), P("tensor", None), P(),
            P(None, "tensor", None), P("tensor", None),
        ),
        check_vma=False,
    )
```

```python
import functools
import math

import jax
import jax.numpy as jnp
from jax import lax
from jax.experimental import pallas as pl
from jax.experimental.pallas import tpu as pltpu
from jax.sharding import PartitionSpec as P

BF = jnp.bfloat16
F32 = jnp.float32
MESH = pl.DeviceIdType.MESH
EPSILON = 1e-06
GELU_A = math.sqrt(2.0 / math.pi)
GELU_B = 0.044715
VMEM_LIMIT = 58 << 20


def nt(left, right):
    return lax.dot_general(left, right, (((1,), (1,)), ((), ())), preferred_element_type=F32)


def nn(left, right):
    return lax.dot_general(left, right, (((1,), (0,)), ((), ())), preferred_element_type=F32)


def tn(left, right):
    return lax.dot_general(left, right, (((0,), (0,)), ((), ())), preferred_element_type=F32)


def flip(value, mask, bits):
    total = 0
    for bit in range(bits):
        unit = 1 << bit
        total = total + lax.rem(value // unit + mask // unit, 2) * unit
    return total


def norm(values):
    center = values - jnp.mean(values, axis=-1, keepdims=True)
    inverse = lax.rsqrt(jnp.mean(center * center, axis=-1, keepdims=True) + EPSILON)
    return center * inverse, inverse


def norm_back(grad, normed, inverse):
    mean_grad = jnp.mean(grad, axis=-1, keepdims=True)
    mean_cross = jnp.mean(grad * normed, axis=-1, keepdims=True)
    return inverse * (grad - mean_grad - normed * mean_cross)


class Plan:
    def __init__(self, groups, members, rows, items, width, heads, modwidth, headwidth, channels):
        self.D = groups
        self.T = members
        self.G = members // 2
        self.bits = self.G.bit_length() - 1
        self.tbits = members.bit_length() - 1
        self.dbits = groups.bit_length() - 1
        self.R = rows
        self.I = items
        self.L = rows // items
        self.W = width
        self.Rc = rows // 2
        self.Ro = rows // members
        self.Ic = items // 2
        self.sub = self.L // self.Ro
        self.lh = heads
        self.mw = modwidth
        self.cw = -(-modwidth // 128) * 128
        self.hw = headwidth
        self.hd = headwidth // heads
        self.ch = channels
        self.gc = channels // heads
        self.hr = 2 * headwidth
        self.units = 8
        self.fr = 2 * channels // self.units
        self.zr = 4 * headwidth // self.units
        self.fe = 2
        self.ze = 4

    def place(self):
        d = lax.axis_index("dp")
        t = lax.axis_index("tensor")
        return d, t, t // 2, lax.rem(t, 2)


def greet(devices):
    barrier = pltpu.get_barrier_semaphore()
    for device in devices:
        pl.semaphore_signal(barrier, inc=1, device_id=device, device_id_type=MESH)
    return barrier


def meet(devices):
    pl.semaphore_wait(greet(devices), len(devices))


def meet_line(g, devices, group, middle):
    barrier = pltpu.get_barrier_semaphore()
    for device in devices + [group(1)]:
        pl.semaphore_signal(barrier, inc=1, device_id=device, device_id_type=MESH)
    others = [group(3)] + [group(4 << level) for level in range(g.dbits - 2)]

    @pl.when(middle == 1)
    def _():
        for device in others:
            pl.semaphore_signal(barrier, inc=1, device_id=device, device_id_type=MESH)
        pl.semaphore_wait(barrier, len(devices) + 1 + len(others))

    @pl.when(middle == 0)
    def _():
        pl.semaphore_wait(barrier, len(devices) + 1)


def remote(src, dst, send, recv, device):
    return pltpu.make_async_remote_copy(
        src_ref=src, dst_ref=dst, send_sem=send, recv_sem=recv, device_id=device, device_id_type=MESH
    )


class GroupSum:
    def __init__(self, g, count, work, first, second, more, full, sems):
        self.g, self.count, self.work, self.first, self.second = g, count, work, first, second
        self.more, self.full, self.sems = more, full, sems
        self.d, self.t = lax.axis_index("dp"), lax.axis_index("tensor")
        self.middle = lax.rem(lax.rem(self.d, 4) + 1, 4) // 2

    def device(self, mask):
        return (flip(self.d, mask, self.g.dbits), self.t)

    def copy(self, kind, src, dst, unit, mask):
        return remote(src.at[unit], dst.at[unit], self.sems.at[kind, unit], self.sems.at[kind + 1, unit], self.device(mask))

    def up(self, unit):
        return self.copy(0, self.work, self.first, unit, 1)

    def over(self, unit):
        return self.copy(2, self.work, self.second, unit, 3)

    def down(self, unit):
        return self.copy(4, self.full, self.full, unit, 1)

    def across(self, unit, level):
        src = self.more.at[2 * level, unit]
        dst = self.more.at[2 * level + 1, unit]
        kind = 6 + 2 * level
        return remote(src, dst, self.sems.at[kind, unit], self.sems.at[kind + 1, unit], self.device(4 << level))

    def start(self, units):
        @pl.when(self.middle == 0)
        def _():
            for unit in units:
                self.up(unit).start()

    def resume(self, units):
        @pl.when(self.middle == 1)
        def _():
            for unit in units:
                self.over(unit).start()

    def join(self, units):
        @pl.when(self.middle == 1)
        def _():
            for unit in units:
                self.up(unit).wait_recv()
                self.work[unit] = (self.work[unit].astype(F32) + self.first[unit].astype(F32)).astype(BF)
                self.over(unit).start()

    def settle(self, units):
        @pl.when(self.middle == 1)
        def _():
            for unit in units:
                self.over(unit).wait_recv()
                value = (self.work[unit].astype(F32) + self.second[unit].astype(F32)).astype(BF)
                for level in range(self.g.dbits - 2):
                    self.more[2 * level, unit] = value
                    copy = self.across(unit, level)
                    copy.start()
                    copy.wait()
                    value = (value.astype(F32) + self.more[2 * level + 1, unit].astype(F32)).astype(BF)
                self.full[unit] = value
                self.down(unit).start()

    def end(self, units, started):
        @pl.when(self.middle == 0)
        def _():
            for unit in started:
                self.up(unit).wait_send()
            for unit in units:
                self.down(unit).wait_recv()

        @pl.when(self.middle == 1)
        def _():
            for unit in units:
                self.over(unit).wait_send()
                self.down(unit).wait_send()

    @staticmethod
    def scratch(g, count, rows):
        levels = max(g.dbits - 2, 0)
        return [
            pltpu.VMEM((count, rows, g.W), BF), pltpu.VMEM((count, rows, g.W), BF), pltpu.VMEM((count, rows, g.W), BF),
            pltpu.VMEM((max(2 * levels, 1), count if levels else 1, rows if levels else 16, g.W), BF),
            pltpu.SemaphoreType.DMA((6 + 2 * levels, count)),
        ]


class FirstLeg:
    def __init__(self, g, units, work, inbox, sems):
        self.g, self.units, self.work, self.inbox, self.sems = g, units, work, inbox, sems
        d = lax.axis_index("dp")
        self.middle = lax.rem(lax.rem(d, 4) + 1, 4) // 2
        self.other = (flip(d, 1, g.dbits), lax.axis_index("tensor"))

    def copy(self, unit):
        return remote(self.work.at[unit], self.inbox.at[unit], self.sems.at[0, unit], self.sems.at[1, unit], self.other)

    def start(self):
        @pl.when(self.middle == 0)
        def _():
            for unit in range(self.units):
                self.copy(unit).start()

    def add(self):
        @pl.when(self.middle == 1)
        def _():
            for unit in range(self.units):
                self.copy(unit).wait_recv()
                self.work[unit] = (self.work[unit].astype(F32) + self.inbox[unit].astype(F32)).astype(BF)

    def sent(self):
        @pl.when(self.middle == 0)
        def _():
            for unit in range(self.units):
                self.copy(unit).wait_send()

    @staticmethod
    def scratch(g, units, rows):
        return [pltpu.VMEM((units, rows, g.W), BF), pltpu.SemaphoreType.DMA((2, units))]


def half(g, ref, which):
    return ref.at[pl.ds(which * (g.Ro // 2), g.Ro // 2)]


class PlaneGather:
    def __init__(self, g, src, place, send, recv, chip, p):
        self.g, self.src, self.place, self.send, self.recv, self.chip, self.p = g, src, place, send, recv, chip, p
        self.relayed = g.G == 4

    def source(self, k):
        return flip(self.p, k, self.g.bits)

    def own(self, k, h):
        g = self.g
        return remote(
            half(g, self.src, h), half(g, self.place(k, self.p), h), self.send.at[k, h], self.recv.at[k, h], self.chip(k)
        )

    def arrival(self, k, h):
        g = self.g
        place = half(g, self.place(k, self.source(k)), h)
        return remote(place, place, self.send.at[k, h], self.recv.at[k, h], self.chip(k))

    def onward(self, h):
        g = self.g
        k = 1 + h
        src = half(g, self.place(k, self.source(k)), h)
        dst = half(g, self.place(3, self.source(k)), h)
        return remote(src, dst, self.send.at[3, h], self.recv.at[3, h], self.chip(2 - h))

    def start(self):
        if self.relayed:
            for k, h in ((1, 0), (2, 1), (1, 1), (2, 0)):
                self.own(k, h).start()
        else:
            for k in range(1, self.g.G):
                for h in range(2):
                    self.own(k, h).start()

    def relay(self):
        if self.relayed:
            for h in range(2):
                self.arrival(1 + h, h).wait_recv()
                self.onward(h).start()

    def wait(self, k):
        for h in range(2):
            if not (self.relayed and k < 3 and h == k - 1):
                self.arrival(k, h).wait_recv()

    def sent(self):
        for h in range(2):
            for k in range(1, 3 if self.relayed else self.g.G):
                self.own(k, h).wait_send()
            if self.relayed:
                self.onward(h).wait_send()


class PlaneScatter:
    def __init__(self, g, part, joint, final, send, recv, chip):
        self.g, self.part, self.joint, self.final = g, part, joint, final
        self.send, self.recv, self.chip = send, recv, chip
        self.relayed = g.G == 4

    def far(self, h):
        return remote(
            half(self.g, self.part(3), h), self.joint.at[h], self.send.at[2, h], self.recv.at[2, h], self.chip(1 + h)
        )

    def near(self, k, h):
        g = self.g
        return remote(
            half(g, self.part(k), h), half(g, self.final.at[k - 1], h), self.send.at[k - 1, h], self.recv.at[k - 1, h],
            self.chip(k),
        )

    def put(self, k):
        if not self.relayed:
            for h in range(2):
                self.near(k, h).start()
        elif isinstance(k, int):
            if k == 3:
                self.far(0).start()
                self.far(1).start()
            else:
                self.near(k, k - 1).start()
        else:
            for kk in range(1, 4):

                @pl.when(k == kk)
                def _():
                    self.put(kk)

    def join(self):
        if self.relayed:
            for h in range(2):
                k = 2 - h
                self.far(h).wait_recv()
                rows = pl.ds(h * (self.g.Ro // 2), self.g.Ro // 2)
                ref = self.part(k)
                ref[rows] = (ref[rows].astype(F32) + self.joint[h].astype(F32)).astype(BF)
                self.near(k, h).start()

    def total(self, value):
        for k in range(1, 3 if self.relayed else self.g.G):
            for h in range(2):
                self.near(k, h).wait_recv()
            value = value + self.final[k - 1].astype(F32)
        return value

    def sent(self):
        for h in range(2):
            for k in range(1, 3 if self.relayed else self.g.G):
                self.near(k, h).wait_send()
            if self.relayed:
                self.far(h).wait_send()

    @staticmethod
    def scratch(g):
        dma = pltpu.SemaphoreType.DMA
        return [
            pltpu.VMEM((2, g.Ro // 2, g.W), BF), pltpu.VMEM((2 if g.G == 4 else g.G - 1, g.Ro, g.W), BF),
            dma((g.G, 2)), dma((g.G, 2)),
        ]


def call(kernel, name, inputs, in_spaces, outs, out_spaces, scratch, collective, cost=None):
    spec = {
        "v": pl.BlockSpec(memory_space=pltpu.VMEM),
        "h": pl.BlockSpec(memory_space=pl.ANY),
        "s": pl.BlockSpec(memory_space=pltpu.SMEM),
    }
    flops, moved = cost or (10**8, 10**7)
    return pl.pallas_call(
        kernel,
        name=name,
        out_shape=[jax.ShapeDtypeStruct(s, t) for s, t in outs],
        in_specs=[spec[x] for x in in_spaces],
        out_specs=[spec[x] for x in out_spaces],
        scratch_shapes=scratch,
        cost_estimate=pl.CostEstimate(flops=flops, bytes_accessed=moved, transcendentals=0),
        compiler_params=pltpu.CompilerParams(
            collective_id=collective, has_side_effects=collective is not None, vmem_limit_bytes=VMEM_LIMIT
        ),
    )(*inputs)


def start_kernel(
    g, cond, wm, mb, ts, masks, rw, rb, eb, ib, wi,
    mod, gat, dsg, smc, call_all, wix,
    mpart, gx, sx, cx, send_m, recv_m, send_w, recv_w, send_c, recv_c,
):
    d, t, p, c = g.place()
    partner = (d, p * 2 + 1 - c)
    devices = [(d, flip(t, k, g.tbits)) for k in range(1, g.T)]
    devices = devices + [(flip(d, k, g.dbits), t) for k in range(1, g.D)]
    barrier = greet(devices)
    value = cond[...]
    silu = (value / (1.0 + jnp.exp(-value))).astype(BF)
    part = nt(silu, wm[...])
    w = g.mw
    bias = mb[...].astype(F32)
    for row in range(6):
        mpart[t, :, row * w : (row + 1) * w] = part[:, row * w : (row + 1) * w] + bias[row : row + 1]

    pl.semaphore_wait(barrier, len(devices))
    pair = remote(wi, wix, send_w.at[2], recv_w.at[2], partner)

    def spread(k):
        return remote(
            mpart.at[t], mpart.at[t], send_m.at[k], recv_m.at[k], (d, flip(t, k, g.tbits))
        )

    for k in range(1, g.T):
        spread(k).start()
    pair.start()
    low = value.astype(BF)
    steps = masks.shape[2]
    row = lax.broadcasted_iota(jnp.int32, (g.I, steps), 0)
    wanted = jnp.zeros((g.I, steps), jnp.int32)
    for item in range(g.I):
        wanted = jnp.where(row == item, ts[item], wanted)
    hot = (wanted == lax.broadcasted_iota(jnp.int32, (g.I, steps), 1)).astype(F32).astype(BF)
    dsg[...] = jnp.zeros_like(dsg)
    gx[0] = jnp.zeros((g.I, 128), F32)
    scale = rb[...].astype(F32)
    for h in range(g.lh):
        logits = nt(low, rw[h]) + scale[h : h + 1]
        sigmoid = 1.0 / (1.0 + jnp.exp(-logits))
        mask = nt(hot, masks[h].astype(F32).astype(BF))
        dsg[:, 2 * h : 2 * h + 2] = mask * sigmoid * (1.0 - sigmoid)
        gx[0, :, 2 * h : 2 * h + 2] = mask * sigmoid
    sx[0] = jnp.zeros((8, g.W), F32)
    sx[0, 0:1, : g.ch] = eb[...].astype(F32).reshape(1, g.ch)
    sx[0, 1:3, : g.hw] = ib[...].astype(F32)
    small = [
        remote(gx.at[0], gx.at[1], send_w.at[0], recv_w.at[0], partner),
        remote(sx.at[0], sx.at[1], send_w.at[1], recv_w.at[1], partner),
    ]
    for copy in small:
        copy.start()

    def conditions(k):
        return remote(cond, cx.at[d], send_c.at[k], recv_c.at[k], (flip(d, k, g.dbits), t))

    for k in range(1, g.D):
        conditions(k).start()
    cx[d] = value
    for k in range(1, g.T):
        spread(k).wait()
    for member in range(g.T):
        for row in range(6):
            mod[row, :, member * w : (member + 1) * w] = mpart[member, :, row * w : (row + 1) * w]
    for copy in small:
        copy.wait()
    gat[...] = gx[...]
    smc[...] = sx[...]
    pair.wait()
    for k in range(1, g.D):
        conditions(k).wait()
    call_all[...] = cx[...]


def split_heads(g, wide):
    return [wide[r * g.hw + h * g.hd : r * g.hw + (h + 1) * g.hd] for r in range(3) for h in range(g.lh)]


def attend_kernel(
    g, tokens, mod, gat, smc, wi, wix, wo, ob, we, wr,
    h1_out, qkv_out, lse, att, res, h2, gath, wof, wex, wrx,
    tok, h1, qkv, gsend, gbuf, wob, bias, send_w, recv_w, load, keep, save, send, recv, send_o, recv_o, send_f, recv_f,
):
    d, t, p, c = g.place()
    partner = (d, p * 2 + 1 - c)
    weights = (wi, wix)
    copy = pltpu.make_async_copy(tokens.at[pl.ds(pl.multiple_of(c * g.Rc, g.Rc), g.Rc)], tok, load)
    copy.start()
    meet([(d, flip(p, k, g.bits) * 2 + c) for k in range(1, g.G)] + [partner])

    def share(k):
        return remote(wo, wob.at[t], send_o.at[k], recv_o.at[k], (d, flip(p, k, g.bits) * 2 + c))

    def forward(k):
        row = flip(p, k, g.bits) * 2 + c
        src = wo if k == 0 else wob.at[row]
        return remote(src, wob.at[row], send_f.at[k], recv_f.at[k], partner)

    for k in range(1, g.G):
        share(k).start()
    forward(0).start()
    pair = [
        remote(src, dst, send_w.at[index], recv_w.at[index], partner)
        for index, (src, dst) in enumerate(((we, wex), (wr, wrx)))
    ]
    for weight in pair:
        weight.start()
    wob[t] = wo[...]
    copy.wait()
    scale = 1.0 / math.sqrt(g.hd)
    ones = jnp.ones((8, g.L), BF)
    for s in range(2):
        for r in range(2):
            line = jnp.where(
                lax.broadcasted_iota(jnp.int32, (8, g.hw), 0) == r + 1, smc[s, :, : g.hw], 0.0
            )
            bias[s, r] = tn(line.astype(BF), ones)

    def chunk(j):
        i, u = j // g.sub, lax.rem(j, g.sub)
        src = gsend.at[i] if g.sub == 1 else gsend.at[i, :, :, pl.ds(pl.multiple_of(u * g.Ro, g.Ro), g.Ro)]
        return src, gbuf.at[pl.ds(p * 2, 2)]

    def away(j):
        src, dst = chunk(j)
        return remote(src, dst, send.at[j], recv.at[p], (d, j * 2 + c))

    def arrive(j):
        src, _ = chunk(j)
        dst = gbuf.at[pl.ds(j * 2, 2)]
        return remote(src, dst, send.at[j], recv.at[j], (d, j * 2 + c))

    def home():
        src, dst = chunk(p)
        return pltpu.make_async_copy(src, dst, keep)

    def item(ii, carry):
        i = flip(p // g.sub, g.Ic - 1 - ii, g.bits)
        rows = pl.ds(pl.multiple_of(i * g.L, g.L), g.L)
        row = c * g.Ic + i

        @pl.when(ii == g.Ic - 1)
        def _():
            for k in range(1, g.G):
                share(k).wait_recv()
                forward(k).start()

        normed, _ = norm(tok[rows].astype(F32))
        hidden = (
            normed * (1.0 + mod[1, pl.ds(row, 1), :]) + mod[0, pl.ds(row, 1), :]
        ).astype(BF)
        h1[rows] = hidden
        for s in range(2):
            wide = nt(weights[s][...], hidden)
            core = c + s - 2 * c * s
            parts = split_heads(g, wide)
            for h in range(g.lh):
                hh = s * g.lh + h
                rows_h = slice(h * g.hd, (h + 1) * g.hd)
                q = (parts[h] + bias[s, 0, rows_h]).astype(BF)
                k = parts[g.lh + h].astype(BF)
                v = (parts[2 * g.lh + h] + bias[s, 1, rows_h]).astype(BF)
                qkv[hh * 3 + 0, :, rows] = q
                qkv[hh * 3 + 1, :, rows] = k
                qkv[hh * 3 + 2, :, rows] = v
                scores = tn(k, q) * scale
                peak = jnp.max(scores, axis=0, keepdims=True)
                powers = jnp.exp(scores - peak)
                total = jnp.sum(powers, axis=0, keepdims=True)
                lse[hh : hh + 1, rows] = peak + jnp.log(total)
                probs = (powers * (1.0 / total)).astype(BF)
                mixed = nn(v, probs)
                gate = gat[s, pl.ds(row, 1), 2 * h : 2 * h + 1]
                gsend[i, core, rows_h, :] = (mixed * gate).astype(BF)
        for u in range(g.sub):
            j = i * g.sub + u

            @pl.when(j == p)
            def _():
                home().start()

            @pl.when(j != p)
            def _():
                away(j).start()

        return carry

    lax.fori_loop(0, g.Ic, item, 0)
    saves = [pltpu.make_async_copy(h1, h1_out, save.at[0]), pltpu.make_async_copy(qkv, qkv_out, save.at[1])]
    for copy in saves:
        copy.start()
    home().wait()
    for k in range(1, g.G):
        arrive(flip(p, k, g.bits)).wait_recv()
    heads = gbuf[...].reshape(g.T * g.hw, g.Ro)
    gath[...] = heads
    for k in range(g.G):
        forward(k).wait_recv()
    saves.append(pltpu.make_async_copy(wob, wof, save.at[2]))
    saves[-1].start()
    full = wob[...].reshape(g.T * g.hw, g.W)
    attention = tn(heads, full) + ob[...].astype(F32).reshape(1, g.W)
    own = c * g.Ic + p // g.sub
    base = tok[pl.ds(pl.multiple_of(p * g.Ro, g.Ro), g.Ro)].astype(F32)
    residual = base + mod[2, pl.ds(own, 1), :] * attention
    att[...] = attention
    res[...] = residual
    normed, _ = norm(residual)
    h2[...] = (normed * (1.0 + mod[4, pl.ds(own, 1), :]) + mod[3, pl.ds(own, 1), :]).astype(BF)
    for k in range(1, g.G):
        away(flip(p, k, g.bits)).wait_send()
        share(k).wait_send()
    for k in range(g.G):
        forward(k).wait_send()
    for copy in saves:
        copy.wait()
    for copy in pair:
        copy.wait()


def feed_kernel(
    g, h2, cotangent, mod, gat, smc, we_in, wex_in, wr_in, wrx_in,
    grad_out, mpart_out, dwf_out, small, gates, ebs,
    cot, we, wex, wr, wrx, h2buf, bgbuf, gch, egb, sgb, own_g, xs, xr, mpart, dwf,
    joint, final, send_g, recv_g, leg_box, leg_sems, done, load, save, send_h, recv_h, send_p, recv_p,
):
    d, t, p, c = g.place()
    partner = (d, p * 2 + 1 - c)
    wec = (we, wex)
    wrc = (wr, wrx)

    def chip(k):
        return (d, flip(p, k, g.bits) * 2 + c)

    cot_rows = cotangent.at[pl.ds(pl.multiple_of(c * g.Rc, g.Rc), g.Rc)]
    loads = [
        pltpu.make_async_copy(src, dst, load.at[index])
        for index, (src, dst) in enumerate(
            ((cot_rows, cot), (wr_in, wr), (wrx_in, wrx), (we_in, we), (wex_in, wex))
        )
    ]
    for copy in loads:
        copy.start()
    leg = FirstLeg(g, g.fe, dwf, leg_box, leg_sems)
    meet([chip(k) for k in range(1, g.G)] + [partner, leg.other])

    spread = PlaneGather(g, h2, lambda k, source: h2buf.at[k], send_h, recv_h, chip, p)
    spread.start()
    back = PlaneScatter(g, lambda k: sgb.at[k - 1], joint, final, send_g, recv_g, chip)
    h2buf[0] = h2[...]
    for copy in loads:
        copy.wait()
    lane = lax.broadcasted_iota(jnp.int32, (1, g.ch), 1)
    tile_row = lax.broadcasted_iota(jnp.int32, (8, 128), 0)
    tile_lane = lax.broadcasted_iota(jnp.int32, (8, 128), 1)
    ebs[...] = jnp.zeros_like(ebs)
    gates[...] = jnp.zeros_like(gates)

    def block(k, carry):
        j = flip(p, k, g.bits)
        local = j // g.sub
        item = c * g.Ic + local
        rows = pl.ds(pl.multiple_of(j * g.Ro, g.Ro), g.Ro)
        here = pl.ds(pl.multiple_of(k * g.Ro, g.Ro), g.Ro)
        branch = (mod[5, pl.ds(item, 1), :] * cot[rows].astype(F32)).astype(BF)
        bgbuf[here] = branch
        grads = [nt(branch, wrc[s][...]) for s in range(2)]

        @pl.when(k == 1)
        def _():
            spread.relay()

        for kk in range(1, g.G):

            @pl.when(k == kk)
            def _():
                spread.wait(kk)

        hidden = h2buf[k]
        total = None
        for s in range(2):
            wide = nt(hidden, wec[s][...]) + smc[s, 0:1, : g.ch]
            inner = GELU_A * (wide + GELU_B * wide * wide * wide)
            tanh = jnp.tanh(inner)
            act = 0.5 * wide * (1.0 + tanh)
            slope = 0.5 * (1.0 + tanh) + 0.5 * wide * (1.0 - tanh * tanh) * (
                GELU_A * (1.0 + 3.0 * GELU_B * wide * wide)
            )
            gate = gat[s, pl.ds(item, 1), 1:2]
            for h in range(1, g.lh):
                gate = jnp.where(lane >= h * g.gc, gat[s, pl.ds(item, 1), 2 * h + 1 : 2 * h + 2], gate)
            gch[s, here] = (act * gate).astype(BF)
            line = jnp.sum(grads[s] * act, axis=0, keepdims=True)
            tile = gates[s]
            for h in range(g.lh):
                inside = jnp.where((lane >= h * g.gc) & (lane < (h + 1) * g.gc), line, 0.0)
                value = jnp.sum(inside, axis=1, keepdims=True)
                tile = tile + jnp.where((tile_row == local) & (tile_lane == 2 * h + 1), value, 0.0)
            gates[s] = tile
            egrad = (grads[s] * gate * slope).astype(BF)
            egb[s, here] = egrad
            ebs[s, 0:1, : g.ch] += jnp.sum(egrad.astype(F32), axis=0, keepdims=True)
            part = nn(egrad, wec[s][...])
            total = part if total is None else total + part

        @pl.when(k > 0)
        def _():
            sgb[k - 1] = total.astype(BF)
            back.put(k)

        @pl.when(k == 0)
        def _():
            own_g[...] = total

        return carry

    lax.fori_loop(0, g.G, block, 0)
    def swap(index):
        return remote(xs.at[index], xr.at[index], send_p.at[index], recv_p.at[index], partner)

    half_units = g.units // 2
    saves = []
    for index, left in enumerate((gch, egb)):
        right = bgbuf[...] if index == 0 else h2buf[...].reshape(g.Rc, g.W)
        xs[index] = tn(left[1], right).astype(BF)
        swap(index).start()
        value = tn(left[0], right)
        swap(index).wait_recv()
        value = (value + xr[index].astype(F32)).astype(BF)
        for u in range(half_units):
            dwf[index * half_units + u] = value[u * g.fr : (u + 1) * g.fr]
        if index == 0:
            leg.start()
            back.join()
    copy = pltpu.make_async_copy(dwf.at[pl.ds(g.fe, g.units - g.fe)], dwf_out.at[pl.ds(g.fe, g.units - g.fe)], save.at[0])
    copy.start()
    saves.append(copy)
    for k in range(g.G):
        rows = pl.ds(k * g.Ro, g.Ro)
        mpart[k] = (nn(gch[0, rows], wr[...]) + nn(gch[1, rows], wrx[...])).astype(BF)
    saves.append(pltpu.make_async_copy(mpart, mpart_out, save.at[2]))
    saves[-1].start()
    small[...] = jnp.zeros_like(small)
    small[7:8, :] = jnp.sum(bgbuf[0 : g.Ro].astype(F32), axis=0, keepdims=True)
    grad_out[...] = back.total(own_g[...])
    leg.add()
    copy = pltpu.make_async_copy(dwf.at[pl.ds(0, g.fe)], dwf_out.at[pl.ds(0, g.fe)], save.at[1])
    copy.start()
    saves.append(copy)
    leg.sent()

    @pl.when(leg.middle == 1)
    def _():
        pl.semaphore_signal(done, inc=1, device_id=leg.other, device_id_type=MESH)

    @pl.when(leg.middle == 0)
    def _():
        pl.semaphore_wait(done, 1)

    spread.sent()
    back.sent()
    swap(0).wait_send()
    swap(1).wait_send()
    for copy in saves:
        copy.wait()


def unattend_kernel(
    g, hgrad, h1_in, qkv_in, lse, gat, wi_in, wix_in, small_in, mpart_in, dwf, mod, att, res, wof_in, gath_in,
    cotangent, rbias, ebs, gates_in,
    grad, rgrad, bout, dwz, dwf_out, lines, sums, pay, gates,
    h1, qkv, wi, wix, mpart, wof, gath,
    hgs, hgbuf, wof_x, orr, osum, small, dqkv, acc, own_g, sgb, xs, xr, orv, sx, cot,
    work, first_z, second_z, more_z, sems_z, leg_box, leg_sems, joint_g, final_g, send_g, recv_g, joint_m, final_m, send_m, recv_m,
    send_o, recv_o, send_s, recv_s, send_p, recv_p, send_a, recv_a, send_x, recv_x,
    load,
):
    d, t, p, c = g.place()
    partner = (d, p * 2 + 1 - c)
    weights = (wi, wix)
    block = c * g.G + p

    def chip(k):
        return (d, flip(p, k, g.bits) * 2 + c)

    def peer(k):
        return (d, flip(t, k, g.tbits))

    def group(k):
        return (flip(d, k, g.dbits), t)

    fetch = pltpu.make_async_copy(
        cotangent.at[pl.ds(pl.multiple_of(block * g.Ro, g.Ro), g.Ro)], cot, load.at[0]
    )
    fetch.start()
    half = pltpu.make_async_copy(dwf, work, load.at[1])
    half.start()
    loads = [
        pltpu.make_async_copy(src, dst, load.at[2 + index])
        for index, (src, dst) in enumerate(
            (
                (wof_in, wof), (mpart_in, mpart), (gath_in, gath), (h1_in, h1), (qkv_in, qkv), (wi_in, wi),
                (wix_in, wix),
            )
        )
    ]
    for copy in loads:
        copy.start()
    zsum = GroupSum(g, g.units, work, first_z, second_z, more_z, dwf_out, sems_z)
    meet_line(g, [peer(k) for k in range(1, g.T)], group, zsum.middle)

    def rest(k):
        return remote(osum.at[flip(p, k, g.bits)], orv.at[k - 1], send_o.at[k], recv_o.at[k], chip(k))

    on = PlaneScatter(g, lambda k: mpart.at[k], joint_m, final_m, send_m, recv_m, chip)
    back = PlaneScatter(g, lambda k: sgb.at[k - 1], joint_g, final_g, send_g, recv_g, chip)

    def sumup(k):
        return remote(small, sx.at[k], send_s.at[k], recv_s.at[k], peer(k))

    def heads_out(k):
        return remote(hgs.at[pl.ds(flip(p, k, g.bits) * 2, 2)], hgbuf.at[k], send_a.at[k], recv_a.at[k], chip(k))

    def cross(q):
        return remote(wof_x.at[2 * q + 1 - c], orr.at[q], send_x.at[q], recv_x.at[q], partner)

    half.wait()
    everything = list(range(g.units))
    zsum.resume(everything[: g.fe])
    zsum.start(everything[g.fe :])
    leg = FirstLeg(g, g.ze, dwz, leg_box, leg_sems)
    fetch.wait()
    value = hgrad[...]
    own = c * g.Ic + p // g.sub
    normed, inverse = norm(res[...])
    cot_own = cot[...].astype(F32)
    residual = cot_own + norm_back(value * (1.0 + mod[4, pl.ds(own, 1), :]), normed, inverse)
    branch_one = (mod[2, pl.ds(own, 1), :] * residual).astype(BF)
    loads[0].wait()
    hgs[...] = nt(wof[...], branch_one).astype(BF).reshape(g.T, g.hw, g.Ro)
    for k in reversed(range(1, g.G)):
        heads_out(k).start()
    hgbuf[0] = hgs[pl.ds(p * 2, 2)]
    loads[1].wait()
    for k in reversed(range(1, g.G)):
        on.put(k)
    rgrad[...] = residual
    small[...] = small_in[...]
    small[2:3, :] = jnp.sum(residual * att[...], axis=0, keepdims=True)
    small[3:4, :] = jnp.sum(value, axis=0, keepdims=True)
    small[4:5, :] = jnp.sum(value * normed, axis=0, keepdims=True)
    small[6:7, :] = jnp.sum(branch_one.astype(F32), axis=0, keepdims=True)
    for k in range(1, g.T):
        sumup(k).start()
    for copy in loads[2:]:
        copy.wait()
    wof_x[...] = nn(gath[...], branch_one).astype(BF).reshape(g.T, g.hw, g.W)
    for q in range(g.G):
        cross(q).start()
    scale = 1.0 / math.sqrt(g.hd)
    acc[...] = jnp.zeros_like(acc)
    ones = jnp.ones((8, g.L), BF)
    tile_row = lax.broadcasted_iota(jnp.int32, (8, 128), 0)
    tile_lane = lax.broadcasted_iota(jnp.int32, (8, 128), 1)
    gates[...] = gates_in[...]
    pay[...] = ebs[...]

    def item(ii, carry):
        kk = lax.rem(g.Ic - ii, g.Ic)
        i = flip(p // g.sub, kk, g.bits)
        row = c * g.Ic + i
        rows = pl.ds(pl.multiple_of(i * g.L, g.L), g.L)
        slots = [kk * g.sub + (flip(lax.rem(p, g.sub), u, 4) if g.sub > 1 else 0) for u in range(g.sub)]
        hidden = h1[rows]
        total = None
        for u, slot in enumerate(slots):

            @pl.when(slot != 0)
            def _():
                heads_out(slot).wait_recv()

        @pl.when(ii == min(2, g.Ic - 1))
        def _():
            zsum.settle([1])
            zsum.join([3])

        @pl.when(ii == 1)
        def _():
            zsum.settle([0])
            zsum.join([2])
            for q in range(g.G):
                cross(q).wait()
                osum[q] = (wof_x[2 * q + c].astype(F32) + orr[q].astype(F32)).astype(BF)
            for k in range(1, g.G):
                rest(k).start()

        @pl.when(ii == g.Ic - 1)
        def _():
            on.join()

        for s in range(2):
            core = c + s - 2 * c * s
            tile = gates[s]
            for h in range(g.lh):
                hh = s * g.lh + h
                q = qkv[hh * 3 + 0, :, rows]
                k = qkv[hh * 3 + 1, :, rows]
                v = qkv[hh * 3 + 2, :, rows]
                pieces = [hgbuf[slot, core, h * g.hd : (h + 1) * g.hd, :] for slot in slots]
                heads = (pieces[0] if g.sub == 1 else jnp.concatenate(pieces, axis=1)).astype(F32)
                probs = jnp.exp(tn(k, q) * scale - lse[hh : hh + 1, rows])
                low = probs.astype(BF)
                mixed = nn(v, low)
                value = jnp.sum(jnp.sum(heads * mixed, axis=0, keepdims=True), axis=1, keepdims=True)
                tile = tile + jnp.where((tile_row == i) & (tile_lane == 2 * h), value, 0.0)
                mixed_grad = (gat[s, pl.ds(row, 1), 2 * h : 2 * h + 1] * heads).astype(BF)
                probs_grad = tn(v, mixed_grad)
                values_grad = nt(mixed_grad, low)
                score = (
                    probs * (probs_grad - jnp.sum(probs_grad * probs, axis=0, keepdims=True))
                ).astype(BF)
                queries_grad = nn(k, score) * scale
                keys_grad = nt(q, score) * scale
                for r, value in enumerate((queries_grad, keys_grad, values_grad)):
                    dqkv[s, r * g.hw + h * g.hd : r * g.hw + (h + 1) * g.hd, :] = value.astype(BF)
            gates[s] = tile
            wide = dqkv[s]
            part = tn(wide, weights[s][...])
            total = part if total is None else total + part
            acc[s] += nn(wide, hidden)
            pay[s, 1:2, : 3 * g.hw] += nt(ones, wide)[0:1]
        for u, slot in enumerate(slots):
            piece = total[u * g.Ro : (u + 1) * g.Ro]

            @pl.when(slot == 0)
            def _():
                own_g[...] = piece

            @pl.when(slot != 0)
            def _():
                sgb[slot - 1] = piece.astype(BF)
                back.put(slot)

        return carry

    lax.fori_loop(0, g.Ic, item, 0)
    xs[...] = acc[1].astype(BF)
    swap = remote(xs, xr, send_p, recv_p, partner)
    swap.start()
    zsum.settle([2])
    zsum.join([4])
    swap.wait()
    for u in range(g.units):
        low = u * g.zr
        if low < 3 * g.hw:
            span = slice(low, low + g.zr)
            dwz[u] = (acc[0, span] + xr[span].astype(F32)).astype(BF)
    leg.start()
    zsum.settle([3])
    zsum.join([5])
    zsum.settle([4])
    zsum.join([6])
    back.join()
    zsum.settle([5])
    zsum.join([7])
    value = small[...]
    for k in range(1, g.T):
        sumup(k).wait()
        value = value + sx[k]
    sums[...] = value
    out = osum[p].astype(F32)
    for k in range(1, g.G):
        rest(k).wait()
        out = out + orv[k - 1].astype(F32)
    for u in range(g.units):
        low = u * g.zr
        if low >= 3 * g.hw:
            dwz[u] = out[low - 3 * g.hw : low - 3 * g.hw + g.zr].astype(BF)
    zsum.settle([6])
    branch = on.total(mpart[0].astype(F32)) + rbias[...].astype(F32).reshape(1, g.W)
    bout[...] = (res[...] + mod[5, pl.ds(own, 1), :] * branch).astype(BF)
    lines[...] = small[...]
    lines[5:6, :] = jnp.sum(cot[...].astype(F32) * branch, axis=0, keepdims=True)
    grad[...] = back.total(own_g[...])
    on.sent()
    back.sent()
    zsum.settle([7])
    leg.add()
    zsum.end(everything, everything[g.fe :])
    leg.sent()
    for k in range(1, g.G):
        heads_out(k).wait_send()


def finish_kernel(
    g, grad, rgrad, tokens, mod, lines_in, sums, bout, pay, gates, dsg, dwz,
    tall, ball, colall, zall, logall, dwz_out,
    tok, tsend, stage, cbuf, zbuf, lbuf, pbuf, gbuf, work, first_z, second_z, more_z, sems_z,
    load, send_t, recv_t, send_f, recv_f, send_c, recv_c, send_p, recv_p, send_s, recv_s, keep,
):
    d, t, p, c = g.place()
    partner = (d, p * 2 + 1 - c)

    def chip(k):
        return (d, flip(p, k, g.bits) * 2 + c)

    def peer(k):
        return (d, flip(t, k, g.tbits))

    def group(k):
        return (flip(d, k, g.dbits), t)

    meet([peer(k) for k in range(1, g.T)] + [group(k) for k in range(1, g.D)])
    block = c * g.G + p
    mine = pl.ds(pl.multiple_of(block * g.Ro, g.Ro), g.Ro)
    copy = pltpu.make_async_copy(tokens.at[mine], tok, load)
    copy.start()
    swaps = [
        remote(pay.at[1], pbuf, send_p.at[0], recv_p.at[0], partner),
        remote(gates.at[1], gbuf, send_p.at[1], recv_p.at[1], partner),
    ]
    for swap in swaps:
        swap.start()
    zsum = GroupSum(g, g.units, work, first_z, second_z, more_z, dwz_out, sems_z)
    everything = list(range(g.units))
    work[...] = dwz[...]
    zsum.resume(everything[: g.ze])
    zsum.start(everything[g.ze :])

    def rows_of(dst):
        return lambda k, source: dst.at[pl.ds(pl.multiple_of((c * g.G + source) * g.Ro, g.Ro), g.Ro)]

    outs = PlaneGather(g, bout, rows_of(ball), send_t.at[0], recv_t.at[0], chip, p)
    grads = PlaneGather(g, tsend, rows_of(tall), send_t.at[1], recv_t.at[1], chip, p)
    outs.start()
    copy.wait()
    own = c * g.Ic + p // g.sub
    normed, inverse = norm(tok[...].astype(F32))
    value = grad[...]
    scaled = value * (1.0 + mod[1, pl.ds(own, 1), :])
    tsend[...] = (rgrad[...] + norm_back(scaled, normed, inverse)).astype(BF)
    lines = lines_in[...]
    kind = lax.broadcasted_iota(jnp.int32, lines.shape, 0)
    first = jnp.sum(value, axis=0, keepdims=True)
    second = jnp.sum(value * normed, axis=0, keepdims=True)
    lines = jnp.where(kind == 0, first, jnp.where(kind == 1, second, lines))
    w = g.mw
    stage[...] = jnp.zeros_like(stage)
    for member in range(g.T):
        stage[member, :, :w] = lines[:, member * w : (member + 1) * w]

    def columns(k):
        return remote(stage.at[flip(t, k, g.tbits)], cbuf.at[d, t], send_c.at[k], recv_c.at[k], peer(k))

    def column_in(k):
        return remote(stage.at[t], cbuf.at[d, flip(t, k, g.tbits)], send_c.at[k], recv_c.at[k], peer(k))

    for k in range(1, g.T):
        columns(k).start()
    cbuf[d, t] = stage[t]
    grads.start()
    local = [
        pltpu.make_async_copy(bout, ball.at[mine], keep.at[0]),
        pltpu.make_async_copy(tsend, tall.at[mine], keep.at[1]),
    ]
    for item in local:
        item.start()

    def forward(which, dst, k):
        rows = pl.ds(pl.multiple_of((c * g.G + flip(p, k, g.bits)) * g.Ro, g.Ro), g.Ro)
        return remote(dst.at[rows], dst.at[rows], send_f.at[which, k], recv_f.at[which, k], partner)

    def arrive_forward(which, dst, k):
        rows = pl.ds(pl.multiple_of(((1 - c) * g.G + flip(p, k, g.bits)) * g.Ro, g.Ro), g.Ro)
        return remote(dst.at[rows], dst.at[rows], send_f.at[which, k], recv_f.at[which, k], partner)

    outs.relay()
    zsum.join([4])
    zsum.settle([0, 1])
    for swap in swaps:
        swap.wait()
    zbuf[d] = jnp.zeros((8, g.W), F32)
    zbuf[d, 0:2] = pay[0, 0:2] + pbuf[0:2]
    zbuf[d, 2:4] = sums[6:8]
    both = jnp.concatenate([gates[0, : g.Ic], gbuf[: g.Ic]], axis=0)
    turned = jnp.concatenate([gbuf[: g.Ic], gates[0, : g.Ic]], axis=0)
    lbuf[d] = jnp.where(c == 0, both, turned) * dsg[...]
    zsum.join([5, 6])
    zsum.settle([2])
    for k in range(1, g.T):
        columns(k).wait_send()
        column_in(k).wait_recv()

    def share(k):
        return [
            remote(cbuf.at[d], cbuf.at[d], send_s.at[0, k], recv_s.at[0, k], group(k)),
            remote(zbuf.at[d], zbuf.at[d], send_s.at[1, k], recv_s.at[1, k], group(k)),
            remote(lbuf.at[d], lbuf.at[d], send_s.at[2, k], recv_s.at[2, k], group(k)),
        ]

    def shared(k):
        other = flip(d, k, g.dbits)
        return [
            remote(cbuf.at[other], cbuf.at[other], send_s.at[0, k], recv_s.at[0, k], group(k)),
            remote(zbuf.at[other], zbuf.at[other], send_s.at[1, k], recv_s.at[1, k], group(k)),
            remote(lbuf.at[other], lbuf.at[other], send_s.at[2, k], recv_s.at[2, k], group(k)),
        ]

    for k in range(1, g.D):
        for item in share(k):
            item.start()
    for which, dst in ((0, ball), (1, tall)):
        local[which].wait()
        forward(which, dst, 0).start()
    zsum.join([7])
    zsum.settle([3, 4])
    grads.relay()
    zsum.settle([5, 6, 7])
    for k in range(1, g.G):
        outs.wait(k)
        forward(0, ball, k).start()
    for k in range(1, g.D):
        for item in share(k):
            item.wait_send()
        for item in shared(k):
            item.wait_recv()
    colall[...] = cbuf[...]
    zall[...] = zbuf[...]
    logall[...] = lbuf[...]
    for k in range(1, g.G):
        grads.wait(k)
        forward(1, tall, k).start()
    zsum.end(everything, everything[g.ze :])
    outs.sent()
    grads.sent()
    for which, dst in ((0, ball), (1, tall)):
        for k in range(g.G):
            forward(which, dst, k).wait_send()
            arrive_forward(which, dst, k).wait_recv()


def wrap_kernel(
    g, ball, tall, dwf, dwz, colall, zall, logall, conds,
    out, tokens_grad, dwr, dwe, dwi, dwo, dwm, dmb, drw, drb, dib, deb, dob, drb_all,
    twice,
):
    step = pl.program_id(0)
    out[...] = ball[...].astype(F32)
    tokens_grad[...] = tall[...].astype(F32)
    half_units = g.units // 2
    heads = 3 * g.units // 4

    @pl.when(step < half_units)
    def _():
        dwr[...] = dwf[...].astype(F32)

    @pl.when(step >= half_units)
    def _():
        dwe[...] = dwf[...].astype(F32)

    @pl.when(step < heads)
    def _():
        dwi[...] = dwz[...].astype(F32)

    @pl.when(step >= heads)
    def _():
        dwo[...] = dwz[...].astype(F32)

    w = g.mw

    @pl.when(step == 0)
    def _():
        rows = []
        for member in range(g.T):
            rows.append(((member % 2) * g.G + member // 2) * g.Ro // g.L)
        value = conds[...]
        silu = value / (1.0 + jnp.exp(-value))
        picked = jnp.concatenate([silu[z, i : i + 1] for z in range(g.D) for i in rows], axis=0).astype(BF)
        twice[...] = jnp.concatenate([picked, picked], axis=0)
        logits = jnp.concatenate([logall[z] for z in range(g.D)], axis=0)
        high = logits.astype(BF)
        low = (logits - high.astype(F32)).astype(BF)
        flat = jnp.concatenate([value[z] for z in range(g.D)], axis=0).astype(BF)
        router = tn(jnp.concatenate([high, low], axis=0), jnp.concatenate([flat, flat], axis=0))
        sums = jnp.sum(logits, axis=0, keepdims=True)
        for h in range(g.lh):
            drw[h] = router[2 * h : 2 * h + 2, :]
            drb[h : h + 1, :] = sums[:, 2 * h : 2 * h + 2]
        total = zall[0]
        for z in range(1, g.D):
            total = total + zall[z]
        dib[0:1, :] = total[1:2, : g.hw]
        dib[1:2, :] = total[1:2, 2 * g.hw : 3 * g.hw]
        deb[...] = total[0, : g.ch]
        dob[...] = total[2]
        drb_all[...] = total[3]

    @pl.when(step < 6)
    def _():
        part = jnp.concatenate(
            [colall[z, member, pl.ds(step, 1), :] for z in range(g.D) for member in range(g.T)], axis=0
        )
        dmb[pl.ds(step, 1), :] = jnp.sum(part, axis=0, keepdims=True)[:, :w]
        high = part.astype(BF)
        low = (part - high.astype(F32)).astype(BF)
        dwm[...] = tn(jnp.concatenate([high, low], axis=0), twice[...])[:w]


def wrap(g, ball, tall, dwf, dwz, colall, zall, logall, conds):
    n, W = g.units, g.W
    half_units, heads = n // 2, 3 * n // 4
    rows = g.R // n

    def whole(shape):
        return pl.BlockSpec(shape, lambda i: (0,) * len(shape))

    def part(shape, low, count):
        return pl.BlockSpec(shape, lambda i: (jnp.clip(i - low, 0, count - 1),) + (0,) * (len(shape) - 1))

    outs = [
        ((g.R, W), part((rows, W), 0, n)), ((g.R, W), part((rows, W), 0, n)),
        ((half_units, g.fr, W), part((1, g.fr, W), 0, half_units)),
        ((half_units, g.fr, W), part((1, g.fr, W), half_units, half_units)),
        ((heads, g.zr, W), part((1, g.zr, W), 0, heads)), ((n - heads, g.zr, W), part((1, g.zr, W), heads, n - heads)),
        ((6 * g.mw, W), part((g.mw, W), 0, 6)), ((6, g.mw), whole((6, g.mw))), ((g.lh, 2, W), whole((g.lh, 2, W))),
        ((g.lh, 2), whole((g.lh, 2))), ((2, g.hw), whole((2, g.hw))), ((g.ch,), whole((g.ch,))), ((W,), whole((W,))),
        ((W,), whole((W,))),
    ]
    return pl.pallas_call(
        functools.partial(wrap_kernel, g),
        name="wrap",
        grid=(n,),
        out_shape=[jax.ShapeDtypeStruct(s, F32) for s, _ in outs],
        in_specs=[
            part((rows, W), 0, n), part((rows, W), 0, n), part((1, g.fr, W), 0, n), part((1, g.zr, W), 0, n),
            whole(colall.shape), whole(zall.shape), whole(logall.shape), whole(conds.shape),
        ],
        out_specs=[spec for _, spec in outs],
        scratch_shapes=[pltpu.VMEM((2 * g.D * g.T, W), BF)],
        cost_estimate=pl.CostEstimate(flops=10**9, bytes_accessed=4 * 10**7, transcendentals=0),
        compiler_params=pltpu.CompilerParams(vmem_limit_bytes=VMEM_LIMIT),
    )(ball, tall, dwf, dwz, colall, zall, logall, conds)


def body(
    groups, members,
    tokens, condition, timesteps, route_masks, modulate_weight, modulate_bias, input_weight, input_bias,
    output_weight, output_bias, expand_weight, expand_bias, reduce_weight, reduce_bias, router_weight, router_bias,
    out_cotangent,
):
    g = Plan(
        groups, members, tokens.shape[0], condition.shape[0], tokens.shape[1], router_weight.shape[1],
        modulate_weight.shape[2], input_weight.shape[2], expand_weight.shape[1],
    )
    dma = pltpu.SemaphoreType.DMA
    V = pltpu.VMEM
    W, T, G, D, I = g.W, g.T, g.G, g.D, g.I
    wide = 2 * g.lh
    wm = jnp.transpose(modulate_weight, (1, 2, 0)).reshape(6 * g.mw, W)
    wi = jnp.transpose(input_weight, (1, 2, 0)).reshape(3 * g.hw, W)
    we = expand_weight.T
    wr = reduce_weight
    rw = jnp.transpose(router_weight, (1, 2, 0))
    masks = jnp.transpose(route_masks, (1, 2, 0))
    eb, ob, rbias = expand_bias, output_bias, reduce_bias

    mod, gat, dsg, smc, conds, wix = call(
        functools.partial(start_kernel, g), "start",
        (condition, wm, modulate_bias, timesteps, masks, rw, router_bias, eb, input_bias, wi),
        "vvvsvvvvvh",
        [
            ((6, I, W), F32), ((2, I, 128), F32), ((I, 128), F32), ((2, 8, W), F32), ((D, I, W), F32),
            ((3 * g.hw, W), BF),
        ],
        "vvvvvh",
        [
            V((T, I, 6 * g.mw), F32), V((2, I, 128), F32), V((2, 8, W), F32), V((D, I, W), F32),
            dma((T,)), dma((T,)), dma((3,)), dma((3,)), dma((D,)), dma((D,)),
        ],
        1,
    )
    h1, qkv, lse, att, res, h2, gath, wof, wex, wrx = call(
        functools.partial(attend_kernel, g), "attend",
        (tokens, mod, gat, smc, wi, wix, output_weight, ob, we, wr), "hvvvvvvvhh",
        [
            ((g.Rc, W), BF), ((wide * 3, g.hd, g.Rc), BF), ((wide, g.Rc), F32),
            ((g.Ro, W), F32), ((g.Ro, W), F32), ((g.Ro, W), BF), ((T * g.hw, g.Ro), BF), ((T, g.hw, W), BF),
            ((g.ch, W), BF), ((g.ch, W), BF),
        ],
        "hhvvvvvhhh",
        [
            V((g.Rc, W), BF), V((g.Rc, W), BF), V((wide * 3, g.hd, g.Rc), BF), V((g.Ic, 2, g.hw, g.L), BF), V((T, g.hw, g.Ro), BF), V((T, g.hw, W), BF),
            V((2, 2, g.hw, g.L), F32), dma((2,)), dma((2,)), dma, dma, dma((3,)), dma((G,)), dma((G,)), dma((G,)), dma((G,)), dma((G,)), dma((G,)),
        ],
        2,
    )
    hgrad, mpart, dwf, small, gates, ebs = call(
        functools.partial(feed_kernel, g), "feed",
        (h2, out_cotangent, mod, gat, smc, we, wex, wr, wrx), "vhvvvhhhh",
        [
            ((g.Ro, W), F32), ((G, g.Ro, W), BF), ((g.units, g.fr, W), BF),
            ((8, W), F32), ((2, 8, 128), F32), ((2, 8, W), F32),
        ],
        "vhhvvv",
        [
            V((g.Rc, W), BF), V((g.ch, W), BF), V((g.ch, W), BF), V((g.ch, W), BF), V((g.ch, W), BF),
            V((G, g.Ro, W), BF), V((g.Rc, W), BF), V((2, g.Rc, g.ch), BF), V((2, g.Rc, g.ch), BF),
            V((G - 1, g.Ro, W), BF), V((g.Ro, W), F32),
            V((2, g.ch, W), BF), V((2, g.ch, W), BF), V((G, g.Ro, W), BF), V((g.units, g.fr, W), BF),
        ]
        + PlaneScatter.scratch(g)
        + FirstLeg.scratch(g, g.fe, g.fr)
        + [pltpu.SemaphoreType.REGULAR, dma((5,)), dma((3,)), dma((G, 2)), dma((G, 2)), dma((2,)), dma((2,))],
        3,
    )
    grad, rgrad, bout, dwz, dwf, lines, sums, pay, gates = call(
        functools.partial(unattend_kernel, g), "unattend",
        (
            hgrad, h1, qkv, lse, gat, wi, wix, small, mpart, dwf, mod, att, res,
            wof.reshape(T * g.hw, W), gath, out_cotangent, rbias, ebs, gates,
        ),
        "vhhvvhhvhhvvvhhhvvv",
        [
            ((g.Ro, W), F32), ((g.Ro, W), F32), ((g.Ro, W), BF), ((g.units, g.zr, W), BF),
            ((g.units, g.fr, W), BF), ((8, W), F32), ((8, W), F32), ((2, 8, W), F32), ((2, 8, 128), F32),
        ],
        "vvvvvvvvv",
        [
            V((g.Rc, W), BF), V((wide * 3, g.hd, g.Rc), BF), V((3 * g.hw, W), BF), V((3 * g.hw, W), BF),
            V((G, g.Ro, W), BF), V((T * g.hw, W), BF), V((T * g.hw, g.Ro), BF),
            V((T, g.hw, g.Ro), BF), V((G, 2, g.hw, g.Ro), BF), V((T, g.hw, W), BF), V((G, g.hw, W), BF),
            V((G, g.hw, W), BF), V((8, W), F32),
            V((2, 3 * g.hw, g.L), BF), V((2, 3 * g.hw, W), F32), V((g.Ro, W), F32), V((G - 1, g.Ro, W), BF),
            V((3 * g.hw, W), BF), V((3 * g.hw, W), BF),
            V((G - 1, g.hw, W), BF), V((T, 8, W), F32), V((g.Ro, W), BF),
        ]
        + GroupSum.scratch(g, g.units, g.fr)
        + FirstLeg.scratch(g, g.ze, g.zr)
        + PlaneScatter.scratch(g)
        + PlaneScatter.scratch(g)
        + [
            dma((G,)), dma((G,)), dma((T,)), dma((T,)), dma, dma,
            dma((G,)), dma((G,)), dma((G,)), dma((G,)), dma((9,)),
        ],
        4,
    )
    tall, ball, colall, zall, logall, dwz = call(
        functools.partial(finish_kernel, g), "finish",
        (grad, rgrad, tokens, mod, lines, sums, bout, pay, gates, dsg, dwz), "vvhvvvvvvvv",
        [
            ((g.R, W), BF), ((g.R, W), BF), ((D, T, 8, g.cw), F32), ((D, 8, W), F32), ((D, I, 128), F32),
            ((g.units, g.zr, W), BF),
        ],
        "hhvvvv",
        [
            V((g.Ro, W), BF), V((g.Ro, W), BF), V((T, 8, g.cw), F32), V((D, T, 8, g.cw), F32), V((D, 8, W), F32),
            V((D, I, 128), F32), V((8, W), F32), V((8, 128), F32),
        ]
        + GroupSum.scratch(g, g.units, g.zr)
        + [
            dma, dma((2, G, 2)), dma((2, G, 2)), dma((2, G)), dma((2, G)), dma((T,)), dma((T,)), dma((2,)), dma((2,)),
            dma((3, D)), dma((3, D)), dma((2,)),
        ],
        5,
    )
    out, tokens_grad, dwr, dwe, dwi, dwo, dwm, dmb, drw, drb, dib, deb, dob, drb_all = wrap(
        g, ball, tall, dwf, dwz, colall, zall, logall, conds
    )
    return (
        out,
        tokens_grad,
        jnp.transpose(dwm.reshape(6, g.mw, W), (2, 0, 1)),
        dmb,
        jnp.transpose(dwi.reshape(3, g.hw, W), (2, 0, 1)),
        dib,
        dwo.reshape(g.hw, W),
        dob,
        dwe.reshape(g.ch, W).T,
        deb,
        dwr.reshape(g.ch, W),
        drb_all,
        jnp.transpose(drw, (2, 0, 1)),
        drb,
    )


def solution(mesh):
    return jax.shard_map(
        functools.partial(body, mesh.shape["dp"], mesh.shape["tensor"]),
        mesh=mesh,
        in_specs=(
            P("dp", None), P("dp", None), P("dp"), P(None, "tensor", None), P(None, None, "tensor"),
            P(None, "tensor"), P(None, None, "tensor"), P(None, "tensor"), P("tensor", None), P(),
            P(None, "tensor"), P("tensor"), P("tensor", None), P(), P(None, "tensor", None), P("tensor", None),
            P("dp", None),
        ),
        out_specs=(
            P("dp", None), P("dp", None), P(None, None, "tensor"), P(None, "tensor"), P(None, None, "tensor"),
            P(None, "tensor"), P("tensor", None), P(), P(None, "tensor"), P("tensor"), P("tensor", None), P(),
            P(None, "tensor", None), P("tensor", None),
        ),
        check_vma=False,
    )
```

```python
import functools
import math

import jax
import jax.numpy as jnp
from jax import lax
from jax.experimental import pallas as pl
from jax.experimental.pallas import tpu as pltpu
from jax.sharding import PartitionSpec as P

BF = jnp.bfloat16
F32 = jnp.float32
MESH = pl.DeviceIdType.MESH
EPSILON = 1e-06
GELU_A = math.sqrt(2.0 / math.pi)
GELU_B = 0.044715
VMEM_LIMIT = 58 << 20


def nt(left, right):
    return lax.dot_general(left, right, (((1,), (1,)), ((), ())), preferred_element_type=F32)


def nn(left, right):
    return lax.dot_general(left, right, (((1,), (0,)), ((), ())), preferred_element_type=F32)


def tn(left, right):
    return lax.dot_general(left, right, (((0,), (0,)), ((), ())), preferred_element_type=F32)


def flip(value, mask, bits):
    total = 0
    for bit in range(bits):
        unit = 1 << bit
        total = total + lax.rem(value // unit + mask // unit, 2) * unit
    return total


def norm(values):
    center = values - jnp.mean(values, axis=-1, keepdims=True)
    inverse = lax.rsqrt(jnp.mean(center * center, axis=-1, keepdims=True) + EPSILON)
    return center * inverse, inverse


def norm_back(grad, normed, inverse):
    mean_grad = jnp.mean(grad, axis=-1, keepdims=True)
    mean_cross = jnp.mean(grad * normed, axis=-1, keepdims=True)
    return inverse * (grad - mean_grad - normed * mean_cross)


class Plan:
    def __init__(self, groups, members, rows, items, width, heads, modwidth, headwidth, channels):
        self.D = groups
        self.T = members
        self.G = members // 2
        self.bits = self.G.bit_length() - 1
        self.tbits = members.bit_length() - 1
        self.dbits = groups.bit_length() - 1
        self.R = rows
        self.I = items
        self.L = rows // items
        self.W = width
        self.Rc = rows // 2
        self.Ro = rows // members
        self.Ic = items // 2
        self.sub = self.L // self.Ro
        self.lh = heads
        self.mw = modwidth
        self.cw = -(-modwidth // 128) * 128
        self.hw = headwidth
        self.hd = headwidth // heads
        self.ch = channels
        self.gc = channels // heads
        self.hr = 2 * headwidth
        self.units = 8
        self.fr = 2 * channels // self.units
        self.zr = 4 * headwidth // self.units
        self.fe = 2
        self.ze = 4

    def place(self):
        d = lax.axis_index("dp")
        t = lax.axis_index("tensor")
        return d, t, t // 2, lax.rem(t, 2)


def greet(devices):
    barrier = pltpu.get_barrier_semaphore()
    for device in devices:
        pl.semaphore_signal(barrier, inc=1, device_id=device, device_id_type=MESH)
    return barrier


def meet(devices):
    pl.semaphore_wait(greet(devices), len(devices))


def meet_line(g, devices, group, middle):
    barrier = pltpu.get_barrier_semaphore()
    for device in devices + [group(1)]:
        pl.semaphore_signal(barrier, inc=1, device_id=device, device_id_type=MESH)
    others = [group(3)] + [group(4 << level) for level in range(g.dbits - 2)]

    @pl.when(middle == 1)
    def _():
        for device in others:
            pl.semaphore_signal(barrier, inc=1, device_id=device, device_id_type=MESH)
        pl.semaphore_wait(barrier, len(devices) + 1 + len(others))

    @pl.when(middle == 0)
    def _():
        pl.semaphore_wait(barrier, len(devices) + 1)


def remote(src, dst, send, recv, device):
    return pltpu.make_async_remote_copy(
        src_ref=src, dst_ref=dst, send_sem=send, recv_sem=recv, device_id=device, device_id_type=MESH
    )


class GroupSum:
    def __init__(self, g, count, work, first, second, more, full, sems):
        self.g, self.count, self.work, self.first, self.second = g, count, work, first, second
        self.more, self.full, self.sems = more, full, sems
        self.d, self.t = lax.axis_index("dp"), lax.axis_index("tensor")
        self.middle = lax.rem(lax.rem(self.d, 4) + 1, 4) // 2

    def device(self, mask):
        return (flip(self.d, mask, self.g.dbits), self.t)

    def copy(self, kind, src, dst, unit, mask):
        return remote(src.at[unit], dst.at[unit], self.sems.at[kind, unit], self.sems.at[kind + 1, unit], self.device(mask))

    def up(self, unit):
        return self.copy(0, self.work, self.first, unit, 1)

    def over(self, unit):
        return self.copy(2, self.work, self.second, unit, 3)

    def down(self, unit):
        return self.copy(4, self.full, self.full, unit, 1)

    def across(self, unit, level):
        src = self.more.at[2 * level, unit]
        dst = self.more.at[2 * level + 1, unit]
        kind = 6 + 2 * level
        return remote(src, dst, self.sems.at[kind, unit], self.sems.at[kind + 1, unit], self.device(4 << level))

    def start(self, units):
        @pl.when(self.middle == 0)
        def _():
            for unit in units:
                self.up(unit).start()

    def resume(self, units):
        @pl.when(self.middle == 1)
        def _():
            for unit in units:
                self.over(unit).start()

    def join(self, units):
        @pl.when(self.middle == 1)
        def _():
            for unit in units:
                self.up(unit).wait_recv()
                self.work[unit] = (self.work[unit].astype(F32) + self.first[unit].astype(F32)).astype(BF)
                self.over(unit).start()

    def settle(self, units):
        @pl.when(self.middle == 1)
        def _():
            for unit in units:
                self.over(unit).wait_recv()
                value = (self.work[unit].astype(F32) + self.second[unit].astype(F32)).astype(BF)
                for level in range(self.g.dbits - 2):
                    self.more[2 * level, unit] = value
                    copy = self.across(unit, level)
                    copy.start()
                    copy.wait()
                    value = (value.astype(F32) + self.more[2 * level + 1, unit].astype(F32)).astype(BF)
                self.full[unit] = value
                self.down(unit).start()

    def end(self, units, started):
        @pl.when(self.middle == 0)
        def _():
            for unit in started:
                self.up(unit).wait_send()
            for unit in units:
                self.down(unit).wait_recv()

        @pl.when(self.middle == 1)
        def _():
            for unit in units:
                self.over(unit).wait_send()
                self.down(unit).wait_send()

    @staticmethod
    def scratch(g, count, rows):
        levels = max(g.dbits - 2, 0)
        return [
            pltpu.VMEM((count, rows, g.W), BF), pltpu.VMEM((count, rows, g.W), BF), pltpu.VMEM((count, rows, g.W), BF),
            pltpu.VMEM((max(2 * levels, 1), count if levels else 1, rows if levels else 16, g.W), BF),
            pltpu.SemaphoreType.DMA((6 + 2 * levels, count)),
        ]


class FirstLeg:
    def __init__(self, g, units, work, inbox, sems):
        self.g, self.units, self.work, self.inbox, self.sems = g, units, work, inbox, sems
        d = lax.axis_index("dp")
        self.middle = lax.rem(lax.rem(d, 4) + 1, 4) // 2
        self.other = (flip(d, 1, g.dbits), lax.axis_index("tensor"))

    def copy(self, unit):
        return remote(self.work.at[unit], self.inbox.at[unit], self.sems.at[0, unit], self.sems.at[1, unit], self.other)

    def start(self):
        @pl.when(self.middle == 0)
        def _():
            for unit in range(self.units):
                self.copy(unit).start()

    def add(self):
        @pl.when(self.middle == 1)
        def _():
            for unit in range(self.units):
                self.copy(unit).wait_recv()
                self.work[unit] = (self.work[unit].astype(F32) + self.inbox[unit].astype(F32)).astype(BF)

    def sent(self):
        @pl.when(self.middle == 0)
        def _():
            for unit in range(self.units):
                self.copy(unit).wait_send()

    @staticmethod
    def scratch(g, units, rows):
        return [pltpu.VMEM((units, rows, g.W), BF), pltpu.SemaphoreType.DMA((2, units))]


def half(g, ref, which):
    return ref.at[pl.ds(which * (g.Ro // 2), g.Ro // 2)]


class PlaneGather:
    def __init__(self, g, src, place, send, recv, chip, p):
        self.g, self.src, self.place, self.send, self.recv, self.chip, self.p = g, src, place, send, recv, chip, p
        self.relayed = g.G == 4

    def source(self, k):
        return flip(self.p, k, self.g.bits)

    def own(self, k, h):
        g = self.g
        return remote(
            half(g, self.src, h), half(g, self.place(k, self.p), h), self.send.at[k, h], self.recv.at[k, h], self.chip(k)
        )

    def arrival(self, k, h):
        g = self.g
        place = half(g, self.place(k, self.source(k)), h)
        return remote(place, place, self.send.at[k, h], self.recv.at[k, h], self.chip(k))

    def onward(self, h):
        g = self.g
        k = 1 + h
        src = half(g, self.place(k, self.source(k)), h)
        dst = half(g, self.place(3, self.source(k)), h)
        return remote(src, dst, self.send.at[3, h], self.recv.at[3, h], self.chip(2 - h))

    def start(self):
        if self.relayed:
            for k, h in ((1, 0), (2, 1), (1, 1), (2, 0)):
                self.own(k, h).start()
        else:
            for k in range(1, self.g.G):
                for h in range(2):
                    self.own(k, h).start()

    def relay(self):
        if self.relayed:
            for h in range(2):
                self.arrival(1 + h, h).wait_recv()
                self.onward(h).start()

    def wait(self, k):
        for h in range(2):
            if not (self.relayed and k < 3 and h == k - 1):
                self.arrival(k, h).wait_recv()

    def sent(self):
        for h in range(2):
            for k in range(1, 3 if self.relayed else self.g.G):
                self.own(k, h).wait_send()
            if self.relayed:
                self.onward(h).wait_send()


class PlaneScatter:
    def __init__(self, g, part, joint, final, send, recv, chip):
        self.g, self.part, self.joint, self.final = g, part, joint, final
        self.send, self.recv, self.chip = send, recv, chip
        self.relayed = g.G == 4

    def far(self, h):
        return remote(
            half(self.g, self.part(3), h), self.joint.at[h], self.send.at[2, h], self.recv.at[2, h], self.chip(1 + h)
        )

    def near(self, k, h):
        g = self.g
        return remote(
            half(g, self.part(k), h), half(g, self.final.at[k - 1], h), self.send.at[k - 1, h], self.recv.at[k - 1, h],
            self.chip(k),
        )

    def put(self, k):
        if not self.relayed:
            for h in range(2):
                self.near(k, h).start()
        elif isinstance(k, int):
            if k == 3:
                self.far(0).start()
                self.far(1).start()
            else:
                self.near(k, k - 1).start()
        else:
            for kk in range(1, 4):

                @pl.when(k == kk)
                def _():
                    self.put(kk)

    def join(self):
        if self.relayed:
            for h in range(2):
                k = 2 - h
                self.far(h).wait_recv()
                rows = pl.ds(h * (self.g.Ro // 2), self.g.Ro // 2)
                ref = self.part(k)
                ref[rows] = (ref[rows].astype(F32) + self.joint[h].astype(F32)).astype(BF)
                self.near(k, h).start()

    def total(self, value):
        for k in range(1, 3 if self.relayed else self.g.G):
            for h in range(2):
                self.near(k, h).wait_recv()
            value = value + self.final[k - 1].astype(F32)
        return value

    def sent(self):
        for h in range(2):
            for k in range(1, 3 if self.relayed else self.g.G):
                self.near(k, h).wait_send()
            if self.relayed:
                self.far(h).wait_send()

    @staticmethod
    def scratch(g):
        dma = pltpu.SemaphoreType.DMA
        return [
            pltpu.VMEM((2, g.Ro // 2, g.W), BF), pltpu.VMEM((2 if g.G == 4 else g.G - 1, g.Ro, g.W), BF),
            dma((g.G, 2)), dma((g.G, 2)),
        ]


def call(kernel, name, inputs, in_spaces, outs, out_spaces, scratch, collective, cost=None):
    spec = {
        "v": pl.BlockSpec(memory_space=pltpu.VMEM),
        "h": pl.BlockSpec(memory_space=pl.ANY),
        "s": pl.BlockSpec(memory_space=pltpu.SMEM),
    }
    flops, moved = cost or (10**8, 10**7)
    return pl.pallas_call(
        kernel,
        name=name,
        out_shape=[jax.ShapeDtypeStruct(s, t) for s, t in outs],
        in_specs=[spec[x] for x in in_spaces],
        out_specs=[spec[x] for x in out_spaces],
        scratch_shapes=scratch,
        cost_estimate=pl.CostEstimate(flops=flops, bytes_accessed=moved, transcendentals=0),
        compiler_params=pltpu.CompilerParams(
            collective_id=collective, has_side_effects=collective is not None, vmem_limit_bytes=VMEM_LIMIT
        ),
    )(*inputs)


def start_kernel(
    g, cond, wm, mb, ts, masks, rw, rb, eb, ib, wi,
    mod, gat, dsg, smc, call_all, wix,
    mpart, gx, sx, cx, send_m, recv_m, send_w, recv_w, send_c, recv_c,
):
    d, t, p, c = g.place()
    partner = (d, p * 2 + 1 - c)
    devices = [(d, flip(t, k, g.tbits)) for k in range(1, g.T)]
    devices = devices + [(flip(d, k, g.dbits), t) for k in range(1, g.D)]
    barrier = greet(devices)
    value = cond[...]
    silu = (value / (1.0 + jnp.exp(-value))).astype(BF)
    part = nt(silu, wm[...])
    w = g.mw
    bias = mb[...].astype(F32)
    for row in range(6):
        mpart[t, :, row * w : (row + 1) * w] = part[:, row * w : (row + 1) * w] + bias[row : row + 1]

    pl.semaphore_wait(barrier, len(devices))
    pair = remote(wi, wix, send_w.at[2], recv_w.at[2], partner)

    def spread(k):
        return remote(
            mpart.at[t], mpart.at[t], send_m.at[k], recv_m.at[k], (d, flip(t, k, g.tbits))
        )

    for k in range(1, g.T):
        spread(k).start()
    pair.start()
    low = value.astype(BF)
    steps = masks.shape[2]
    row = lax.broadcasted_iota(jnp.int32, (g.I, steps), 0)
    wanted = jnp.zeros((g.I, steps), jnp.int32)
    for item in range(g.I):
        wanted = jnp.where(row == item, ts[item], wanted)
    hot = (wanted == lax.broadcasted_iota(jnp.int32, (g.I, steps), 1)).astype(F32).astype(BF)
    dsg[...] = jnp.zeros_like(dsg)
    gx[0] = jnp.zeros((g.I, 128), F32)
    scale = rb[...].astype(F32)
    for h in range(g.lh):
        logits = nt(low, rw[h]) + scale[h : h + 1]
        sigmoid = 1.0 / (1.0 + jnp.exp(-logits))
        mask = nt(hot, masks[h].astype(F32).astype(BF))
        dsg[:, 2 * h : 2 * h + 2] = mask * sigmoid * (1.0 - sigmoid)
        gx[0, :, 2 * h : 2 * h + 2] = mask * sigmoid
    sx[0] = jnp.zeros((8, g.W), F32)
    sx[0, 0:1, : g.ch] = eb[...].astype(F32).reshape(1, g.ch)
    sx[0, 1:3, : g.hw] = ib[...].astype(F32)
    small = [
        remote(gx.at[0], gx.at[1], send_w.at[0], recv_w.at[0], partner),
        remote(sx.at[0], sx.at[1], send_w.at[1], recv_w.at[1], partner),
    ]
    for copy in small:
        copy.start()

    def conditions(k):
        return remote(cond, cx.at[d], send_c.at[k], recv_c.at[k], (flip(d, k, g.dbits), t))

    for k in range(1, g.D):
        conditions(k).start()
    cx[d] = value
    for k in range(1, g.T):
        spread(k).wait()
    for member in range(g.T):
        for row in range(6):
            mod[row, :, member * w : (member + 1) * w] = mpart[member, :, row * w : (row + 1) * w]
    for copy in small:
        copy.wait()
    gat[...] = gx[...]
    smc[...] = sx[...]
    pair.wait()
    for k in range(1, g.D):
        conditions(k).wait()
    call_all[...] = cx[...]


def split_heads(g, wide):
    return [wide[r * g.hw + h * g.hd : r * g.hw + (h + 1) * g.hd] for r in range(3) for h in range(g.lh)]


def attend_kernel(
    g, tokens, mod, gat, smc, wi, wix, wo, ob, we, wr,
    h1_out, qkv_out, lse, att, res, h2, gath, wof, wex, wrx,
    tok, h1, qkv, gsend, gbuf, wob, bias, send_w, recv_w, load, keep, save, send, recv, send_o, recv_o, send_f, recv_f,
):
    d, t, p, c = g.place()
    partner = (d, p * 2 + 1 - c)
    weights = (wi, wix)
    copy = pltpu.make_async_copy(tokens.at[pl.ds(pl.multiple_of(c * g.Rc, g.Rc), g.Rc)], tok, load)
    copy.start()
    meet([(d, flip(p, k, g.bits) * 2 + c) for k in range(1, g.G)] + [partner])

    def share(k):
        return remote(wo, wob.at[t], send_o.at[k], recv_o.at[k], (d, flip(p, k, g.bits) * 2 + c))

    def forward(k):
        row = flip(p, k, g.bits) * 2 + c
        src = wo if k == 0 else wob.at[row]
        return remote(src, wob.at[row], send_f.at[k], recv_f.at[k], partner)

    for k in range(1, g.G):
        share(k).start()
    forward(0).start()
    pair = [
        remote(src, dst, send_w.at[index], recv_w.at[index], partner)
        for index, (src, dst) in enumerate(((we, wex), (wr, wrx)))
    ]
    for weight in pair:
        weight.start()
    wob[t] = wo[...]
    copy.wait()
    scale = 1.0 / math.sqrt(g.hd)
    ones = jnp.ones((8, g.L), BF)
    for s in range(2):
        for r in range(2):
            line = jnp.where(
                lax.broadcasted_iota(jnp.int32, (8, g.hw), 0) == r + 1, smc[s, :, : g.hw], 0.0
            )
            bias[s, r] = tn(line.astype(BF), ones)

    def chunk(j):
        i, u = j // g.sub, lax.rem(j, g.sub)
        src = gsend.at[i] if g.sub == 1 else gsend.at[i, :, :, pl.ds(pl.multiple_of(u * g.Ro, g.Ro), g.Ro)]
        return src, gbuf.at[pl.ds(p * 2, 2)]

    def away(j):
        src, dst = chunk(j)
        return remote(src, dst, send.at[j], recv.at[p], (d, j * 2 + c))

    def arrive(j):
        src, _ = chunk(j)
        dst = gbuf.at[pl.ds(j * 2, 2)]
        return remote(src, dst, send.at[j], recv.at[j], (d, j * 2 + c))

    def home():
        src, dst = chunk(p)
        return pltpu.make_async_copy(src, dst, keep)

    def item(ii, carry):
        i = flip(p // g.sub, g.Ic - 1 - ii, g.bits)
        rows = pl.ds(pl.multiple_of(i * g.L, g.L), g.L)
        row = c * g.Ic + i

        @pl.when(ii == g.Ic - 1)
        def _():
            for k in range(1, g.G):
                share(k).wait_recv()
                forward(k).start()

        normed, _ = norm(tok[rows].astype(F32))
        hidden = (
            normed * (1.0 + mod[1, pl.ds(row, 1), :]) + mod[0, pl.ds(row, 1), :]
        ).astype(BF)
        h1[rows] = hidden
        for s in range(2):
            wide = nt(weights[s][...], hidden)
            core = c + s - 2 * c * s
            parts = split_heads(g, wide)
            for h in range(g.lh):
                hh = s * g.lh + h
                rows_h = slice(h * g.hd, (h + 1) * g.hd)
                q = (parts[h] + bias[s, 0, rows_h]).astype(BF)
                k = parts[g.lh + h].astype(BF)
                v = (parts[2 * g.lh + h] + bias[s, 1, rows_h]).astype(BF)
                qkv[hh * 3 + 0, :, rows] = q
                qkv[hh * 3 + 1, :, rows] = k
                qkv[hh * 3 + 2, :, rows] = v
                scores = tn(k, q) * scale
                peak = jnp.max(scores, axis=0, keepdims=True)
                powers = jnp.exp(scores - peak)
                total = jnp.sum(powers, axis=0, keepdims=True)
                lse[hh : hh + 1, rows] = peak + jnp.log(total)
                probs = (powers * (1.0 / total)).astype(BF)
                mixed = nn(v, probs)
                gate = gat[s, pl.ds(row, 1), 2 * h : 2 * h + 1]
                gsend[i, core, rows_h, :] = (mixed * gate).astype(BF)
        for u in range(g.sub):
            j = i * g.sub + u

            @pl.when(j == p)
            def _():
                home().start()

            @pl.when(j != p)
            def _():
                away(j).start()

        return carry

    lax.fori_loop(0, g.Ic, item, 0)
    saves = [pltpu.make_async_copy(h1, h1_out, save.at[0]), pltpu.make_async_copy(qkv, qkv_out, save.at[1])]
    for copy in saves:
        copy.start()
    home().wait()
    for k in range(1, g.G):
        arrive(flip(p, k, g.bits)).wait_recv()
    heads = gbuf[...].reshape(g.T * g.hw, g.Ro)
    gath[...] = heads
    for k in range(g.G):
        forward(k).wait_recv()
    saves.append(pltpu.make_async_copy(wob, wof, save.at[2]))
    saves[-1].start()
    full = wob[...].reshape(g.T * g.hw, g.W)
    attention = tn(heads, full) + ob[...].astype(F32).reshape(1, g.W)
    own = c * g.Ic + p // g.sub
    base = tok[pl.ds(pl.multiple_of(p * g.Ro, g.Ro), g.Ro)].astype(F32)
    residual = base + mod[2, pl.ds(own, 1), :] * attention
    att[...] = attention
    res[...] = residual
    normed, _ = norm(residual)
    h2[...] = (normed * (1.0 + mod[4, pl.ds(own, 1), :]) + mod[3, pl.ds(own, 1), :]).astype(BF)
    for k in range(1, g.G):
        away(flip(p, k, g.bits)).wait_send()
        share(k).wait_send()
    for k in range(g.G):
        forward(k).wait_send()
    for copy in saves:
        copy.wait()
    for copy in pair:
        copy.wait()


def feed_kernel(
    g, h2, cotangent, mod, gat, smc, we_in, wex_in, wr_in, wrx_in,
    grad_out, mpart_out, dwf_out, small, gates, ebs,
    cot, we, wex, wr, wrx, h2buf, bgbuf, gch, egb, sgb, own_g, xs, xr, mpart, dwf,
    joint, final, send_g, recv_g, leg_box, leg_sems, done, load, save, send_h, recv_h, send_p, recv_p,
):
    d, t, p, c = g.place()
    partner = (d, p * 2 + 1 - c)
    wec = (we, wex)
    wrc = (wr, wrx)

    def chip(k):
        return (d, flip(p, k, g.bits) * 2 + c)

    cot_rows = cotangent.at[pl.ds(pl.multiple_of(c * g.Rc, g.Rc), g.Rc)]
    loads = [
        pltpu.make_async_copy(src, dst, load.at[index])
        for index, (src, dst) in enumerate(
            ((cot_rows, cot), (wr_in, wr), (wrx_in, wrx), (we_in, we), (wex_in, wex))
        )
    ]
    for copy in loads:
        copy.start()
    leg = FirstLeg(g, g.fe, dwf, leg_box, leg_sems)
    meet([chip(k) for k in range(1, g.G)] + [partner, leg.other])

    spread = PlaneGather(g, h2, lambda k, source: h2buf.at[k], send_h, recv_h, chip, p)
    spread.start()
    back = PlaneScatter(g, lambda k: sgb.at[k - 1], joint, final, send_g, recv_g, chip)
    h2buf[0] = h2[...]
    for copy in loads:
        copy.wait()
    lane = lax.broadcasted_iota(jnp.int32, (1, g.ch), 1)
    tile_row = lax.broadcasted_iota(jnp.int32, (8, 128), 0)
    tile_lane = lax.broadcasted_iota(jnp.int32, (8, 128), 1)
    ebs[...] = jnp.zeros_like(ebs)
    gates[...] = jnp.zeros_like(gates)

    def block(k, carry):
        j = flip(p, k, g.bits)
        local = j // g.sub
        item = c * g.Ic + local
        rows = pl.ds(pl.multiple_of(j * g.Ro, g.Ro), g.Ro)
        here = pl.ds(pl.multiple_of(k * g.Ro, g.Ro), g.Ro)
        branch = (mod[5, pl.ds(item, 1), :] * cot[rows].astype(F32)).astype(BF)
        bgbuf[here] = branch
        grads = [nt(branch, wrc[s][...]) for s in range(2)]

        @pl.when(k == 1)
        def _():
            spread.relay()

        for kk in range(1, g.G):

            @pl.when(k == kk)
            def _():
                spread.wait(kk)

        hidden = h2buf[k]
        total = None
        for s in range(2):
            wide = nt(hidden, wec[s][...]) + smc[s, 0:1, : g.ch]
            inner = GELU_A * (wide + GELU_B * wide * wide * wide)
            tanh = jnp.tanh(inner)
            act = 0.5 * wide * (1.0 + tanh)
            slope = 0.5 * (1.0 + tanh) + 0.5 * wide * (1.0 - tanh * tanh) * (
                GELU_A * (1.0 + 3.0 * GELU_B * wide * wide)
            )
            gate = gat[s, pl.ds(item, 1), 1:2]
            for h in range(1, g.lh):
                gate = jnp.where(lane >= h * g.gc, gat[s, pl.ds(item, 1), 2 * h + 1 : 2 * h + 2], gate)
            gch[s, here] = (act * gate).astype(BF)
            line = jnp.sum(grads[s] * act, axis=0, keepdims=True)
            tile = gates[s]
            for h in range(g.lh):
                inside = jnp.where((lane >= h * g.gc) & (lane < (h + 1) * g.gc), line, 0.0)
                value = jnp.sum(inside, axis=1, keepdims=True)
                tile = tile + jnp.where((tile_row == local) & (tile_lane == 2 * h + 1), value, 0.0)
            gates[s] = tile
            egrad = (grads[s] * gate * slope).astype(BF)
            egb[s, here] = egrad
            ebs[s, 0:1, : g.ch] += jnp.sum(egrad.astype(F32), axis=0, keepdims=True)
            part = nn(egrad, wec[s][...])
            total = part if total is None else total + part

        @pl.when(k > 0)
        def _():
            sgb[k - 1] = total.astype(BF)
            back.put(k)

        @pl.when(k == 0)
        def _():
            own_g[...] = total

        return carry

    lax.fori_loop(0, g.G, block, 0)
    def swap(index):
        return remote(xs.at[index], xr.at[index], send_p.at[index], recv_p.at[index], partner)

    half_units = g.units // 2
    saves = []
    for index, left in enumerate((gch, egb)):
        right = bgbuf[...] if index == 0 else h2buf[...].reshape(g.Rc, g.W)
        xs[index] = tn(left[1], right).astype(BF)
        swap(index).start()
        value = tn(left[0], right)
        swap(index).wait_recv()
        value = (value + xr[index].astype(F32)).astype(BF)
        for u in range(half_units):
            dwf[index * half_units + u] = value[u * g.fr : (u + 1) * g.fr]
        if index == 0:
            leg.start()
            back.join()
    copy = pltpu.make_async_copy(dwf.at[pl.ds(g.fe, g.units - g.fe)], dwf_out.at[pl.ds(g.fe, g.units - g.fe)], save.at[0])
    copy.start()
    saves.append(copy)
    for k in range(g.G):
        rows = pl.ds(k * g.Ro, g.Ro)
        mpart[k] = (nn(gch[0, rows], wr[...]) + nn(gch[1, rows], wrx[...])).astype(BF)
    saves.append(pltpu.make_async_copy(mpart, mpart_out, save.at[2]))
    saves[-1].start()
    small[...] = jnp.zeros_like(small)
    small[7:8, :] = jnp.sum(bgbuf[0 : g.Ro].astype(F32), axis=0, keepdims=True)
    grad_out[...] = back.total(own_g[...])
    leg.add()
    copy = pltpu.make_async_copy(dwf.at[pl.ds(0, g.fe)], dwf_out.at[pl.ds(0, g.fe)], save.at[1])
    copy.start()
    saves.append(copy)
    leg.sent()

    @pl.when(leg.middle == 1)
    def _():
        pl.semaphore_signal(done, inc=1, device_id=leg.other, device_id_type=MESH)

    @pl.when(leg.middle == 0)
    def _():
        pl.semaphore_wait(done, 1)

    spread.sent()
    back.sent()
    swap(0).wait_send()
    swap(1).wait_send()
    for copy in saves:
        copy.wait()


def unattend_kernel(
    g, hgrad, h1_in, qkv_in, lse, gat, wi_in, wix_in, small_in, mpart_in, dwf, mod, att, res, wof_in, gath_in,
    cotangent, rbias, ebs, gates_in,
    grad, rgrad, bout, dwz, dwf_out, lines, sums, pay, gates,
    h1, qkv, wi, wix, mpart, wof, gath,
    hgs, hgbuf, wof_x, orr, osum, small, dqkv, acc, own_g, sgb, xs, xr, orv, sx, cot,
    work, first_z, second_z, more_z, sems_z, leg_box, leg_sems, joint_g, final_g, send_g, recv_g, joint_m, final_m, send_m, recv_m,
    send_o, recv_o, send_s, recv_s, send_p, recv_p, send_a, recv_a, send_x, recv_x,
    load,
):
    d, t, p, c = g.place()
    partner = (d, p * 2 + 1 - c)
    weights = (wi, wix)
    block = c * g.G + p

    def chip(k):
        return (d, flip(p, k, g.bits) * 2 + c)

    def peer(k):
        return (d, flip(t, k, g.tbits))

    def group(k):
        return (flip(d, k, g.dbits), t)

    fetch = pltpu.make_async_copy(
        cotangent.at[pl.ds(pl.multiple_of(block * g.Ro, g.Ro), g.Ro)], cot, load.at[0]
    )
    fetch.start()
    half = pltpu.make_async_copy(dwf, work, load.at[1])
    half.start()
    loads = [
        pltpu.make_async_copy(src, dst, load.at[2 + index])
        for index, (src, dst) in enumerate(
            (
                (wof_in, wof), (mpart_in, mpart), (gath_in, gath), (h1_in, h1), (qkv_in, qkv), (wi_in, wi),
                (wix_in, wix),
            )
        )
    ]
    for copy in loads:
        copy.start()
    zsum = GroupSum(g, g.units, work, first_z, second_z, more_z, dwf_out, sems_z)
    meet_line(g, [peer(k) for k in range(1, g.T)], group, zsum.middle)

    def rest(k):
        return remote(osum.at[flip(p, k, g.bits)], orv.at[k - 1], send_o.at[k], recv_o.at[k], chip(k))

    on = PlaneScatter(g, lambda k: mpart.at[k], joint_m, final_m, send_m, recv_m, chip)
    back = PlaneScatter(g, lambda k: sgb.at[k - 1], joint_g, final_g, send_g, recv_g, chip)

    def sumup(k):
        return remote(small, sx.at[k], send_s.at[k], recv_s.at[k], peer(k))

    def heads_out(k):
        return remote(hgs.at[pl.ds(flip(p, k, g.bits) * 2, 2)], hgbuf.at[k], send_a.at[k], recv_a.at[k], chip(k))

    def cross(q):
        return remote(wof_x.at[2 * q + 1 - c], orr.at[q], send_x.at[q], recv_x.at[q], partner)

    half.wait()
    everything = list(range(g.units))
    zsum.resume(everything[: g.fe])
    zsum.start(everything[g.fe :])
    leg = FirstLeg(g, g.ze, dwz, leg_box, leg_sems)
    fetch.wait()
    value = hgrad[...]
    own = c * g.Ic + p // g.sub
    normed, inverse = norm(res[...])
    cot_own = cot[...].astype(F32)
    residual = cot_own + norm_back(value * (1.0 + mod[4, pl.ds(own, 1), :]), normed, inverse)
    branch_one = (mod[2, pl.ds(own, 1), :] * residual).astype(BF)
    loads[0].wait()
    hgs[...] = nt(wof[...], branch_one).astype(BF).reshape(g.T, g.hw, g.Ro)
    for k in reversed(range(1, g.G)):
        heads_out(k).start()
    hgbuf[0] = hgs[pl.ds(p * 2, 2)]
    loads[1].wait()
    for k in reversed(range(1, g.G)):
        on.put(k)
    rgrad[...] = residual
    small[...] = small_in[...]
    small[2:3, :] = jnp.sum(residual * att[...], axis=0, keepdims=True)
    small[3:4, :] = jnp.sum(value, axis=0, keepdims=True)
    small[4:5, :] = jnp.sum(value * normed, axis=0, keepdims=True)
    small[6:7, :] = jnp.sum(branch_one.astype(F32), axis=0, keepdims=True)
    for k in range(1, g.T):
        sumup(k).start()
    for copy in loads[2:]:
        copy.wait()
    wof_x[...] = nn(gath[...], branch_one).astype(BF).reshape(g.T, g.hw, g.W)
    for q in range(g.G):
        cross(q).start()
    scale = 1.0 / math.sqrt(g.hd)
    acc[...] = jnp.zeros_like(acc)
    ones = jnp.ones((8, g.L), BF)
    tile_row = lax.broadcasted_iota(jnp.int32, (8, 128), 0)
    tile_lane = lax.broadcasted_iota(jnp.int32, (8, 128), 1)
    gates[...] = gates_in[...]
    pay[...] = ebs[...]

    def item(ii, carry):
        kk = lax.rem(g.Ic - ii, g.Ic)
        i = flip(p // g.sub, kk, g.bits)
        row = c * g.Ic + i
        rows = pl.ds(pl.multiple_of(i * g.L, g.L), g.L)
        slots = [kk * g.sub + (flip(lax.rem(p, g.sub), u, 4) if g.sub > 1 else 0) for u in range(g.sub)]
        hidden = h1[rows]
        total = None
        for u, slot in enumerate(slots):

            @pl.when(slot != 0)
            def _():
                heads_out(slot).wait_recv()

        @pl.when(ii == min(2, g.Ic - 1))
        def _():
            zsum.settle([1])
            zsum.join([3])

        @pl.when(ii == 1)
        def _():
            zsum.settle([0])
            zsum.join([2])
            for q in range(g.G):
                cross(q).wait()
                osum[q] = (wof_x[2 * q + c].astype(F32) + orr[q].astype(F32)).astype(BF)
            for k in range(1, g.G):
                rest(k).start()

        @pl.when(ii == g.Ic - 1)
        def _():
            on.join()

        for s in range(2):
            core = c + s - 2 * c * s
            tile = gates[s]
            for h in range(g.lh):
                hh = s * g.lh + h
                q = qkv[hh * 3 + 0, :, rows]
                k = qkv[hh * 3 + 1, :, rows]
                v = qkv[hh * 3 + 2, :, rows]
                pieces = [hgbuf[slot, core, h * g.hd : (h + 1) * g.hd, :] for slot in slots]
                heads = (pieces[0] if g.sub == 1 else jnp.concatenate(pieces, axis=1)).astype(F32)
                probs = jnp.exp(tn(k, q) * scale - lse[hh : hh + 1, rows])
                low = probs.astype(BF)
                mixed = nn(v, low)
                value = jnp.sum(jnp.sum(heads * mixed, axis=0, keepdims=True), axis=1, keepdims=True)
                tile = tile + jnp.where((tile_row == i) & (tile_lane == 2 * h), value, 0.0)
                mixed_grad = (gat[s, pl.ds(row, 1), 2 * h : 2 * h + 1] * heads).astype(BF)
                probs_grad = tn(v, mixed_grad)
                values_grad = nt(mixed_grad, low)
                score = (
                    probs * (probs_grad - jnp.sum(probs_grad * probs, axis=0, keepdims=True))
                ).astype(BF)
                queries_grad = nn(k, score) * scale
                keys_grad = nt(q, score) * scale
                for r, value in enumerate((queries_grad, keys_grad, values_grad)):
                    dqkv[s, r * g.hw + h * g.hd : r * g.hw + (h + 1) * g.hd, :] = value.astype(BF)
            gates[s] = tile
            wide = dqkv[s]
            part = tn(wide, weights[s][...])
            total = part if total is None else total + part
            acc[s] += nn(wide, hidden)
            pay[s, 1:2, : 3 * g.hw] += nt(ones, wide)[0:1]
        for u, slot in enumerate(slots):
            piece = total[u * g.Ro : (u + 1) * g.Ro]

            @pl.when(slot == 0)
            def _():
                own_g[...] = piece

            @pl.when(slot != 0)
            def _():
                sgb[slot - 1] = piece.astype(BF)
                back.put(slot)

        return carry

    lax.fori_loop(0, g.Ic, item, 0)
    xs[...] = acc[1].astype(BF)
    swap = remote(xs, xr, send_p, recv_p, partner)
    swap.start()
    zsum.settle([2])
    zsum.join([4])
    swap.wait()
    for u in range(g.units):
        low = u * g.zr
        if low < 3 * g.hw:
            span = slice(low, low + g.zr)
            dwz[u] = (acc[0, span] + xr[span].astype(F32)).astype(BF)
    leg.start()
    zsum.settle([3])
    zsum.join([5])
    zsum.settle([4])
    zsum.join([6])
    back.join()
    zsum.settle([5])
    zsum.join([7])
    value = small[...]
    for k in range(1, g.T):
        sumup(k).wait()
        value = value + sx[k]
    sums[...] = value
    out = osum[p].astype(F32)
    for k in range(1, g.G):
        rest(k).wait()
        out = out + orv[k - 1].astype(F32)
    for u in range(g.units):
        low = u * g.zr
        if low >= 3 * g.hw:
            dwz[u] = out[low - 3 * g.hw : low - 3 * g.hw + g.zr].astype(BF)
    zsum.settle([6])
    branch = on.total(mpart[0].astype(F32)) + rbias[...].astype(F32).reshape(1, g.W)
    bout[...] = (res[...] + mod[5, pl.ds(own, 1), :] * branch).astype(BF)
    lines[...] = small[...]
    lines[5:6, :] = jnp.sum(cot[...].astype(F32) * branch, axis=0, keepdims=True)
    zsum.settle([7])
    grad[...] = back.total(own_g[...])
    on.sent()
    back.sent()
    leg.add()
    zsum.end(everything, everything[g.fe :])
    leg.sent()
    for k in range(1, g.G):
        heads_out(k).wait_send()


def finish_kernel(
    g, grad, rgrad, tokens, mod, lines_in, sums, bout, pay, gates, dsg, dwz,
    tall, ball, colall, zall, logall, dwz_out,
    tok, tsend, stage, cbuf, zbuf, lbuf, pbuf, gbuf, work, first_z, second_z, more_z, sems_z,
    load, send_t, recv_t, send_f, recv_f, send_c, recv_c, send_p, recv_p, send_s, recv_s, keep,
):
    d, t, p, c = g.place()
    partner = (d, p * 2 + 1 - c)

    def chip(k):
        return (d, flip(p, k, g.bits) * 2 + c)

    def peer(k):
        return (d, flip(t, k, g.tbits))

    def group(k):
        return (flip(d, k, g.dbits), t)

    meet([peer(k) for k in range(1, g.T)] + [group(k) for k in range(1, g.D)])
    block = c * g.G + p
    mine = pl.ds(pl.multiple_of(block * g.Ro, g.Ro), g.Ro)
    copy = pltpu.make_async_copy(tokens.at[mine], tok, load)
    copy.start()
    swaps = [
        remote(pay.at[1], pbuf, send_p.at[0], recv_p.at[0], partner),
        remote(gates.at[1], gbuf, send_p.at[1], recv_p.at[1], partner),
    ]
    for swap in swaps:
        swap.start()
    zsum = GroupSum(g, g.units, work, first_z, second_z, more_z, dwz_out, sems_z)
    everything = list(range(g.units))
    work[...] = dwz[...]
    zsum.resume(everything[: g.ze])
    zsum.start(everything[g.ze :])

    def rows_of(dst):
        return lambda k, source: dst.at[pl.ds(pl.multiple_of((c * g.G + source) * g.Ro, g.Ro), g.Ro)]

    outs = PlaneGather(g, bout, rows_of(ball), send_t.at[0], recv_t.at[0], chip, p)
    grads = PlaneGather(g, tsend, rows_of(tall), send_t.at[1], recv_t.at[1], chip, p)
    outs.start()
    copy.wait()
    own = c * g.Ic + p // g.sub
    normed, inverse = norm(tok[...].astype(F32))
    value = grad[...]
    scaled = value * (1.0 + mod[1, pl.ds(own, 1), :])
    tsend[...] = (rgrad[...] + norm_back(scaled, normed, inverse)).astype(BF)
    lines = lines_in[...]
    kind = lax.broadcasted_iota(jnp.int32, lines.shape, 0)
    first = jnp.sum(value, axis=0, keepdims=True)
    second = jnp.sum(value * normed, axis=0, keepdims=True)
    lines = jnp.where(kind == 0, first, jnp.where(kind == 1, second, lines))
    w = g.mw
    stage[...] = jnp.zeros_like(stage)
    for member in range(g.T):
        stage[member, :, :w] = lines[:, member * w : (member + 1) * w]

    def columns(k):
        return remote(stage.at[flip(t, k, g.tbits)], cbuf.at[d, t], send_c.at[k], recv_c.at[k], peer(k))

    def column_in(k):
        return remote(stage.at[t], cbuf.at[d, flip(t, k, g.tbits)], send_c.at[k], recv_c.at[k], peer(k))

    for k in range(1, g.T):
        columns(k).start()
    cbuf[d, t] = stage[t]
    grads.start()
    local = [
        pltpu.make_async_copy(bout, ball.at[mine], keep.at[0]),
        pltpu.make_async_copy(tsend, tall.at[mine], keep.at[1]),
    ]
    for item in local:
        item.start()

    def forward(which, dst, k):
        rows = pl.ds(pl.multiple_of((c * g.G + flip(p, k, g.bits)) * g.Ro, g.Ro), g.Ro)
        return remote(dst.at[rows], dst.at[rows], send_f.at[which, k], recv_f.at[which, k], partner)

    def arrive_forward(which, dst, k):
        rows = pl.ds(pl.multiple_of(((1 - c) * g.G + flip(p, k, g.bits)) * g.Ro, g.Ro), g.Ro)
        return remote(dst.at[rows], dst.at[rows], send_f.at[which, k], recv_f.at[which, k], partner)

    outs.relay()
    zsum.join([4])
    zsum.settle([0, 1])
    for swap in swaps:
        swap.wait()
    zbuf[d] = jnp.zeros((8, g.W), F32)
    zbuf[d, 0:2] = pay[0, 0:2] + pbuf[0:2]
    zbuf[d, 2:4] = sums[6:8]
    both = jnp.concatenate([gates[0, : g.Ic], gbuf[: g.Ic]], axis=0)
    turned = jnp.concatenate([gbuf[: g.Ic], gates[0, : g.Ic]], axis=0)
    lbuf[d] = jnp.where(c == 0, both, turned) * dsg[...]
    zsum.join([5, 6])
    zsum.settle([2])
    for k in range(1, g.T):
        columns(k).wait_send()
        column_in(k).wait_recv()

    def share(k):
        return [
            remote(cbuf.at[d], cbuf.at[d], send_s.at[0, k], recv_s.at[0, k], group(k)),
            remote(zbuf.at[d], zbuf.at[d], send_s.at[1, k], recv_s.at[1, k], group(k)),
            remote(lbuf.at[d], lbuf.at[d], send_s.at[2, k], recv_s.at[2, k], group(k)),
        ]

    def shared(k):
        other = flip(d, k, g.dbits)
        return [
            remote(cbuf.at[other], cbuf.at[other], send_s.at[0, k], recv_s.at[0, k], group(k)),
            remote(zbuf.at[other], zbuf.at[other], send_s.at[1, k], recv_s.at[1, k], group(k)),
            remote(lbuf.at[other], lbuf.at[other], send_s.at[2, k], recv_s.at[2, k], group(k)),
        ]

    for k in range(1, g.D):
        for item in share(k):
            item.start()
    for which, dst in ((0, ball), (1, tall)):
        local[which].wait()
        forward(which, dst, 0).start()
    zsum.join([7])
    zsum.settle([3, 4])
    grads.relay()
    zsum.settle([5, 6, 7])
    for k in range(1, g.G):
        outs.wait(k)
        forward(0, ball, k).start()
    for k in range(1, g.D):
        for item in share(k):
            item.wait_send()
        for item in shared(k):
            item.wait_recv()
    colall[...] = cbuf[...]
    zall[...] = zbuf[...]
    logall[...] = lbuf[...]
    for k in range(1, g.G):
        grads.wait(k)
        forward(1, tall, k).start()
    zsum.end(everything, everything[g.ze :])
    outs.sent()
    grads.sent()
    for which, dst in ((0, ball), (1, tall)):
        for k in range(g.G):
            forward(which, dst, k).wait_send()
            arrive_forward(which, dst, k).wait_recv()


def wrap_kernel(
    g, ball, tall, dwf, dwz, colall, zall, logall, conds,
    out, tokens_grad, dwr, dwe, dwi, dwo, dwm, dmb, drw, drb, dib, deb, dob, drb_all,
    twice,
):
    step = pl.program_id(0)
    out[...] = ball[...].astype(F32)
    tokens_grad[...] = tall[...].astype(F32)
    half_units = g.units // 2
    heads = 3 * g.units // 4

    @pl.when(step < half_units)
    def _():
        dwr[...] = dwf[...].astype(F32)

    @pl.when(step >= half_units)
    def _():
        dwe[...] = dwf[...].astype(F32)

    @pl.when(step < heads)
    def _():
        dwi[...] = dwz[...].astype(F32)

    @pl.when(step >= heads)
    def _():
        dwo[...] = dwz[...].astype(F32)

    w = g.mw

    @pl.when(step == 0)
    def _():
        rows = []
        for member in range(g.T):
            rows.append(((member % 2) * g.G + member // 2) * g.Ro // g.L)
        value = conds[...]
        silu = value / (1.0 + jnp.exp(-value))
        picked = jnp.concatenate([silu[z, i : i + 1] for z in range(g.D) for i in rows], axis=0).astype(BF)
        twice[...] = jnp.concatenate([picked, picked], axis=0)
        logits = jnp.concatenate([logall[z] for z in range(g.D)], axis=0)
        high = logits.astype(BF)
        low = (logits - high.astype(F32)).astype(BF)
        flat = jnp.concatenate([value[z] for z in range(g.D)], axis=0).astype(BF)
        router = tn(jnp.concatenate([high, low], axis=0), jnp.concatenate([flat, flat], axis=0))
        sums = jnp.sum(logits, axis=0, keepdims=True)
        for h in range(g.lh):
            drw[h] = router[2 * h : 2 * h + 2, :]
            drb[h : h + 1, :] = sums[:, 2 * h : 2 * h + 2]
        total = zall[0]
        for z in range(1, g.D):
            total = total + zall[z]
        dib[0:1, :] = total[1:2, : g.hw]
        dib[1:2, :] = total[1:2, 2 * g.hw : 3 * g.hw]
        deb[...] = total[0, : g.ch]
        dob[...] = total[2]
        drb_all[...] = total[3]

    @pl.when(step < 6)
    def _():
        part = jnp.concatenate(
            [colall[z, member, pl.ds(step, 1), :] for z in range(g.D) for member in range(g.T)], axis=0
        )
        dmb[pl.ds(step, 1), :] = jnp.sum(part, axis=0, keepdims=True)[:, :w]
        high = part.astype(BF)
        low = (part - high.astype(F32)).astype(BF)
        dwm[...] = tn(jnp.concatenate([high, low], axis=0), twice[...])[:w]


def wrap(g, ball, tall, dwf, dwz, colall, zall, logall, conds):
    n, W = g.units, g.W
    half_units, heads = n // 2, 3 * n // 4
    rows = g.R // n

    def whole(shape):
        return pl.BlockSpec(shape, lambda i: (0,) * len(shape))

    def part(shape, low, count):
        return pl.BlockSpec(shape, lambda i: (jnp.clip(i - low, 0, count - 1),) + (0,) * (len(shape) - 1))

    outs = [
        ((g.R, W), part((rows, W), 0, n)), ((g.R, W), part((rows, W), 0, n)),
        ((half_units, g.fr, W), part((1, g.fr, W), 0, half_units)),
        ((half_units, g.fr, W), part((1, g.fr, W), half_units, half_units)),
        ((heads, g.zr, W), part((1, g.zr, W), 0, heads)), ((n - heads, g.zr, W), part((1, g.zr, W), heads, n - heads)),
        ((6 * g.mw, W), part((g.mw, W), 0, 6)), ((6, g.mw), whole((6, g.mw))), ((g.lh, 2, W), whole((g.lh, 2, W))),
        ((g.lh, 2), whole((g.lh, 2))), ((2, g.hw), whole((2, g.hw))), ((g.ch,), whole((g.ch,))), ((W,), whole((W,))),
        ((W,), whole((W,))),
    ]
    return pl.pallas_call(
        functools.partial(wrap_kernel, g),
        name="wrap",
        grid=(n,),
        out_shape=[jax.ShapeDtypeStruct(s, F32) for s, _ in outs],
        in_specs=[
            part((rows, W), 0, n), part((rows, W), 0, n), part((1, g.fr, W), 0, n), part((1, g.zr, W), 0, n),
            whole(colall.shape), whole(zall.shape), whole(logall.shape), whole(conds.shape),
        ],
        out_specs=[spec for _, spec in outs],
        scratch_shapes=[pltpu.VMEM((2 * g.D * g.T, W), BF)],
        cost_estimate=pl.CostEstimate(flops=10**9, bytes_accessed=4 * 10**7, transcendentals=0),
        compiler_params=pltpu.CompilerParams(vmem_limit_bytes=VMEM_LIMIT),
    )(ball, tall, dwf, dwz, colall, zall, logall, conds)


def body(
    groups, members,
    tokens, condition, timesteps, route_masks, modulate_weight, modulate_bias, input_weight, input_bias,
    output_weight, output_bias, expand_weight, expand_bias, reduce_weight, reduce_bias, router_weight, router_bias,
    out_cotangent,
):
    g = Plan(
        groups, members, tokens.shape[0], condition.shape[0], tokens.shape[1], router_weight.shape[1],
        modulate_weight.shape[2], input_weight.shape[2], expand_weight.shape[1],
    )
    dma = pltpu.SemaphoreType.DMA
    V = pltpu.VMEM
    W, T, G, D, I = g.W, g.T, g.G, g.D, g.I
    wide = 2 * g.lh
    wm = jnp.transpose(modulate_weight, (1, 2, 0)).reshape(6 * g.mw, W)
    wi = jnp.transpose(input_weight, (1, 2, 0)).reshape(3 * g.hw, W)
    we = expand_weight.T
    wr = reduce_weight
    rw = jnp.transpose(router_weight, (1, 2, 0))
    masks = jnp.transpose(route_masks, (1, 2, 0))
    eb, ob, rbias = expand_bias, output_bias, reduce_bias

    mod, gat, dsg, smc, conds, wix = call(
        functools.partial(start_kernel, g), "start",
        (condition, wm, modulate_bias, timesteps, masks, rw, router_bias, eb, input_bias, wi),
        "vvvsvvvvvh",
        [
            ((6, I, W), F32), ((2, I, 128), F32), ((I, 128), F32), ((2, 8, W), F32), ((D, I, W), F32),
            ((3 * g.hw, W), BF),
        ],
        "vvvvvh",
        [
            V((T, I, 6 * g.mw), F32), V((2, I, 128), F32), V((2, 8, W), F32), V((D, I, W), F32),
            dma((T,)), dma((T,)), dma((3,)), dma((3,)), dma((D,)), dma((D,)),
        ],
        1,
    )
    h1, qkv, lse, att, res, h2, gath, wof, wex, wrx = call(
        functools.partial(attend_kernel, g), "attend",
        (tokens, mod, gat, smc, wi, wix, output_weight, ob, we, wr), "hvvvvvvvhh",
        [
            ((g.Rc, W), BF), ((wide * 3, g.hd, g.Rc), BF), ((wide, g.Rc), F32),
            ((g.Ro, W), F32), ((g.Ro, W), F32), ((g.Ro, W), BF), ((T * g.hw, g.Ro), BF), ((T, g.hw, W), BF),
            ((g.ch, W), BF), ((g.ch, W), BF),
        ],
        "hhvvvvvhhh",
        [
            V((g.Rc, W), BF), V((g.Rc, W), BF), V((wide * 3, g.hd, g.Rc), BF), V((g.Ic, 2, g.hw, g.L), BF), V((T, g.hw, g.Ro), BF), V((T, g.hw, W), BF),
            V((2, 2, g.hw, g.L), F32), dma((2,)), dma((2,)), dma, dma, dma((3,)), dma((G,)), dma((G,)), dma((G,)), dma((G,)), dma((G,)), dma((G,)),
        ],
        2,
    )
    hgrad, mpart, dwf, small, gates, ebs = call(
        functools.partial(feed_kernel, g), "feed",
        (h2, out_cotangent, mod, gat, smc, we, wex, wr, wrx), "vhvvvhhhh",
        [
            ((g.Ro, W), F32), ((G, g.Ro, W), BF), ((g.units, g.fr, W), BF),
            ((8, W), F32), ((2, 8, 128), F32), ((2, 8, W), F32),
        ],
        "vhhvvv",
        [
            V((g.Rc, W), BF), V((g.ch, W), BF), V((g.ch, W), BF), V((g.ch, W), BF), V((g.ch, W), BF),
            V((G, g.Ro, W), BF), V((g.Rc, W), BF), V((2, g.Rc, g.ch), BF), V((2, g.Rc, g.ch), BF),
            V((G - 1, g.Ro, W), BF), V((g.Ro, W), F32),
            V((2, g.ch, W), BF), V((2, g.ch, W), BF), V((G, g.Ro, W), BF), V((g.units, g.fr, W), BF),
        ]
        + PlaneScatter.scratch(g)
        + FirstLeg.scratch(g, g.fe, g.fr)
        + [pltpu.SemaphoreType.REGULAR, dma((5,)), dma((3,)), dma((G, 2)), dma((G, 2)), dma((2,)), dma((2,))],
        3,
    )
    grad, rgrad, bout, dwz, dwf, lines, sums, pay, gates = call(
        functools.partial(unattend_kernel, g), "unattend",
        (
            hgrad, h1, qkv, lse, gat, wi, wix, small, mpart, dwf, mod, att, res,
            wof.reshape(T * g.hw, W), gath, out_cotangent, rbias, ebs, gates,
        ),
        "vhhvvhhvhhvvvhhhvvv",
        [
            ((g.Ro, W), F32), ((g.Ro, W), F32), ((g.Ro, W), BF), ((g.units, g.zr, W), BF),
            ((g.units, g.fr, W), BF), ((8, W), F32), ((8, W), F32), ((2, 8, W), F32), ((2, 8, 128), F32),
        ],
        "vvvvvvvvv",
        [
            V((g.Rc, W), BF), V((wide * 3, g.hd, g.Rc), BF), V((3 * g.hw, W), BF), V((3 * g.hw, W), BF),
            V((G, g.Ro, W), BF), V((T * g.hw, W), BF), V((T * g.hw, g.Ro), BF),
            V((T, g.hw, g.Ro), BF), V((G, 2, g.hw, g.Ro), BF), V((T, g.hw, W), BF), V((G, g.hw, W), BF),
            V((G, g.hw, W), BF), V((8, W), F32),
            V((2, 3 * g.hw, g.L), BF), V((2, 3 * g.hw, W), F32), V((g.Ro, W), F32), V((G - 1, g.Ro, W), BF),
            V((3 * g.hw, W), BF), V((3 * g.hw, W), BF),
            V((G - 1, g.hw, W), BF), V((T, 8, W), F32), V((g.Ro, W), BF),
        ]
        + GroupSum.scratch(g, g.units, g.fr)
        + FirstLeg.scratch(g, g.ze, g.zr)
        + PlaneScatter.scratch(g)
        + PlaneScatter.scratch(g)
        + [
            dma((G,)), dma((G,)), dma((T,)), dma((T,)), dma, dma,
            dma((G,)), dma((G,)), dma((G,)), dma((G,)), dma((9,)),
        ],
        4,
    )
    tall, ball, colall, zall, logall, dwz = call(
        functools.partial(finish_kernel, g), "finish",
        (grad, rgrad, tokens, mod, lines, sums, bout, pay, gates, dsg, dwz), "vvhvvvvvvvv",
        [
            ((g.R, W), BF), ((g.R, W), BF), ((D, T, 8, g.cw), F32), ((D, 8, W), F32), ((D, I, 128), F32),
            ((g.units, g.zr, W), BF),
        ],
        "hhvvvv",
        [
            V((g.Ro, W), BF), V((g.Ro, W), BF), V((T, 8, g.cw), F32), V((D, T, 8, g.cw), F32), V((D, 8, W), F32),
            V((D, I, 128), F32), V((8, W), F32), V((8, 128), F32),
        ]
        + GroupSum.scratch(g, g.units, g.zr)
        + [
            dma, dma((2, G, 2)), dma((2, G, 2)), dma((2, G)), dma((2, G)), dma((T,)), dma((T,)), dma((2,)), dma((2,)),
            dma((3, D)), dma((3, D)), dma((2,)),
        ],
        5,
    )
    out, tokens_grad, dwr, dwe, dwi, dwo, dwm, dmb, drw, drb, dib, deb, dob, drb_all = wrap(
        g, ball, tall, dwf, dwz, colall, zall, logall, conds
    )
    return (
        out,
        tokens_grad,
        jnp.transpose(dwm.reshape(6, g.mw, W), (2, 0, 1)),
        dmb,
        jnp.transpose(dwi.reshape(3, g.hw, W), (2, 0, 1)),
        dib,
        dwo.reshape(g.hw, W),
        dob,
        dwe.reshape(g.ch, W).T,
        deb,
        dwr.reshape(g.ch, W),
        drb_all,
        jnp.transpose(drw, (2, 0, 1)),
        drb,
    )


def solution(mesh):
    return jax.shard_map(
        functools.partial(body, mesh.shape["dp"], mesh.shape["tensor"]),
        mesh=mesh,
        in_specs=(
            P("dp", None), P("dp", None), P("dp"), P(None, "tensor", None), P(None, None, "tensor"),
            P(None, "tensor"), P(None, None, "tensor"), P(None, "tensor"), P("tensor", None), P(),
            P(None, "tensor"), P("tensor"), P("tensor", None), P(), P(None, "tensor", None), P("tensor", None),
            P("dp", None),
        ),
        out_specs=(
            P("dp", None), P("dp", None), P(None, None, "tensor"), P(None, "tensor"), P(None, None, "tensor"),
            P(None, "tensor"), P("tensor", None), P(), P(None, "tensor"), P("tensor"), P("tensor", None), P(),
            P(None, "tensor", None), P("tensor", None),
        ),
        check_vma=False,
    )
```
